128 devices in a mesh: seq: 32 (over y, z, x_lo), tp: 4 (over x_hi, core).
Axes of the slice: x: 4 (x_hi: 2, x_lo: 2; x = x_hi * 2 + x_lo), y: 4, z: 4, core: 2. Of those that a mesh axis runs over, the one named last changes fastest.
Arguments:
- queries: bfloat16 [6144, 2048], P('seq', 'tp'), may hold values from -6 to 6
- keys: bfloat16 [6144, 2048], P('seq', 'tp'), may hold values from -6 to 6
- values: bfloat16 [6144, 2048], P('seq', 'tp'), may hold values from -6 to 6
- lengths: int32 [4], replicated, may hold values from 1 to 3072, 6144 in all
- resid: bfloat16 [6144, 2048], P(('seq', 'tp')), may hold values from -6 to 6
- w_out: bfloat16 [2048, 2048], P('tp'), may hold values from -0.5 to 0.5
- moe_gain: float32 [2048], replicated, may hold values from 0.25 to 1.75
- routes: int32 [6144, 8], P(('seq', 'tp')), may hold values from 0 to 63, all different within a row; in each aligned block of 48 rows (0 to 47, 48 to 95, ...) at most 9 rows name the same one
- gates: float32 [6144, 8], P(('seq', 'tp')), may hold values from 0.05 to 0.3
- w_gate_up: bfloat16 [64, 2048, 2, 1024], P('seq', None, None, 'tp'), may hold values from -0.125 to 0.125
- w_down: bfloat16 [64, 1024, 2048], P('seq', 'tp'), may hold values from -0.1875 to 0.1875
Outputs:
- attended: bfloat16 [6144, 2048], P(('seq', 'tp'))
- expert_mix: bfloat16 [6144, 2048], P(('seq', 'tp'))
The draws below stay inside these ranges and needn't reach their ends.
Inputs may be any that keep to these rules, and one draw needn't show every extreme that they name: The 4 lengths sum to 6144; the largest is exactly 3072. `routes`: each row names 8 different experts. Within each aligned block of 48 rows (the rows of one device) no expert is named by more than 9 rows, a bound that some block reaches.
All inputs are finite; a program needn't handle non-finite values.
Results may differ from the reference program's by a relative error of at most 0.03.
Values may be sent and summed in bfloat16 or wider, within the bound.
A program may use at most 128 MiB of HBM per device.

```python
import math
import jax
import jax.numpy as jnp
import numpy as np
from jax import lax

D = 2048
HEADS = 16
HEAD_DIM = 128
FF = 1024
TOP = 8
TENANTS = 4
EXPERTS = 64
TOKENS = 6144
ROWS_DEV = 48
CAP = 9
N_TP = 4


def base_field(key):
    return jax.random.truncated_normal(key, -6.0, 6.0, (TOKENS, HEADS * HEAD_DIM), jnp.float32)


def draw_queries(key, part):
    field = base_field(jax.random.fold_in(key, 1))
    return field.astype(jnp.bfloat16)


def draw_keys(key, part):
    field = base_field(jax.random.fold_in(key, 2))
    return field.astype(jnp.bfloat16)


def levels(rng, extent, shards, smallest, top_value):
    factor_of = 1.0
    for dim, blocks in shards:
        heights = jax.random.uniform(jax.random.fold_in(jax.random.fold_in(rng, 6), dim), (blocks,), jnp.float32, smallest / len(shards), top_value / len(shards))
        factor_of = factor_of * jnp.repeat(jnp.exp(heights), extent[dim] // blocks).reshape((-1,) + (1,) * (len(extent) - 1 - dim))
    return factor_of


def length_profile(count, total, bound, lean):
    loads = [(1 << 20) // math.isqrt(rank ** lean) + 1 for rank in range(2, count + 1)]
    spare, holding = total - bound - (count - 1), [1] * (count - 1)
    while spare > 0:
        candidates = [i for i in range(count - 1) if holding[i] < bound]
        pool, remaining = sum([loads[i] for i in candidates]), spare
        for i in candidates:
            extra = min(bound - holding[i], max(1, remaining * loads[i] // pool), spare)
            holding[i] = holding[i] + extra
            spare = spare - extra
    return np.array([bound] + holding)


def ragged_sizes(own_key, number_of, total, reach, slope):
    if number_of == 2:
        one = jax.random.randint(own_key, (), max(1, total - reach), min(reach, total - 1) + 1)
        return jnp.stack([one, total - one])
    sizes = jnp.asarray(length_profile(number_of, total, reach, slope), jnp.int32)
    couples = (number_of - 1) // 2
    giver, taker = sizes[1:1 + 2 * couples:2], sizes[2:2 + 2 * couples:2]
    room = jnp.minimum(giver - 1, reach - taker)
    shifted = jax.random.randint(jax.random.fold_in(own_key, 1), (couples,), 0, 1 << 20) % (room + 1)
    sizes = sizes.at[1:1 + 2 * couples:2].set(giver - shifted).at[2:2 + 2 * couples:2].set(taker + shifted)
    return sizes[jax.random.permutation(jax.random.fold_in(own_key, 2), number_of)]


def assign_block(stream_key, own, number, rows, amount, top, most, skew):
    sequence = jax.random.permutation(stream_key, amount)
    packed, usual = portions_of(amount, rows * top, most, skew, True), portions_of(amount, rows * top, most, skew, False)
    places = jnp.arange(amount)

    def named(tallies, offset_by):
        used = int((tallies > 0).sum())
        fixed = max(1, used // 4)
        passed = fixed + (places - fixed + offset_by * (used - fixed)) % max(1, amount - fixed)
        return jnp.zeros((amount,), jnp.int32).at[sequence[jnp.where(places < fixed, places, passed)]].set(jnp.asarray(tallies, jnp.int32))

    tallies = jnp.where(number % 4 == 0, named(packed, number // 4), named(usual, number - number // 4 - 1))
    mixed = jax.random.permutation(jax.random.fold_in(own, 3), amount)
    source_of, receiver = mixed[0:amount // 2 * 2:2], mixed[1:amount // 2 * 2:2]
    slack = jnp.minimum(tallies[source_of] - 1, most - tallies[receiver]) // 2
    slack = jnp.where((source_of == sequence[0]) | (receiver == sequence[0]) | (tallies[receiver] == 0), 0, jnp.maximum(slack, 0))
    passed = jax.random.randint(jax.random.fold_in(own, 4), (amount // 2,), 0, 1 << 20) % (slack + 1)
    tallies = tallies.at[source_of].add(-passed).at[receiver].add(passed)
    items = jnp.searchsorted(jnp.cumsum(tallies), jnp.arange(rows * top), side="right").astype(jnp.int32)
    table = items.reshape(top, rows).T
    table = table[jax.random.permutation(jax.random.fold_in(own, 1), rows)]
    offset_by = jax.random.randint(jax.random.fold_in(own, 2), (rows, 1), 0, top)
    return jnp.take_along_axis(table, (jnp.arange(top)[None, :] + offset_by) % top, axis=1)


def portions_of(number_of, total, most, slope, full):
    weights = [(1 << 20) // math.isqrt(grade ** slope) + 1 for grade in range(1, number_of + 1)]
    largest = most if full else min(most, max(-(-total // number_of), total * weights[0] // sum(weights)))
    least = 1 if total - largest >= number_of - 1 else 0
    given, rest = [largest] + [least] * (number_of - 1), total - largest - least * (number_of - 1)
    while rest > 0:
        free = [i for i in range(1, number_of) if given[i] < largest] or [i for i in range(1, number_of) if given[i] < most]
        pool, budget = sum([weights[i] for i in free]), rest
        for i in free:
            more = min(most - given[i], max(1, budget * weights[i] // pool), rest)
            given[i] = given[i] + more
            rest = rest - more
    return np.array(given)


def scatter_about(stream_key, dims, width, most, pieces=(), kind=jnp.bfloat16):
    result = jax.random.normal(stream_key, dims, jnp.float32) * width
    if len(pieces) > 0:
        result = levels(stream_key, dims, pieces, -0.22, 0.18) * result
    return jnp.clip(result, min=-most, max=most).astype(kind)


def setup_inputs(seed: int = 0) -> dict:
    arg_keys = jax.random.split(jax.random.key(seed), 12)
    queries = draw_queries(jax.random.fold_in(arg_keys[11], 71), 0)
    keys = draw_keys(jax.random.fold_in(arg_keys[11], 71), 0)
    values = scatter_about(arg_keys[2], (TOKENS, HEADS * HEAD_DIM), 1.0, 6.0, ((0, 32), (1, 4)))
    lengths = ragged_sizes(arg_keys[3], TENANTS, TOKENS, TOKENS // 2, 2).astype(jnp.int32)
    resid = scatter_about(arg_keys[4], (TOKENS, D), 0.5, 6.0, ((0, 128),))
    w_out = scatter_about(arg_keys[5], (HEADS * HEAD_DIM, D), HEAD_DIM ** -0.5, 0.5, ((0, 4),))
    moe_gain = jnp.clip(1.0 + 0.15 * jax.random.normal(arg_keys[6], (D,), jnp.float32), 0.25, 1.75)
    routes_keys = jax.random.split(jax.random.fold_in(arg_keys[7], 1), TOKENS // ROWS_DEV)
    routes_turns = jax.random.permutation(jax.random.fold_in(arg_keys[7], 3), TOKENS // ROWS_DEV)
    routes = jax.vmap(lambda own, number: assign_block(jax.random.fold_in(arg_keys[7], 2), own, number, ROWS_DEV, EXPERTS, TOP, CAP, 2))(routes_keys, routes_turns).reshape((TOKENS, TOP))
    gates = jnp.clip(0.05 + 0.25 * jax.random.uniform(arg_keys[8], (TOKENS, TOP), jnp.float32) ** levels(arg_keys[8], (TOKENS, TOP), ((0, 128),), -0.2, 0.2), 0.05, 0.3)
    w_gate_up = scatter_about(arg_keys[9], (EXPERTS, D, 2, FF), D ** -0.5, 0.125, ((0, 32), (3, 4)))
    w_down = scatter_about(arg_keys[10], (EXPERTS, FF, D), FF ** -0.5, 0.1875, ((0, 32), (1, 4)))
    return dict(queries=queries, keys=keys, values=values, lengths=lengths, resid=resid, w_out=w_out, moe_gain=moe_gain, routes=routes, gates=gates, w_gate_up=w_gate_up, w_down=w_down)


def tenant_of(positions, lengths):
    bounds = jnp.cumsum(lengths).astype(jnp.int32)
    return lax.optimization_barrier(jnp.sum((positions[:, None] >= bounds[None, :]).astype(jnp.int32), axis=1))

def reference(queries, keys, values, lengths, resid, w_out, moe_gain, routes, gates, w_gate_up, w_down):
    positions = jnp.arange(TOKENS, dtype=jnp.int32)
    tenant = tenant_of(positions, lengths)
    visible = (tenant[:, None] == tenant[None, :]) & (positions[None, :] <= positions[:, None])
    score_scale = 1.0 / math.sqrt(HEAD_DIM)
    q_heads = queries.reshape(TOKENS, HEADS, HEAD_DIM).transpose(1, 0, 2)
    k_heads = keys.reshape(TOKENS, HEADS, HEAD_DIM).transpose(1, 0, 2)
    v_heads = values.reshape(TOKENS, HEADS, HEAD_DIM).transpose(1, 0, 2)

    def one_head(operands):
        q_block, k_block, v_block = operands
        scores = jnp.dot(q_block, k_block.T, preferred_element_type=jnp.float32) * score_scale
        scores = jnp.where(visible, scores, -jnp.inf)
        largest = lax.optimization_barrier(jnp.max(scores, axis=1, keepdims=True))
        weights = jnp.where(visible, jnp.exp(scores - largest), 0.0)
        denominator = lax.optimization_barrier(jnp.sum(weights, axis=1, keepdims=True))
        rounded_weights = weights.astype(jnp.bfloat16)
        weighted = jnp.dot(rounded_weights, v_block, preferred_element_type=jnp.float32)
        return (weighted / denominator).astype(jnp.bfloat16)
    heads_out = lax.map(one_head, (q_heads, k_heads, v_heads))
    attention = heads_out.transpose(1, 0, 2).reshape(TOKENS, HEADS * HEAD_DIM)
    projected = jnp.dot(attention, w_out, preferred_element_type=jnp.float32)
    attended = (resid.astype(jnp.float32) + projected).astype(jnp.bfloat16)
    widened = attended.astype(jnp.float32)
    meansq = lax.optimization_barrier(jnp.mean(widened * widened, axis=1, keepdims=True))
    normed = (widened * lax.rsqrt(meansq + 1e-05) * moe_gain[None, :]).astype(jnp.bfloat16)
    ff_part = FF // N_TP
    max_rows = CAP * (TOKENS // ROWS_DEV)
    expert_ids = jnp.arange(EXPERTS, dtype=jnp.int32)
    matches = routes[:, :, None] == expert_ids[None, None, :]
    weight_of = lax.optimization_barrier(jnp.sum(jnp.where(matches, gates[:, :, None], 0.0), axis=1))
    members = jnp.any(matches, axis=1)

    def per_expert(summed, expert):
        column = lax.dynamic_index_in_dim(members, expert, 1, keepdims=False)
        how_many = jnp.sum(column.astype(jnp.int32))
        chosen_rows = jnp.nonzero(column, size=max_rows, fill_value=0)[0].astype(jnp.int32)
        selected = normed[chosen_rows]
        gate_up = w_gate_up[expert]
        gate_proj = jnp.dot(selected, gate_up[:, 0, :], preferred_element_type=jnp.float32)
        up_proj = jnp.dot(selected, gate_up[:, 1, :], preferred_element_type=jnp.float32)
        hidden = (jax.nn.silu(gate_proj) * up_proj).astype(jnp.bfloat16)
        down_rows = w_down[expert]
        blocks_total = jnp.zeros((max_rows, D), jnp.float32)
        for block_index in range(N_TP):
            partial_value = jnp.dot(hidden[:, block_index * ff_part:(block_index + 1) * ff_part], down_rows[block_index * ff_part:(block_index + 1) * ff_part], preferred_element_type=jnp.float32)
            blocks_total = blocks_total + lax.optimization_barrier(partial_value.astype(jnp.bfloat16)).astype(jnp.float32)
        expert_out = lax.optimization_barrier(blocks_total.astype(jnp.bfloat16)).astype(jnp.float32)
        in_use = jnp.arange(max_rows, dtype=jnp.int32) < how_many
        factor = jnp.where(in_use, weight_of[chosen_rows, expert], 0.0)
        summed = summed.at[chosen_rows].add(factor[:, None] * expert_out)
        return (summed, None)
    mixed_total, _ = lax.scan(per_expert, jnp.zeros((TOKENS, D), jnp.float32), expert_ids)
    expert_mix = mixed_total.astype(jnp.bfloat16)
    return (attended, expert_mix)
```

```python
import math

import jax
import jax.numpy as jnp
from jax import lax
from jax.sharding import PartitionSpec as P

HEAD_DIM = 128


def tenant_of(positions, lengths):
    bounds = jnp.cumsum(lengths)
    return jnp.sum((positions[:, None] >= bounds[None, :]).astype(jnp.int32), axis=1)


def shards(
    queries, keys, values, lengths, resid, w_out, moe_gain, routes, gates, w_gate_up, w_down
):
    seq_count = lax.axis_size("seq")
    me = lax.axis_index("seq")
    query_rows = queries.shape[0]
    local_heads = queries.shape[1] // HEAD_DIM
    cols = queries.shape[1]
    width = resid.shape[1]
    score_scale = 1.0 / math.sqrt(HEAD_DIM)
    longest = (seq_count * query_rows) // 2
    reach = min(seq_count - 1, -(-(longest - 1) // query_rows))
    query_pos = me * query_rows + jnp.arange(query_rows, dtype=jnp.int32)
    query_tenant = tenant_of(query_pos, lengths)
    query_heads = queries.reshape(query_rows, local_heads, HEAD_DIM)
    kv = jnp.concatenate([keys, values], axis=1)
    pieces = [kv]
    positions = [query_pos]
    for shift in range(1, reach + 1):
        pieces.append(
            lax.ppermute(kv, "seq", perm=[(s, s + shift) for s in range(seq_count - shift)])
        )
        positions.append(query_pos - shift * query_rows)
    kv_piece = jnp.concatenate(pieces, axis=0)
    key_pos = jnp.concatenate(positions, axis=0)
    key_piece = kv_piece[:, :cols]
    value_piece = kv_piece[:, cols:]
    row_count = key_piece.shape[0]
    key_tenant = tenant_of(key_pos, lengths)
    visible = (
        (key_tenant[None, :] == query_tenant[:, None])
        & (key_pos[None, :] <= query_pos[:, None])
        & (key_pos[None, :] >= 0)
    )
    scores = (
        jnp.einsum(
            "qhd,khd->hqk",
            query_heads,
            key_piece.reshape(row_count, local_heads, HEAD_DIM),
            preferred_element_type=jnp.float32,
        )
        * score_scale
    )
    scores = jnp.where(visible[None], scores, -1e30)
    new_max = jnp.max(scores, axis=2)
    exponent = jnp.where(visible[None], jnp.exp(scores - new_max[:, :, None]), 0.0)
    run_sum = jnp.sum(exponent, axis=2)
    value_heads = value_piece.reshape(row_count, local_heads, HEAD_DIM)
    accumulated = jnp.einsum(
        "hqk,khd->hqd",
        exponent.astype(jnp.bfloat16),
        value_heads,
        preferred_element_type=jnp.float32,
    )
    attention = (
        (accumulated / run_sum[:, :, None])
        .transpose(1, 0, 2)
        .reshape(query_rows, local_heads * HEAD_DIM)
    )
    attention = attention.astype(jnp.bfloat16)
    projected = lax.psum_scatter(
        jnp.dot(attention, w_out, preferred_element_type=jnp.float32).astype(jnp.bfloat16),
        "tp",
        scatter_dimension=0,
        tiled=True,
    ).astype(jnp.float32)
    attended = (resid.astype(jnp.float32) + projected).astype(jnp.bfloat16)
    widened = attended.astype(jnp.float32)
    meansq = jnp.mean(widened * widened, axis=1, keepdims=True)
    normed = (widened * lax.rsqrt(meansq + 1e-05) * moe_gain[None, :]).astype(jnp.bfloat16)
    local_rows = resid.shape[0]
    top_count = routes.shape[1]
    owned = w_gate_up.shape[0]
    experts_all = owned * seq_count
    capacity = 3 * local_rows * top_count // (2 * experts_all)
    matches = routes[:, :, None] == jnp.arange(experts_all, dtype=jnp.int32)[None, None, :]
    member = jnp.any(matches, axis=1)
    slot = jnp.cumsum(member.astype(jnp.int32), axis=0) - 1
    place = member[:, :, None] & (
        slot[:, :, None] == jnp.arange(capacity, dtype=jnp.int32)[None, None, :]
    )
    buffer = jnp.einsum(
        "iec,id->ecd", place.astype(jnp.bfloat16), normed, preferred_element_type=jnp.float32
    ).astype(jnp.bfloat16)
    arrived = lax.all_to_all(
        buffer.reshape(seq_count, owned, capacity, width),
        "seq",
        split_axis=0,
        concat_axis=0,
        tiled=True,
    )
    expand_arrived = lax.all_gather(arrived, "tp", axis=0, tiled=True)
    projections = jnp.einsum(
        "nxcd,xdgf->nxcgf", expand_arrived, w_gate_up, preferred_element_type=jnp.float32
    )
    hidden = (jax.nn.silu(projections[..., 0, :]) * projections[..., 1, :]).astype(jnp.bfloat16)
    summed = lax.psum_scatter(
        jnp.einsum("nxcf,xfd->nxcd", hidden, w_down, preferred_element_type=jnp.float32).astype(
            jnp.bfloat16
        ),
        "tp",
        scatter_dimension=0,
        tiled=True,
    )
    returned = lax.all_to_all(summed, "seq", split_axis=0, concat_axis=0, tiled=True)
    weight_of = jnp.sum(jnp.where(matches, gates[:, :, None], 0.0), axis=1)
    mix_weights = jnp.where(place, weight_of[:, :, None], 0.0)
    expert_mix = jnp.einsum(
        "iec,ecd->id",
        mix_weights,
        returned.reshape(experts_all, capacity, width).astype(jnp.float32),
        precision=lax.Precision.HIGHEST,
        preferred_element_type=jnp.float32,
    ).astype(jnp.bfloat16)
    return (attended, expert_mix)


def solution(mesh):
    return jax.shard_map(
        shards,
        mesh=mesh,
        in_specs=(
            P("seq", "tp"),
            P("seq", "tp"),
            P("seq", "tp"),
            P(),
            P(("seq", "tp"), None),
            P("tp", None),
            P(),
            P(("seq", "tp"), None),
            P(("seq", "tp"), None),
            P("seq", None, None, "tp"),
            P("seq", "tp", None),
        ),
        out_specs=(P(("seq", "tp"), None), P(("seq", "tp"), None)),
        check_vma=False,
    )
```

```python
import functools
import math

import jax
import jax.numpy as jnp
from jax import lax
from jax.experimental import pallas as pl
from jax.experimental.pallas import tpu as pltpu
from jax.sharding import PartitionSpec as P

HEAD_DIM = 128


def tenant_of(positions, lengths):
    bounds = jnp.cumsum(lengths)
    return jnp.sum((positions[:, None] >= bounds[None, :]).astype(jnp.int32), axis=1)


def window_kernel(reach, count, kv_ref, out_ref, send_sem, recv_sem):
    me = lax.axis_index("seq")
    tp = lax.axis_index("tp")

    def copy(shift):
        return pltpu.make_async_remote_copy(
            src_ref=kv_ref,
            dst_ref=out_ref.at[shift - 1],
            send_sem=send_sem.at[shift - 1],
            recv_sem=recv_sem.at[shift - 1],
            device_id=(lax.rem(me + shift, count), tp),
            device_id_type=pl.DeviceIdType.MESH,
        )

    for shift in range(1, reach + 1):

        @pl.when(me + shift < count)
        def _():
            copy(shift).start()

    for shift in range(1, reach + 1):

        @pl.when(me + shift < count)
        def _():
            copy(shift).wait_send()

        @pl.when(me - shift >= 0)
        def _():
            copy(shift).wait_recv()


def window_exchange(kv, reach, count):
    return pl.pallas_call(
        functools.partial(window_kernel, reach, count),
        out_shape=jax.ShapeDtypeStruct((reach,) + kv.shape, kv.dtype),
        in_specs=[pl.BlockSpec(memory_space=pl.ANY)],
        out_specs=pl.BlockSpec(memory_space=pl.ANY),
        scratch_shapes=[pltpu.SemaphoreType.DMA((reach,)), pltpu.SemaphoreType.DMA((reach,))],
        compiler_params=pltpu.CompilerParams(has_side_effects=True),
    )(kv)


def shards(
    queries, keys, values, lengths, resid, w_out, moe_gain, routes, gates, w_gate_up, w_down
):
    seq_count = lax.axis_size("seq")
    me = lax.axis_index("seq")
    query_rows = queries.shape[0]
    local_heads = queries.shape[1] // HEAD_DIM
    cols = queries.shape[1]
    width = resid.shape[1]
    score_scale = 1.0 / math.sqrt(HEAD_DIM)
    longest = (seq_count * query_rows) // 2
    reach = min(seq_count - 1, -(-(longest - 1) // query_rows))
    query_pos = me * query_rows + jnp.arange(query_rows, dtype=jnp.int32)
    query_tenant = tenant_of(query_pos, lengths)
    query_heads = queries.reshape(query_rows, local_heads, HEAD_DIM)
    kv = jnp.concatenate([keys, values], axis=1)
    received = window_exchange(kv, reach, seq_count)
    kv_piece = jnp.concatenate([kv[None], received], axis=0).reshape(-1, 2 * cols)
    key_pos = (
        me * query_rows
        - jnp.arange(reach + 1, dtype=jnp.int32)[:, None] * query_rows
        + jnp.arange(query_rows, dtype=jnp.int32)[None, :]
    ).reshape(-1)
    kv_piece = jnp.where((key_pos >= 0)[:, None], kv_piece, jnp.zeros_like(kv_piece))
    key_piece = kv_piece[:, :cols]
    value_piece = kv_piece[:, cols:]
    row_count = key_piece.shape[0]
    key_tenant = tenant_of(key_pos, lengths)
    visible = (
        (key_tenant[None, :] == query_tenant[:, None])
        & (key_pos[None, :] <= query_pos[:, None])
        & (key_pos[None, :] >= 0)
    )
    scores = (
        jnp.einsum(
            "qhd,khd->hqk",
            query_heads,
            key_piece.reshape(row_count, local_heads, HEAD_DIM),
            preferred_element_type=jnp.float32,
        )
        * score_scale
    )
    scores = jnp.where(visible[None], scores, -1e30)
    new_max = jnp.max(scores, axis=2)
    exponent = jnp.where(visible[None], jnp.exp(scores - new_max[:, :, None]), 0.0)
    run_sum = jnp.sum(exponent, axis=2)
    value_heads = value_piece.reshape(row_count, local_heads, HEAD_DIM)
    accumulated = jnp.einsum(
        "hqk,khd->hqd",
        exponent.astype(jnp.bfloat16),
        value_heads,
        preferred_element_type=jnp.float32,
    )
    attention = (
        (accumulated / run_sum[:, :, None])
        .transpose(1, 0, 2)
        .reshape(query_rows, local_heads * HEAD_DIM)
    )
    attention = attention.astype(jnp.bfloat16)
    projected = lax.psum_scatter(
        jnp.dot(attention, w_out, preferred_element_type=jnp.float32).astype(jnp.bfloat16),
        "tp",
        scatter_dimension=0,
        tiled=True,
    ).astype(jnp.float32)
    attended = (resid.astype(jnp.float32) + projected).astype(jnp.bfloat16)
    widened = attended.astype(jnp.float32)
    meansq = jnp.mean(widened * widened, axis=1, keepdims=True)
    normed = (widened * lax.rsqrt(meansq + 1e-05) * moe_gain[None, :]).astype(jnp.bfloat16)
    local_rows = resid.shape[0]
    top_count = routes.shape[1]
    owned = w_gate_up.shape[0]
    experts_all = owned * seq_count
    capacity = 3 * local_rows * top_count // (2 * experts_all)
    matches = routes[:, :, None] == jnp.arange(experts_all, dtype=jnp.int32)[None, None, :]
    member = jnp.any(matches, axis=1)
    slot = jnp.cumsum(member.astype(jnp.int32), axis=0) - 1
    place = member[:, :, None] & (
        slot[:, :, None] == jnp.arange(capacity, dtype=jnp.int32)[None, None, :]
    )
    buffer = jnp.einsum(
        "iec,id->ecd", place.astype(jnp.bfloat16), normed, preferred_element_type=jnp.float32
    ).astype(jnp.bfloat16)
    arrived = lax.all_to_all(
        buffer.reshape(seq_count, owned, capacity, width),
        "seq",
        split_axis=0,
        concat_axis=0,
        tiled=True,
    )
    expand_arrived = lax.all_gather(arrived, "tp", axis=0, tiled=True)
    projections = jnp.einsum(
        "nxcd,xdgf->nxcgf", expand_arrived, w_gate_up, preferred_element_type=jnp.float32
    )
    hidden = (jax.nn.silu(projections[..., 0, :]) * projections[..., 1, :]).astype(jnp.bfloat16)
    summed = lax.psum_scatter(
        jnp.einsum("nxcf,xfd->nxcd", hidden, w_down, preferred_element_type=jnp.float32).astype(
            jnp.bfloat16
        ),
        "tp",
        scatter_dimension=0,
        tiled=True,
    )
    returned = lax.all_to_all(summed, "seq", split_axis=0, concat_axis=0, tiled=True)
    weight_of = jnp.sum(jnp.where(matches, gates[:, :, None], 0.0), axis=1)
    mix_weights = jnp.where(place, weight_of[:, :, None], 0.0)
    expert_mix = jnp.einsum(
        "iec,ecd->id",
        mix_weights,
        returned.reshape(experts_all, capacity, width).astype(jnp.float32),
        precision=lax.Precision.HIGHEST,
        preferred_element_type=jnp.float32,
    ).astype(jnp.bfloat16)
    return (attended, expert_mix)


def solution(mesh):
    return jax.shard_map(
        shards,
        mesh=mesh,
        in_specs=(
            P("seq", "tp"),
            P("seq", "tp"),
            P("seq", "tp"),
            P(),
            P(("seq", "tp"), None),
            P("tp", None),
            P(),
            P(("seq", "tp"), None),
            P(("seq", "tp"), None),
            P("seq", None, None, "tp"),
            P("seq", "tp", None),
        ),
        out_specs=(P(("seq", "tp"), None), P(("seq", "tp"), None)),
        check_vma=False,
    )
```

```python
import functools
import math

import jax
import jax.numpy as jnp
from jax import lax
from jax.experimental import pallas as pl
from jax.experimental.pallas import tpu as pltpu
from jax.sharding import PartitionSpec as P

HEAD_DIM = 128


def tenant_of(positions, lengths):
    bounds = jnp.cumsum(lengths)
    return jnp.sum((positions[:, None] >= bounds[None, :]).astype(jnp.int32), axis=1)


def spread_kernel(
    blocks, per, back, q_ref, kv_ref, q_out, kv_out, q_send, q_recv, kv_send, kv_recv
):
    me = lax.axis_index("seq")
    tp = lax.axis_index("tp")
    heads = q_ref.shape[0]
    span = back + per
    tries = back // per + 1
    mine = me % blocks

    def send(src, dst, sem, recv, target):
        @pl.when(target == me)
        def _():
            pltpu.make_async_copy(src, dst, sem).start()

        @pl.when(target != me)
        def _():
            pltpu.make_async_remote_copy(
                src_ref=src,
                dst_ref=dst,
                send_sem=sem,
                recv_sem=recv,
                device_id=(target, tp),
                device_id_type=pl.DeviceIdType.MESH,
            ).start()

    def finish_send(src, dst, sem, recv, target):
        @pl.when(target == me)
        def _():
            pltpu.make_async_copy(src, dst, sem).wait()

        @pl.when(target != me)
        def _():
            pltpu.make_async_remote_copy(
                src_ref=src,
                dst_ref=dst,
                send_sem=sem,
                recv_sem=recv,
                device_id=(target, tp),
                device_id_type=pl.DeviceIdType.MESH,
            ).wait_send()

    def finish_recv(src, dst, sem, recv, source):
        @pl.when(source != me)
        def _():
            pltpu.make_async_remote_copy(
                src_ref=src,
                dst_ref=dst,
                send_sem=sem,
                recv_sem=recv,
                device_id=(source, tp),
                device_id_type=pl.DeviceIdType.MESH,
            ).wait_recv()

    plan = []
    for h in range(heads):
        target = h * blocks + me // per
        plan.append((q_ref.at[h], q_out.at[me % per], q_send.at[h], q_recv.at[me % per], target))
        for r in range(tries):
            block = (me + back) // per - r
            slot = (me + back) % per + per * r
            plan.append(
                (
                    kv_ref.at[h],
                    kv_out.at[slot],
                    kv_send.at[h, r],
                    kv_recv.at[slot],
                    h * blocks + block,
                    (block >= 0) & (block < blocks),
                )
            )
    for item in plan:
        valid = item[5] if len(item) > 5 else True

        @pl.when(valid)
        def _():
            send(*item[:5])

    for item in plan:
        valid = item[5] if len(item) > 5 else True

        @pl.when(valid)
        def _():
            finish_send(*item[:5])

    for i in range(per):
        source = per * mine + i
        finish_recv(q_ref.at[0], q_out.at[i], q_send.at[0], q_recv.at[i], source)
    for slot in range(span):
        source = per * mine - back + slot

        @pl.when(source >= 0)
        def _():
            finish_recv(kv_ref.at[0], kv_out.at[slot], kv_send.at[0, 0], kv_recv.at[slot], source)


def spread(q, kv, blocks, per, back):
    heads = q.shape[0]
    span = back + per
    tries = back // per + 1
    return pl.pallas_call(
        functools.partial(spread_kernel, blocks, per, back),
        out_shape=(
            jax.ShapeDtypeStruct((per,) + q.shape[1:], q.dtype),
            jax.ShapeDtypeStruct((span,) + kv.shape[1:], kv.dtype),
        ),
        in_specs=[pl.BlockSpec(memory_space=pl.ANY)] * 2,
        out_specs=(pl.BlockSpec(memory_space=pl.ANY), pl.BlockSpec(memory_space=pl.ANY)),
        scratch_shapes=[
            pltpu.SemaphoreType.DMA((heads,)),
            pltpu.SemaphoreType.DMA((per,)),
            pltpu.SemaphoreType.DMA((heads, tries)),
            pltpu.SemaphoreType.DMA((span,)),
        ],
        compiler_params=pltpu.CompilerParams(has_side_effects=True),
    )(q, kv)


def gather_kernel(blocks, per, att_ref, out_ref, send_sem, recv_sem):
    me = lax.axis_index("seq")
    tp = lax.axis_index("tp")
    heads = out_ref.shape[0]
    head = me // blocks
    mine = me % blocks

    def copy(i, target):
        return pltpu.make_async_remote_copy(
            src_ref=att_ref.at[i],
            dst_ref=out_ref.at[head],
            send_sem=send_sem.at[i],
            recv_sem=recv_sem.at[head],
            device_id=(target, tp),
            device_id_type=pl.DeviceIdType.MESH,
        )

    for i in range(per):
        target = per * mine + i

        @pl.when(target == me)
        def _():
            pltpu.make_async_copy(att_ref.at[i], out_ref.at[head], send_sem.at[i]).start()

        @pl.when(target != me)
        def _():
            copy(i, target).start()

    for i in range(per):
        target = per * mine + i

        @pl.when(target == me)
        def _():
            pltpu.make_async_copy(att_ref.at[i], out_ref.at[head], send_sem.at[i]).wait()

        @pl.when(target != me)
        def _():
            copy(i, target).wait_send()

    for h in range(heads):
        source = h * blocks + me // per

        @pl.when(source != me)
        def _():
            pltpu.make_async_remote_copy(
                src_ref=att_ref.at[0],
                dst_ref=out_ref.at[h],
                send_sem=send_sem.at[0],
                recv_sem=recv_sem.at[h],
                device_id=(source, tp),
                device_id_type=pl.DeviceIdType.MESH,
            ).wait_recv()


def gather_back(att, heads, blocks):
    per = att.shape[0]
    return pl.pallas_call(
        functools.partial(gather_kernel, blocks, per),
        out_shape=jax.ShapeDtypeStruct((heads,) + att.shape[1:], att.dtype),
        in_specs=[pl.BlockSpec(memory_space=pl.ANY)],
        out_specs=pl.BlockSpec(memory_space=pl.ANY),
        scratch_shapes=[pltpu.SemaphoreType.DMA((per,)), pltpu.SemaphoreType.DMA((heads,))],
        compiler_params=pltpu.CompilerParams(has_side_effects=True),
    )(att)


def shards(
    queries, keys, values, lengths, resid, w_out, moe_gain, routes, gates, w_gate_up, w_down
):
    seq_count = lax.axis_size("seq")
    me = lax.axis_index("seq")
    query_rows = queries.shape[0]
    local_heads = queries.shape[1] // HEAD_DIM
    cols = queries.shape[1]
    width = resid.shape[1]
    score_scale = 1.0 / math.sqrt(HEAD_DIM)
    longest = (seq_count * query_rows) // 2
    reach = min(seq_count - 1, -(-(longest - 1) // query_rows))
    blocks = seq_count // local_heads
    per = seq_count // blocks
    back = -(-reach // per) * per
    span = back + per
    head_q = queries.reshape(query_rows, local_heads, HEAD_DIM).transpose(1, 0, 2)
    head_kv = jnp.concatenate(
        [
            keys.reshape(query_rows, local_heads, HEAD_DIM),
            values.reshape(query_rows, local_heads, HEAD_DIM),
        ],
        axis=2,
    ).transpose(1, 0, 2)
    q_in, kv_in = spread(head_q, head_kv, blocks, per, back)
    mine = me % blocks
    query_pos = mine * per * query_rows + jnp.arange(per * query_rows, dtype=jnp.int32)
    key_pos = (mine * per - back) * query_rows + jnp.arange(span * query_rows, dtype=jnp.int32)
    kv_in = kv_in.reshape(span * query_rows, 2 * HEAD_DIM)
    kv_in = jnp.where((key_pos >= 0)[:, None], kv_in, jnp.zeros_like(kv_in))
    query_tenant = tenant_of(query_pos, lengths)
    key_tenant = tenant_of(key_pos, lengths)
    visible = (
        (key_tenant[None, :] == query_tenant[:, None])
        & (key_pos[None, :] <= query_pos[:, None])
        & (key_pos[None, :] >= 0)
    )
    scores = (
        jnp.dot(
            q_in.reshape(per * query_rows, HEAD_DIM),
            kv_in[:, :HEAD_DIM].T,
            preferred_element_type=jnp.float32,
        )
        * score_scale
    )
    scores = jnp.where(visible, scores, -1e30)
    new_max = jnp.max(scores, axis=1, keepdims=True)
    exponent = jnp.where(visible, jnp.exp(scores - new_max), 0.0)
    run_sum = jnp.sum(exponent, axis=1, keepdims=True)
    accumulated = jnp.dot(
        exponent.astype(jnp.bfloat16), kv_in[:, HEAD_DIM:], preferred_element_type=jnp.float32
    )
    head_att = (accumulated / run_sum).astype(jnp.bfloat16).reshape(per, query_rows, HEAD_DIM)
    attention = (
        gather_back(head_att, local_heads, blocks)
        .transpose(1, 0, 2)
        .reshape(query_rows, local_heads * HEAD_DIM)
    )
    projected = lax.psum_scatter(
        jnp.dot(attention, w_out, preferred_element_type=jnp.float32).astype(jnp.bfloat16),
        "tp",
        scatter_dimension=0,
        tiled=True,
    ).astype(jnp.float32)
    attended = (resid.astype(jnp.float32) + projected).astype(jnp.bfloat16)
    widened = attended.astype(jnp.float32)
    meansq = jnp.mean(widened * widened, axis=1, keepdims=True)
    normed = (widened * lax.rsqrt(meansq + 1e-05) * moe_gain[None, :]).astype(jnp.bfloat16)
    local_rows = resid.shape[0]
    top_count = routes.shape[1]
    owned = w_gate_up.shape[0]
    experts_all = owned * seq_count
    capacity = 3 * local_rows * top_count // (2 * experts_all)
    matches = routes[:, :, None] == jnp.arange(experts_all, dtype=jnp.int32)[None, None, :]
    member = jnp.any(matches, axis=1)
    slot = jnp.cumsum(member.astype(jnp.int32), axis=0) - 1
    place = member[:, :, None] & (
        slot[:, :, None] == jnp.arange(capacity, dtype=jnp.int32)[None, None, :]
    )
    buffer = jnp.einsum(
        "iec,id->ecd", place.astype(jnp.bfloat16), normed, preferred_element_type=jnp.float32
    ).astype(jnp.bfloat16)
    arrived = lax.all_to_all(
        buffer.reshape(seq_count, owned, capacity, width),
        "seq",
        split_axis=0,
        concat_axis=0,
        tiled=True,
    )
    expand_arrived = lax.all_gather(arrived, "tp", axis=0, tiled=True)
    projections = jnp.einsum(
        "nxcd,xdgf->nxcgf", expand_arrived, w_gate_up, preferred_element_type=jnp.float32
    )
    hidden = (jax.nn.silu(projections[..., 0, :]) * projections[..., 1, :]).astype(jnp.bfloat16)
    summed = lax.psum_scatter(
        jnp.einsum("nxcf,xfd->nxcd", hidden, w_down, preferred_element_type=jnp.float32).astype(
            jnp.bfloat16
        ),
        "tp",
        scatter_dimension=0,
        tiled=True,
    )
    returned = lax.all_to_all(summed, "seq", split_axis=0, concat_axis=0, tiled=True)
    weight_of = jnp.sum(jnp.where(matches, gates[:, :, None], 0.0), axis=1)
    mix_weights = jnp.where(place, weight_of[:, :, None], 0.0)
    expert_mix = jnp.einsum(
        "iec,ecd->id",
        mix_weights,
        returned.reshape(experts_all, capacity, width).astype(jnp.float32),
        precision=lax.Precision.HIGHEST,
        preferred_element_type=jnp.float32,
    ).astype(jnp.bfloat16)
    return (attended, expert_mix)


def solution(mesh):
    return jax.shard_map(
        shards,
        mesh=mesh,
        in_specs=(
            P("seq", "tp"),
            P("seq", "tp"),
            P("seq", "tp"),
            P(),
            P(("seq", "tp"), None),
            P("tp", None),
            P(),
            P(("seq", "tp"), None),
            P(("seq", "tp"), None),
            P("seq", None, None, "tp"),
            P("seq", "tp", None),
        ),
        out_specs=(P(("seq", "tp"), None), P(("seq", "tp"), None)),
        check_vma=False,
    )
```

```python
import functools
import math

import jax
import jax.numpy as jnp
from jax import lax
from jax.experimental import pallas as pl
from jax.experimental.pallas import tpu as pltpu
from jax.sharding import PartitionSpec as P

HEAD_DIM = 128


def tenant_of(positions, lengths):
    bounds = jnp.cumsum(lengths)
    return jnp.sum((positions[:, None] >= bounds[None, :]).astype(jnp.int32), axis=1)


def spread_kernel(
    blocks, per, back, q_ref, kv_ref, q_out, kv_out, q_send, q_recv, kv_send, kv_recv
):
    me = lax.axis_index("seq")
    tp = lax.axis_index("tp")
    heads = q_ref.shape[0]
    span = back + per
    tries = back // per + 1
    mine = me % blocks

    def send(src, dst, sem, recv, target):
        @pl.when(target == me)
        def _():
            pltpu.make_async_copy(src, dst, sem).start()

        @pl.when(target != me)
        def _():
            pltpu.make_async_remote_copy(
                src_ref=src,
                dst_ref=dst,
                send_sem=sem,
                recv_sem=recv,
                device_id=(target, tp),
                device_id_type=pl.DeviceIdType.MESH,
            ).start()

    def finish_send(src, dst, sem, recv, target):
        @pl.when(target == me)
        def _():
            pltpu.make_async_copy(src, dst, sem).wait()

        @pl.when(target != me)
        def _():
            pltpu.make_async_remote_copy(
                src_ref=src,
                dst_ref=dst,
                send_sem=sem,
                recv_sem=recv,
                device_id=(target, tp),
                device_id_type=pl.DeviceIdType.MESH,
            ).wait_send()

    def finish_recv(src, dst, sem, recv, source):
        @pl.when(source != me)
        def _():
            pltpu.make_async_remote_copy(
                src_ref=src,
                dst_ref=dst,
                send_sem=sem,
                recv_sem=recv,
                device_id=(source, tp),
                device_id_type=pl.DeviceIdType.MESH,
            ).wait_recv()

    plan = []
    for h in range(heads):
        target = h * blocks + me // per
        plan.append((q_ref.at[h], q_out.at[me % per], q_send.at[h], q_recv.at[me % per], target))
        for r in range(tries):
            block = (me + back) // per - r
            slot = (me + back) % per + per * r
            plan.append(
                (
                    kv_ref.at[h],
                    kv_out.at[slot],
                    kv_send.at[h, r],
                    kv_recv.at[slot],
                    h * blocks + block,
                    (block >= 0) & (block < blocks),
                )
            )
    for item in plan:
        valid = item[5] if len(item) > 5 else True

        @pl.when(valid)
        def _():
            send(*item[:5])

    for item in plan:
        valid = item[5] if len(item) > 5 else True

        @pl.when(valid)
        def _():
            finish_send(*item[:5])

    for i in range(per):
        source = per * mine + i
        finish_recv(q_ref.at[0], q_out.at[i], q_send.at[0], q_recv.at[i], source)
    for slot in range(span):
        source = per * mine - back + slot

        @pl.when(source >= 0)
        def _():
            finish_recv(kv_ref.at[0], kv_out.at[slot], kv_send.at[0, 0], kv_recv.at[slot], source)


def spread(q, kv, blocks, per, back):
    heads = q.shape[0]
    span = back + per
    tries = back // per + 1
    return pl.pallas_call(
        functools.partial(spread_kernel, blocks, per, back),
        out_shape=(
            jax.ShapeDtypeStruct((per,) + q.shape[1:], q.dtype),
            jax.ShapeDtypeStruct((span,) + kv.shape[1:], kv.dtype),
        ),
        in_specs=[pl.BlockSpec(memory_space=pl.ANY)] * 2,
        out_specs=(pl.BlockSpec(memory_space=pl.ANY), pl.BlockSpec(memory_space=pl.ANY)),
        scratch_shapes=[
            pltpu.SemaphoreType.DMA((heads,)),
            pltpu.SemaphoreType.DMA((per,)),
            pltpu.SemaphoreType.DMA((heads, tries)),
            pltpu.SemaphoreType.DMA((span,)),
        ],
        compiler_params=pltpu.CompilerParams(has_side_effects=True),
    )(q, kv)


def gather_kernel(blocks, per, att_ref, out_ref, send_sem, recv_sem):
    me = lax.axis_index("seq")
    tp = lax.axis_index("tp")
    heads = out_ref.shape[0]
    head = me // blocks
    mine = me % blocks

    def copy(i, target):
        return pltpu.make_async_remote_copy(
            src_ref=att_ref.at[i],
            dst_ref=out_ref.at[head],
            send_sem=send_sem.at[i],
            recv_sem=recv_sem.at[head],
            device_id=(target, tp),
            device_id_type=pl.DeviceIdType.MESH,
        )

    for i in range(per):
        target = per * mine + i

        @pl.when(target == me)
        def _():
            pltpu.make_async_copy(att_ref.at[i], out_ref.at[head], send_sem.at[i]).start()

        @pl.when(target != me)
        def _():
            copy(i, target).start()

    for i in range(per):
        target = per * mine + i

        @pl.when(target == me)
        def _():
            pltpu.make_async_copy(att_ref.at[i], out_ref.at[head], send_sem.at[i]).wait()

        @pl.when(target != me)
        def _():
            copy(i, target).wait_send()

    for h in range(heads):
        source = h * blocks + me // per

        @pl.when(source != me)
        def _():
            pltpu.make_async_remote_copy(
                src_ref=att_ref.at[0],
                dst_ref=out_ref.at[h],
                send_sem=send_sem.at[0],
                recv_sem=recv_sem.at[h],
                device_id=(source, tp),
                device_id_type=pl.DeviceIdType.MESH,
            ).wait_recv()


def gather_back(att, heads, blocks):
    per = att.shape[0]
    return pl.pallas_call(
        functools.partial(gather_kernel, blocks, per),
        out_shape=jax.ShapeDtypeStruct((heads,) + att.shape[1:], att.dtype),
        in_specs=[pl.BlockSpec(memory_space=pl.ANY)],
        out_specs=pl.BlockSpec(memory_space=pl.ANY),
        scratch_shapes=[pltpu.SemaphoreType.DMA((per,)), pltpu.SemaphoreType.DMA((heads,))],
        compiler_params=pltpu.CompilerParams(has_side_effects=True),
    )(att)


def shards(
    queries, keys, values, lengths, resid, w_out, moe_gain, routes, gates, w_gate_up, w_down
):
    seq_count = lax.axis_size("seq")
    me = lax.axis_index("seq")
    query_rows = queries.shape[0]
    local_heads = queries.shape[1] // HEAD_DIM
    cols = queries.shape[1]
    width = resid.shape[1]
    score_scale = 1.0 / math.sqrt(HEAD_DIM)
    longest = (seq_count * query_rows) // 2
    reach = min(seq_count - 1, -(-(longest - 1) // query_rows))
    blocks = seq_count // local_heads
    per = seq_count // blocks
    back = -(-reach // per) * per
    span = back + per
    head_q = queries.reshape(query_rows, local_heads, HEAD_DIM).transpose(1, 0, 2)
    head_kv = jnp.concatenate(
        [
            keys.reshape(query_rows, local_heads, HEAD_DIM),
            values.reshape(query_rows, local_heads, HEAD_DIM),
        ],
        axis=2,
    ).transpose(1, 0, 2)
    q_in, kv_in = spread(head_q, head_kv, blocks, per, back)
    mine = me % blocks
    query_pos = mine * per * query_rows + jnp.arange(per * query_rows, dtype=jnp.int32)
    key_pos = (mine * per - back) * query_rows + jnp.arange(span * query_rows, dtype=jnp.int32)
    kv_in = kv_in.reshape(span * query_rows, 2 * HEAD_DIM)
    kv_in = jnp.where((key_pos >= 0)[:, None], kv_in, jnp.zeros_like(kv_in))
    query_tenant = tenant_of(query_pos, lengths)
    key_tenant = tenant_of(key_pos, lengths)
    visible = (
        (key_tenant[None, :] == query_tenant[:, None])
        & (key_pos[None, :] <= query_pos[:, None])
        & (key_pos[None, :] >= 0)
    )
    scores = (
        jnp.dot(
            q_in.reshape(per * query_rows, HEAD_DIM),
            kv_in[:, :HEAD_DIM].T,
            preferred_element_type=jnp.float32,
        )
        * score_scale
    )
    scores = jnp.where(visible, scores, -1e30)
    new_max = jnp.max(scores, axis=1, keepdims=True)
    exponent = jnp.where(visible, jnp.exp(scores - new_max), 0.0)
    run_sum = jnp.sum(exponent, axis=1, keepdims=True)
    accumulated = jnp.dot(
        exponent.astype(jnp.bfloat16), kv_in[:, HEAD_DIM:], preferred_element_type=jnp.float32
    )
    head_att = (accumulated / run_sum).astype(jnp.bfloat16).reshape(per, query_rows, HEAD_DIM)
    attention = (
        gather_back(head_att, local_heads, blocks)
        .transpose(1, 0, 2)
        .reshape(query_rows, local_heads * HEAD_DIM)
    )
    projected = lax.psum_scatter(
        jnp.dot(attention, w_out, preferred_element_type=jnp.float32).astype(jnp.bfloat16),
        "tp",
        scatter_dimension=0,
        tiled=True,
    ).astype(jnp.float32)
    attended = (resid.astype(jnp.float32) + projected).astype(jnp.bfloat16)
    widened = attended.astype(jnp.float32)
    meansq = jnp.mean(widened * widened, axis=1, keepdims=True)
    normed = (widened * lax.rsqrt(meansq + 1e-05) * moe_gain[None, :]).astype(jnp.bfloat16)
    local_rows = resid.shape[0]
    top_count = routes.shape[1]
    owned = w_gate_up.shape[0]
    experts_all = owned * seq_count
    capacity = 3 * local_rows * top_count // (2 * experts_all)
    matches = routes[:, :, None] == jnp.arange(experts_all, dtype=jnp.int32)[None, None, :]
    member = jnp.any(matches, axis=1)
    slot = jnp.cumsum(member.astype(jnp.int32), axis=0) - 1
    place = member[:, :, None] & (
        slot[:, :, None] == jnp.arange(capacity, dtype=jnp.int32)[None, None, :]
    )
    buffer = jnp.einsum(
        "iec,id->ecd", place.astype(jnp.bfloat16), normed, preferred_element_type=jnp.float32
    ).astype(jnp.bfloat16)
    staged = buffer.reshape(seq_count, owned, capacity, width)
    returned_parts = []
    for part in range(owned):
        arrived = lax.all_to_all(staged[:, part], "seq", split_axis=0, concat_axis=0, tiled=True)
        expand_arrived = lax.all_gather(arrived, "tp", axis=0, tiled=True)
        projections = jnp.einsum(
            "ncd,dgf->ncgf", expand_arrived, w_gate_up[part], preferred_element_type=jnp.float32
        )
        hidden = (jax.nn.silu(projections[..., 0, :]) * projections[..., 1, :]).astype(
            jnp.bfloat16
        )
        summed = lax.psum_scatter(
            jnp.einsum("ncf,fd->ncd", hidden, w_down[part], preferred_element_type=jnp.float32)
            .astype(jnp.bfloat16),
            "tp",
            scatter_dimension=0,
            tiled=True,
        )
        returned_parts.append(
            lax.all_to_all(summed, "seq", split_axis=0, concat_axis=0, tiled=True)
        )
    returned = jnp.stack(returned_parts, axis=1)
    weight_of = jnp.sum(jnp.where(matches, gates[:, :, None], 0.0), axis=1)
    mix_weights = jnp.where(place, weight_of[:, :, None], 0.0)
    expert_mix = jnp.einsum(
        "iec,ecd->id",
        mix_weights,
        returned.reshape(experts_all, capacity, width).astype(jnp.float32),
        precision=lax.Precision.HIGHEST,
        preferred_element_type=jnp.float32,
    ).astype(jnp.bfloat16)
    return (attended, expert_mix)


def solution(mesh):
    return jax.shard_map(
        shards,
        mesh=mesh,
        in_specs=(
            P("seq", "tp"),
            P("seq", "tp"),
            P("seq", "tp"),
            P(),
            P(("seq", "tp"), None),
            P("tp", None),
            P(),
            P(("seq", "tp"), None),
            P(("seq", "tp"), None),
            P("seq", None, None, "tp"),
            P("seq", "tp", None),
        ),
        out_specs=(P(("seq", "tp"), None), P(("seq", "tp"), None)),
        check_vma=False,
    )
```

```python
import functools
import math

import jax
import jax.numpy as jnp
from jax import lax
from jax.experimental import pallas as pl
from jax.experimental.pallas import tpu as pltpu
from jax.sharding import PartitionSpec as P

HEAD_DIM = 128


def tenant_of(positions, lengths):
    bounds = jnp.cumsum(lengths)
    return jnp.sum((positions[:, None] >= bounds[None, :]).astype(jnp.int32), axis=1)


def spread_kernel(
    blocks, per, back, q_ref, kv_ref, q_out, kv_out, q_send, q_recv, kv_send, kv_recv
):
    me = lax.axis_index("seq")
    tp = lax.axis_index("tp")
    heads = q_ref.shape[0]
    span = back + per
    tries = back // per + 1
    mine = me % blocks

    def send(src, dst, sem, recv, target):
        @pl.when(target == me)
        def _():
            pltpu.make_async_copy(src, dst, sem).start()

        @pl.when(target != me)
        def _():
            pltpu.make_async_remote_copy(
                src_ref=src,
                dst_ref=dst,
                send_sem=sem,
                recv_sem=recv,
                device_id=(target, tp),
                device_id_type=pl.DeviceIdType.MESH,
            ).start()

    def finish_send(src, dst, sem, recv, target):
        @pl.when(target == me)
        def _():
            pltpu.make_async_copy(src, dst, sem).wait()

        @pl.when(target != me)
        def _():
            pltpu.make_async_remote_copy(
                src_ref=src,
                dst_ref=dst,
                send_sem=sem,
                recv_sem=recv,
                device_id=(target, tp),
                device_id_type=pl.DeviceIdType.MESH,
            ).wait_send()

    def finish_recv(src, dst, sem, recv, source):
        @pl.when(source != me)
        def _():
            pltpu.make_async_remote_copy(
                src_ref=src,
                dst_ref=dst,
                send_sem=sem,
                recv_sem=recv,
                device_id=(source, tp),
                device_id_type=pl.DeviceIdType.MESH,
            ).wait_recv()

    plan = []
    for h in range(heads):
        target = h * blocks + me // per
        plan.append((q_ref.at[h], q_out.at[me % per], q_send.at[h], q_recv.at[me % per], target))
        for r in range(tries):
            block = (me + back) // per - r
            slot = (me + back) % per + per * r
            plan.append(
                (
                    kv_ref.at[h],
                    kv_out.at[slot],
                    kv_send.at[h, r],
                    kv_recv.at[slot],
                    h * blocks + block,
                    (block >= 0) & (block < blocks),
                )
            )
    for item in plan:
        valid = item[5] if len(item) > 5 else True

        @pl.when(valid)
        def _():
            send(*item[:5])

    for item in plan:
        valid = item[5] if len(item) > 5 else True

        @pl.when(valid)
        def _():
            finish_send(*item[:5])

    for i in range(per):
        source = per * mine + i
        finish_recv(q_ref.at[0], q_out.at[i], q_send.at[0], q_recv.at[i], source)
    for slot in range(span):
        source = per * mine - back + slot

        @pl.when(source >= 0)
        def _():
            finish_recv(kv_ref.at[0], kv_out.at[slot], kv_send.at[0, 0], kv_recv.at[slot], source)


def spread(q, kv, blocks, per, back):
    heads = q.shape[0]
    span = back + per
    tries = back // per + 1
    return pl.pallas_call(
        functools.partial(spread_kernel, blocks, per, back),
        out_shape=(
            jax.ShapeDtypeStruct((per,) + q.shape[1:], q.dtype),
            jax.ShapeDtypeStruct((span,) + kv.shape[1:], kv.dtype),
        ),
        in_specs=[pl.BlockSpec(memory_space=pl.ANY)] * 2,
        out_specs=(pl.BlockSpec(memory_space=pl.ANY), pl.BlockSpec(memory_space=pl.ANY)),
        scratch_shapes=[
            pltpu.SemaphoreType.DMA((heads,)),
            pltpu.SemaphoreType.DMA((per,)),
            pltpu.SemaphoreType.DMA((heads, tries)),
            pltpu.SemaphoreType.DMA((span,)),
        ],
        compiler_params=pltpu.CompilerParams(has_side_effects=True),
    )(q, kv)


def gather_kernel(blocks, per, att_ref, out_ref, send_sem, recv_sem):
    me = lax.axis_index("seq")
    tp = lax.axis_index("tp")
    heads = out_ref.shape[0]
    head = me // blocks
    mine = me % blocks

    def copy(i, target):
        return pltpu.make_async_remote_copy(
            src_ref=att_ref.at[i],
            dst_ref=out_ref.at[head],
            send_sem=send_sem.at[i],
            recv_sem=recv_sem.at[head],
            device_id=(target, tp),
            device_id_type=pl.DeviceIdType.MESH,
        )

    for i in range(per):
        target = per * mine + i

        @pl.when(target == me)
        def _():
            pltpu.make_async_copy(att_ref.at[i], out_ref.at[head], send_sem.at[i]).start()

        @pl.when(target != me)
        def _():
            copy(i, target).start()

    for i in range(per):
        target = per * mine + i

        @pl.when(target == me)
        def _():
            pltpu.make_async_copy(att_ref.at[i], out_ref.at[head], send_sem.at[i]).wait()

        @pl.when(target != me)
        def _():
            copy(i, target).wait_send()

    for h in range(heads):
        source = h * blocks + me // per

        @pl.when(source != me)
        def _():
            pltpu.make_async_remote_copy(
                src_ref=att_ref.at[0],
                dst_ref=out_ref.at[h],
                send_sem=send_sem.at[0],
                recv_sem=recv_sem.at[h],
                device_id=(source, tp),
                device_id_type=pl.DeviceIdType.MESH,
            ).wait_recv()


def gather_back(att, heads, blocks):
    per = att.shape[0]
    return pl.pallas_call(
        functools.partial(gather_kernel, blocks, per),
        out_shape=jax.ShapeDtypeStruct((heads,) + att.shape[1:], att.dtype),
        in_specs=[pl.BlockSpec(memory_space=pl.ANY)],
        out_specs=pl.BlockSpec(memory_space=pl.ANY),
        scratch_shapes=[pltpu.SemaphoreType.DMA((per,)), pltpu.SemaphoreType.DMA((heads,))],
        compiler_params=pltpu.CompilerParams(has_side_effects=True),
    )(att)


def shards(
    queries, keys, values, lengths, resid, w_out, moe_gain, routes, gates, w_gate_up, w_down
):
    seq_count = lax.axis_size("seq")
    me = lax.axis_index("seq")
    query_rows = queries.shape[0]
    local_heads = queries.shape[1] // HEAD_DIM
    cols = queries.shape[1]
    width = resid.shape[1]
    score_scale = 1.0 / math.sqrt(HEAD_DIM)
    longest = (seq_count * query_rows) // 2
    reach = min(seq_count - 1, -(-(longest - 1) // query_rows))
    blocks = seq_count // local_heads
    per = seq_count // blocks
    back = -(-reach // per) * per
    span = back + per
    head_q = queries.reshape(query_rows, local_heads, HEAD_DIM).transpose(1, 0, 2)
    head_kv = jnp.concatenate(
        [
            keys.reshape(query_rows, local_heads, HEAD_DIM),
            values.reshape(query_rows, local_heads, HEAD_DIM),
        ],
        axis=2,
    ).transpose(1, 0, 2)
    q_in, kv_in = spread(head_q, head_kv, blocks, per, back)
    mine = me % blocks
    query_pos = mine * per * query_rows + jnp.arange(per * query_rows, dtype=jnp.int32)
    key_pos = (mine * per - back) * query_rows + jnp.arange(span * query_rows, dtype=jnp.int32)
    kv_in = kv_in.reshape(span * query_rows, 2 * HEAD_DIM)
    kv_in = jnp.where((key_pos >= 0)[:, None], kv_in, jnp.zeros_like(kv_in))
    query_tenant = tenant_of(query_pos, lengths)
    key_tenant = tenant_of(key_pos, lengths)
    visible = (
        (key_tenant[None, :] == query_tenant[:, None])
        & (key_pos[None, :] <= query_pos[:, None])
        & (key_pos[None, :] >= 0)
    )
    scores = (
        jnp.dot(
            q_in.reshape(per * query_rows, HEAD_DIM),
            kv_in[:, :HEAD_DIM].T,
            preferred_element_type=jnp.float32,
        )
        * score_scale
    )
    scores = jnp.where(visible, scores, -1e30)
    new_max = jnp.max(scores, axis=1, keepdims=True)
    exponent = jnp.where(visible, jnp.exp(scores - new_max), 0.0)
    run_sum = jnp.sum(exponent, axis=1, keepdims=True)
    accumulated = jnp.dot(
        exponent.astype(jnp.bfloat16), kv_in[:, HEAD_DIM:], preferred_element_type=jnp.float32
    )
    head_att = (accumulated / run_sum).astype(jnp.bfloat16).reshape(per, query_rows, HEAD_DIM)
    attention = (
        gather_back(head_att, local_heads, blocks)
        .transpose(1, 0, 2)
        .reshape(query_rows, local_heads * HEAD_DIM)
    )
    projected = lax.psum_scatter(
        jnp.dot(attention, w_out, preferred_element_type=jnp.float32).astype(jnp.bfloat16),
        "tp",
        scatter_dimension=0,
        tiled=True,
    ).astype(jnp.float32)
    attended = (resid.astype(jnp.float32) + projected).astype(jnp.bfloat16)
    widened = attended.astype(jnp.float32)
    meansq = jnp.mean(widened * widened, axis=1, keepdims=True)
    normed = (widened * lax.rsqrt(meansq + 1e-05) * moe_gain[None, :]).astype(jnp.bfloat16)
    local_rows = resid.shape[0]
    top_count = routes.shape[1]
    owned = w_gate_up.shape[0]
    experts_all = owned * seq_count
    capacity = 3 * local_rows * top_count // (2 * experts_all)
    far_swap = [(t, t ^ 2) for t in range(lax.axis_size("tp"))]
    near_swap = [(t, t ^ 1) for t in range(lax.axis_size("tp"))]
    pair_normed = jnp.stack([normed, lax.ppermute(normed, "tp", far_swap)])
    pair_routes = jnp.stack([routes, lax.ppermute(routes, "tp", far_swap)])
    pair_gates = jnp.stack([gates, lax.ppermute(gates, "tp", far_swap)])
    matches = pair_routes[..., None] == jnp.arange(experts_all, dtype=jnp.int32)
    member = jnp.any(matches, axis=2)
    slot = jnp.cumsum(member.astype(jnp.int32), axis=1) - 1
    place = member[..., None] & (slot[..., None] == jnp.arange(capacity, dtype=jnp.int32))
    buffer = jnp.einsum(
        "xiec,xid->excd", place.astype(jnp.bfloat16), pair_normed,
        preferred_element_type=jnp.float32,
    ).astype(jnp.bfloat16)
    arrived = lax.all_to_all(
        buffer.reshape(seq_count, owned, 2, capacity, width),
        "seq",
        split_axis=0,
        concat_axis=0,
        tiled=True,
    )
    both = jnp.stack([arrived, lax.ppermute(arrived, "tp", near_swap)])
    slots = both.transpose(2, 0, 1, 3, 4, 5).reshape(owned, -1, width)
    projections = jnp.einsum(
        "xnd,xdgf->xngf", slots, w_gate_up, preferred_element_type=jnp.float32
    )
    hidden = (jax.nn.silu(projections[..., 0, :]) * projections[..., 1, :]).astype(jnp.bfloat16)
    partial_out = (
        jnp.einsum("xnf,xfd->xnd", hidden, w_down, preferred_element_type=jnp.float32)
        .astype(jnp.bfloat16)
        .reshape(owned, 2, seq_count, 2, capacity, width)
    )
    from_near = lax.ppermute(partial_out[:, 1], "tp", near_swap)
    reduced = (partial_out[:, 0].astype(jnp.float32) + from_near.astype(jnp.float32)).astype(
        jnp.bfloat16
    )
    returned = lax.all_to_all(
        reduced.transpose(1, 0, 2, 3, 4), "seq", split_axis=0, concat_axis=0, tiled=True
    )
    weight_of = jnp.sum(jnp.where(matches, pair_gates[..., None], 0.0), axis=2)
    mix_weights = jnp.where(place, weight_of[..., None], 0.0)
    mixes = jnp.einsum(
        "xiec,xecd->xid",
        mix_weights,
        returned.transpose(2, 0, 1, 3, 4)
        .reshape(2, experts_all, capacity, width)
        .astype(jnp.float32),
        precision=lax.Precision.HIGHEST,
        preferred_element_type=jnp.float32,
    )
    expert_mix = (mixes[0] + lax.ppermute(mixes[1], "tp", far_swap)).astype(jnp.bfloat16)
    return (attended, expert_mix)


def solution(mesh):
    return jax.shard_map(
        shards,
        mesh=mesh,
        in_specs=(
            P("seq", "tp"),
            P("seq", "tp"),
            P("seq", "tp"),
            P(),
            P(("seq", "tp"), None),
            P("tp", None),
            P(),
            P(("seq", "tp"), None),
            P(("seq", "tp"), None),
            P("seq", None, None, "tp"),
            P("seq", "tp", None),
        ),
        out_specs=(P(("seq", "tp"), None), P(("seq", "tp"), None)),
        check_vma=False,
    )
```

```python
import functools
import math

import jax
import jax.numpy as jnp
from jax import lax
from jax.experimental import pallas as pl
from jax.experimental.pallas import tpu as pltpu
from jax.sharding import PartitionSpec as P

HEAD_DIM = 128


def tenant_of(positions, lengths):
    bounds = jnp.cumsum(lengths)
    return jnp.sum((positions[:, None] >= bounds[None, :]).astype(jnp.int32), axis=1)


def spread_kernel(
    blocks, per, back, q_ref, kv_ref, q_out, kv_out, q_send, q_recv, kv_send, kv_recv
):
    me = lax.axis_index("seq")
    tp = lax.axis_index("tp")
    heads = q_ref.shape[0]
    span = back + per
    tries = back // per + 1
    mine = me % blocks

    def send(src, dst, sem, recv, target):
        @pl.when(target == me)
        def _():
            pltpu.make_async_copy(src, dst, sem).start()

        @pl.when(target != me)
        def _():
            pltpu.make_async_remote_copy(
                src_ref=src,
                dst_ref=dst,
                send_sem=sem,
                recv_sem=recv,
                device_id=(target, tp),
                device_id_type=pl.DeviceIdType.MESH,
            ).start()

    def finish_send(src, dst, sem, recv, target):
        @pl.when(target == me)
        def _():
            pltpu.make_async_copy(src, dst, sem).wait()

        @pl.when(target != me)
        def _():
            pltpu.make_async_remote_copy(
                src_ref=src,
                dst_ref=dst,
                send_sem=sem,
                recv_sem=recv,
                device_id=(target, tp),
                device_id_type=pl.DeviceIdType.MESH,
            ).wait_send()

    def finish_recv(src, dst, sem, recv, source):
        @pl.when(source != me)
        def _():
            pltpu.make_async_remote_copy(
                src_ref=src,
                dst_ref=dst,
                send_sem=sem,
                recv_sem=recv,
                device_id=(source, tp),
                device_id_type=pl.DeviceIdType.MESH,
            ).wait_recv()

    plan = []
    for h in range(heads):
        target = h * blocks + me // per
        plan.append((q_ref.at[h], q_out.at[me % per], q_send.at[h], q_recv.at[me % per], target))
        for r in range(tries):
            block = (me + back) // per - r
            slot = (me + back) % per + per * r
            plan.append(
                (
                    kv_ref.at[h],
                    kv_out.at[slot],
                    kv_send.at[h, r],
                    kv_recv.at[slot],
                    h * blocks + block,
                    (block >= 0) & (block < blocks),
                )
            )
    for item in plan:
        valid = item[5] if len(item) > 5 else True

        @pl.when(valid)
        def _():
            send(*item[:5])

    for item in plan:
        valid = item[5] if len(item) > 5 else True

        @pl.when(valid)
        def _():
            finish_send(*item[:5])

    for i in range(per):
        source = per * mine + i
        finish_recv(q_ref.at[0], q_out.at[i], q_send.at[0], q_recv.at[i], source)
    for slot in range(span):
        source = per * mine - back + slot

        @pl.when(source >= 0)
        def _():
            finish_recv(kv_ref.at[0], kv_out.at[slot], kv_send.at[0, 0], kv_recv.at[slot], source)


def spread(q, kv, blocks, per, back):
    heads = q.shape[0]
    span = back + per
    tries = back // per + 1
    return pl.pallas_call(
        functools.partial(spread_kernel, blocks, per, back),
        out_shape=(
            jax.ShapeDtypeStruct((per,) + q.shape[1:], q.dtype),
            jax.ShapeDtypeStruct((span,) + kv.shape[1:], kv.dtype),
        ),
        in_specs=[pl.BlockSpec(memory_space=pl.ANY)] * 2,
        out_specs=(pl.BlockSpec(memory_space=pl.ANY), pl.BlockSpec(memory_space=pl.ANY)),
        scratch_shapes=[
            pltpu.SemaphoreType.DMA((heads,)),
            pltpu.SemaphoreType.DMA((per,)),
            pltpu.SemaphoreType.DMA((heads, tries)),
            pltpu.SemaphoreType.DMA((span,)),
        ],
        compiler_params=pltpu.CompilerParams(has_side_effects=True),
    )(q, kv)


def gather_kernel(blocks, per, att_ref, out_ref, send_sem, recv_sem):
    me = lax.axis_index("seq")
    tp = lax.axis_index("tp")
    heads = out_ref.shape[0]
    head = me // blocks
    mine = me % blocks

    def copy(i, target):
        return pltpu.make_async_remote_copy(
            src_ref=att_ref.at[i],
            dst_ref=out_ref.at[head],
            send_sem=send_sem.at[i],
            recv_sem=recv_sem.at[head],
            device_id=(target, tp),
            device_id_type=pl.DeviceIdType.MESH,
        )

    for i in range(per):
        target = per * mine + i

        @pl.when(target == me)
        def _():
            pltpu.make_async_copy(att_ref.at[i], out_ref.at[head], send_sem.at[i]).start()

        @pl.when(target != me)
        def _():
            copy(i, target).start()

    for i in range(per):
        target = per * mine + i

        @pl.when(target == me)
        def _():
            pltpu.make_async_copy(att_ref.at[i], out_ref.at[head], send_sem.at[i]).wait()

        @pl.when(target != me)
        def _():
            copy(i, target).wait_send()

    for h in range(heads):
        source = h * blocks + me // per

        @pl.when(source != me)
        def _():
            pltpu.make_async_remote_copy(
                src_ref=att_ref.at[0],
                dst_ref=out_ref.at[h],
                send_sem=send_sem.at[0],
                recv_sem=recv_sem.at[h],
                device_id=(source, tp),
                device_id_type=pl.DeviceIdType.MESH,
            ).wait_recv()


def gather_back(att, heads, blocks):
    per = att.shape[0]
    return pl.pallas_call(
        functools.partial(gather_kernel, blocks, per),
        out_shape=jax.ShapeDtypeStruct((heads,) + att.shape[1:], att.dtype),
        in_specs=[pl.BlockSpec(memory_space=pl.ANY)],
        out_specs=pl.BlockSpec(memory_space=pl.ANY),
        scratch_shapes=[pltpu.SemaphoreType.DMA((per,)), pltpu.SemaphoreType.DMA((heads,))],
        compiler_params=pltpu.CompilerParams(has_side_effects=True),
    )(att)


def shards(
    queries, keys, values, lengths, resid, w_out, moe_gain, routes, gates, w_gate_up, w_down
):
    seq_count = lax.axis_size("seq")
    me = lax.axis_index("seq")
    query_rows = queries.shape[0]
    local_heads = queries.shape[1] // HEAD_DIM
    cols = queries.shape[1]
    width = resid.shape[1]
    score_scale = 1.0 / math.sqrt(HEAD_DIM)
    longest = (seq_count * query_rows) // 2
    reach = min(seq_count - 1, -(-(longest - 1) // query_rows))
    blocks = seq_count // local_heads
    per = seq_count // blocks
    back = -(-reach // per) * per
    span = back + per
    head_q = queries.reshape(query_rows, local_heads, HEAD_DIM).transpose(1, 0, 2)
    head_kv = jnp.concatenate(
        [
            keys.reshape(query_rows, local_heads, HEAD_DIM),
            values.reshape(query_rows, local_heads, HEAD_DIM),
        ],
        axis=2,
    ).transpose(1, 0, 2)
    q_in, kv_in = spread(head_q, head_kv, blocks, per, back)
    mine = me % blocks
    query_pos = mine * per * query_rows + jnp.arange(per * query_rows, dtype=jnp.int32)
    key_pos = (mine * per - back) * query_rows + jnp.arange(span * query_rows, dtype=jnp.int32)
    kv_in = kv_in.reshape(span * query_rows, 2 * HEAD_DIM)
    kv_in = jnp.where((key_pos >= 0)[:, None], kv_in, jnp.zeros_like(kv_in))
    query_tenant = tenant_of(query_pos, lengths)
    key_tenant = tenant_of(key_pos, lengths)
    visible = (
        (key_tenant[None, :] == query_tenant[:, None])
        & (key_pos[None, :] <= query_pos[:, None])
        & (key_pos[None, :] >= 0)
    )
    scores = (
        jnp.dot(
            q_in.reshape(per * query_rows, HEAD_DIM),
            kv_in[:, :HEAD_DIM].T,
            preferred_element_type=jnp.float32,
        )
        * score_scale
    )
    scores = jnp.where(visible, scores, -1e30)
    new_max = jnp.max(scores, axis=1, keepdims=True)
    exponent = jnp.where(visible, jnp.exp(scores - new_max), 0.0)
    run_sum = jnp.sum(exponent, axis=1, keepdims=True)
    accumulated = jnp.dot(
        exponent.astype(jnp.bfloat16), kv_in[:, HEAD_DIM:], preferred_element_type=jnp.float32
    )
    head_att = (accumulated / run_sum).astype(jnp.bfloat16).reshape(per, query_rows, HEAD_DIM)
    attention = (
        gather_back(head_att, local_heads, blocks)
        .transpose(1, 0, 2)
        .reshape(query_rows, local_heads * HEAD_DIM)
    )
    projected = lax.psum_scatter(
        jnp.dot(attention, w_out, preferred_element_type=jnp.float32).astype(jnp.bfloat16),
        "tp",
        scatter_dimension=0,
        tiled=True,
    ).astype(jnp.float32)
    attended = (resid.astype(jnp.float32) + projected).astype(jnp.bfloat16)
    widened = attended.astype(jnp.float32)
    meansq = jnp.mean(widened * widened, axis=1, keepdims=True)
    normed = (widened * lax.rsqrt(meansq + 1e-05) * moe_gain[None, :]).astype(jnp.bfloat16)
    local_rows = resid.shape[0]
    top_count = routes.shape[1]
    owned = w_gate_up.shape[0]
    experts_all = owned * seq_count
    capacity = 3 * local_rows * top_count // (2 * experts_all)
    far_swap = [(t, t ^ 2) for t in range(lax.axis_size("tp"))]
    near_swap = [(t, t ^ 1) for t in range(lax.axis_size("tp"))]
    pair_normed = jnp.stack([normed, lax.ppermute(normed, "tp", far_swap)])
    pair_routes = jnp.stack([routes, lax.ppermute(routes, "tp", far_swap)])
    pair_gates = jnp.stack([gates, lax.ppermute(gates, "tp", far_swap)])
    matches = pair_routes[..., None] == jnp.arange(experts_all, dtype=jnp.int32)
    member = jnp.any(matches, axis=2)
    slot = jnp.cumsum(member.astype(jnp.int32), axis=1) - 1
    place = member[..., None] & (slot[..., None] == jnp.arange(capacity, dtype=jnp.int32))
    buffer = jnp.einsum(
        "xiec,xid->excd", place.astype(jnp.bfloat16), pair_normed,
        preferred_element_type=jnp.float32,
    ).astype(jnp.bfloat16)
    buffer = buffer.reshape(seq_count, owned, 2, capacity, width).transpose(1, 0, 2, 3, 4)
    arrived = lax.all_to_all(buffer, "seq", split_axis=1, concat_axis=1, tiled=True)
    near = lax.ppermute(arrived, "tp", near_swap)

    def expert_part(slots):
        projections = jnp.einsum(
            "xnd,xdgf->xngf", slots.reshape(owned, -1, width), w_gate_up,
            preferred_element_type=jnp.float32,
        )
        hidden = (jax.nn.silu(projections[..., 0, :]) * projections[..., 1, :]).astype(
            jnp.bfloat16
        )
        return jnp.einsum(
            "xnf,xfd->xnd", hidden, w_down, preferred_element_type=jnp.float32
        ).astype(jnp.bfloat16)

    from_near = lax.ppermute(expert_part(near), "tp", near_swap)
    reduced = (
        expert_part(arrived).astype(jnp.float32) + from_near.astype(jnp.float32)
    ).astype(jnp.bfloat16)
    returned = lax.all_to_all(
        reduced.reshape(arrived.shape), "seq", split_axis=1, concat_axis=1, tiled=True
    )
    weight_of = jnp.sum(jnp.where(matches, pair_gates[..., None], 0.0), axis=2)
    mix_weights = jnp.where(place, weight_of[..., None], 0.0)
    mixes = jnp.einsum(
        "xiec,xecd->xid",
        mix_weights,
        returned.transpose(2, 1, 0, 3, 4)
        .reshape(2, experts_all, capacity, width)
        .astype(jnp.float32),
        precision=lax.Precision.HIGHEST,
        preferred_element_type=jnp.float32,
    )
    expert_mix = (mixes[0] + lax.ppermute(mixes[1], "tp", far_swap)).astype(jnp.bfloat16)
    return (attended, expert_mix)


def solution(mesh):
    return jax.shard_map(
        shards,
        mesh=mesh,
        in_specs=(
            P("seq", "tp"),
            P("seq", "tp"),
            P("seq", "tp"),
            P(),
            P(("seq", "tp"), None),
            P("tp", None),
            P(),
            P(("seq", "tp"), None),
            P(("seq", "tp"), None),
            P("seq", None, None, "tp"),
            P("seq", "tp", None),
        ),
        out_specs=(P(("seq", "tp"), None), P(("seq", "tp"), None)),
        check_vma=False,
    )
```

```python
import functools
import math

import jax
import jax.numpy as jnp
from jax import lax
from jax.experimental import pallas as pl
from jax.experimental.pallas import tpu as pltpu
from jax.sharding import PartitionSpec as P

HEAD_DIM = 128


def tenant_of(positions, lengths):
    bounds = jnp.cumsum(lengths)
    return jnp.sum((positions[:, None] >= bounds[None, :]).astype(jnp.int32), axis=1)


def spread_kernel(
    blocks, per, back, q_ref, kv_ref, q_out, kv_out, q_send, q_recv, kv_send, kv_recv
):
    me = lax.axis_index("seq")
    tp = lax.axis_index("tp")
    heads = q_ref.shape[0]
    span = back + per
    tries = back // per + 1
    mine = me % blocks

    def send(src, dst, sem, recv, target):
        @pl.when(target == me)
        def _():
            pltpu.make_async_copy(src, dst, sem).start()

        @pl.when(target != me)
        def _():
            pltpu.make_async_remote_copy(
                src_ref=src,
                dst_ref=dst,
                send_sem=sem,
                recv_sem=recv,
                device_id=(target, tp),
                device_id_type=pl.DeviceIdType.MESH,
            ).start()

    def finish_send(src, dst, sem, recv, target):
        @pl.when(target == me)
        def _():
            pltpu.make_async_copy(src, dst, sem).wait()

        @pl.when(target != me)
        def _():
            pltpu.make_async_remote_copy(
                src_ref=src,
                dst_ref=dst,
                send_sem=sem,
                recv_sem=recv,
                device_id=(target, tp),
                device_id_type=pl.DeviceIdType.MESH,
            ).wait_send()

    def finish_recv(src, dst, sem, recv, source):
        @pl.when(source != me)
        def _():
            pltpu.make_async_remote_copy(
                src_ref=src,
                dst_ref=dst,
                send_sem=sem,
                recv_sem=recv,
                device_id=(source, tp),
                device_id_type=pl.DeviceIdType.MESH,
            ).wait_recv()

    plan = []
    for h in range(heads):
        target = h * blocks + me // per
        plan.append((q_ref.at[h], q_out.at[me % per], q_send.at[h], q_recv.at[me % per], target))
        for r in range(tries):
            block = (me + back) // per - r
            slot = (me + back) % per + per * r
            plan.append(
                (
                    kv_ref.at[h],
                    kv_out.at[slot],
                    kv_send.at[h, r],
                    kv_recv.at[slot],
                    h * blocks + block,
                    (block >= 0) & (block < blocks),
                )
            )
    for item in plan:
        valid = item[5] if len(item) > 5 else True

        @pl.when(valid)
        def _():
            send(*item[:5])

    for item in plan:
        valid = item[5] if len(item) > 5 else True

        @pl.when(valid)
        def _():
            finish_send(*item[:5])

    for i in range(per):
        source = per * mine + i
        finish_recv(q_ref.at[0], q_out.at[i], q_send.at[0], q_recv.at[i], source)
    for slot in range(span):
        source = per * mine - back + slot

        @pl.when(source >= 0)
        def _():
            finish_recv(kv_ref.at[0], kv_out.at[slot], kv_send.at[0, 0], kv_recv.at[slot], source)


def spread(q, kv, blocks, per, back):
    heads = q.shape[0]
    span = back + per
    tries = back // per + 1
    return pl.pallas_call(
        functools.partial(spread_kernel, blocks, per, back),
        out_shape=(
            jax.ShapeDtypeStruct((per,) + q.shape[1:], q.dtype),
            jax.ShapeDtypeStruct((span,) + kv.shape[1:], kv.dtype),
        ),
        in_specs=[pl.BlockSpec(memory_space=pl.ANY)] * 2,
        out_specs=(pl.BlockSpec(memory_space=pl.ANY), pl.BlockSpec(memory_space=pl.ANY)),
        scratch_shapes=[
            pltpu.SemaphoreType.DMA((heads,)),
            pltpu.SemaphoreType.DMA((per,)),
            pltpu.SemaphoreType.DMA((heads, tries)),
            pltpu.SemaphoreType.DMA((span,)),
        ],
        compiler_params=pltpu.CompilerParams(has_side_effects=True),
    )(q, kv)


def gather_kernel(blocks, per, att_ref, out_ref, send_sem, recv_sem):
    me = lax.axis_index("seq")
    tp = lax.axis_index("tp")
    heads = out_ref.shape[0]
    head = me // blocks
    mine = me % blocks

    def copy(i, target):
        return pltpu.make_async_remote_copy(
            src_ref=att_ref.at[i],
            dst_ref=out_ref.at[head],
            send_sem=send_sem.at[i],
            recv_sem=recv_sem.at[head],
            device_id=(target, tp),
            device_id_type=pl.DeviceIdType.MESH,
        )

    for i in range(per):
        target = per * mine + i

        @pl.when(target == me)
        def _():
            pltpu.make_async_copy(att_ref.at[i], out_ref.at[head], send_sem.at[i]).start()

        @pl.when(target != me)
        def _():
            copy(i, target).start()

    for i in range(per):
        target = per * mine + i

        @pl.when(target == me)
        def _():
            pltpu.make_async_copy(att_ref.at[i], out_ref.at[head], send_sem.at[i]).wait()

        @pl.when(target != me)
        def _():
            copy(i, target).wait_send()

    for h in range(heads):
        source = h * blocks + me // per

        @pl.when(source != me)
        def _():
            pltpu.make_async_remote_copy(
                src_ref=att_ref.at[0],
                dst_ref=out_ref.at[h],
                send_sem=send_sem.at[0],
                recv_sem=recv_sem.at[h],
                device_id=(source, tp),
                device_id_type=pl.DeviceIdType.MESH,
            ).wait_recv()


def gather_back(att, heads, blocks):
    per = att.shape[0]
    return pl.pallas_call(
        functools.partial(gather_kernel, blocks, per),
        out_shape=jax.ShapeDtypeStruct((heads,) + att.shape[1:], att.dtype),
        in_specs=[pl.BlockSpec(memory_space=pl.ANY)],
        out_specs=pl.BlockSpec(memory_space=pl.ANY),
        scratch_shapes=[pltpu.SemaphoreType.DMA((per,)), pltpu.SemaphoreType.DMA((heads,))],
        compiler_params=pltpu.CompilerParams(has_side_effects=True),
    )(att)


def shards(
    queries, keys, values, lengths, resid, w_out, moe_gain, routes, gates, w_gate_up, w_down
):
    seq_count = lax.axis_size("seq")
    me = lax.axis_index("seq")
    query_rows = queries.shape[0]
    local_heads = queries.shape[1] // HEAD_DIM
    cols = queries.shape[1]
    width = resid.shape[1]
    score_scale = 1.0 / math.sqrt(HEAD_DIM)
    longest = (seq_count * query_rows) // 2
    reach = min(seq_count - 1, -(-(longest - 1) // query_rows))
    blocks = seq_count // local_heads
    per = seq_count // blocks
    back = -(-reach // per) * per
    span = back + per
    head_q = queries.reshape(query_rows, local_heads, HEAD_DIM).transpose(1, 0, 2)
    head_kv = jnp.concatenate(
        [
            keys.reshape(query_rows, local_heads, HEAD_DIM),
            values.reshape(query_rows, local_heads, HEAD_DIM),
        ],
        axis=2,
    ).transpose(1, 0, 2)
    q_in, kv_in = spread(head_q, head_kv, blocks, per, back)
    mine = me % blocks
    query_pos = mine * per * query_rows + jnp.arange(per * query_rows, dtype=jnp.int32)
    key_pos = (mine * per - back) * query_rows + jnp.arange(span * query_rows, dtype=jnp.int32)
    kv_in = kv_in.reshape(span * query_rows, 2 * HEAD_DIM)
    kv_in = jnp.where((key_pos >= 0)[:, None], kv_in, jnp.zeros_like(kv_in))
    query_tenant = tenant_of(query_pos, lengths)
    key_tenant = tenant_of(key_pos, lengths)
    visible = (
        (key_tenant[None, :] == query_tenant[:, None])
        & (key_pos[None, :] <= query_pos[:, None])
        & (key_pos[None, :] >= 0)
    )
    scores = (
        jnp.dot(
            q_in.reshape(per * query_rows, HEAD_DIM),
            kv_in[:, :HEAD_DIM].T,
            preferred_element_type=jnp.float32,
        )
        * score_scale
    )
    scores = jnp.where(visible, scores, -1e30)
    new_max = jnp.max(scores, axis=1, keepdims=True)
    exponent = jnp.where(visible, jnp.exp(scores - new_max), 0.0)
    run_sum = jnp.sum(exponent, axis=1, keepdims=True)
    accumulated = jnp.dot(
        exponent.astype(jnp.bfloat16), kv_in[:, HEAD_DIM:], preferred_element_type=jnp.float32
    )
    head_att = (accumulated / run_sum).astype(jnp.bfloat16).reshape(per, query_rows, HEAD_DIM)
    attention = (
        gather_back(head_att, local_heads, blocks)
        .transpose(1, 0, 2)
        .reshape(query_rows, local_heads * HEAD_DIM)
    )
    tp_index = lax.axis_index("tp")
    near_swap = [(t, t ^ 1) for t in range(lax.axis_size("tp"))]
    far_swap = [(t, t ^ 2) for t in range(lax.axis_size("tp"))]
    local_rows = resid.shape[0]
    partial_proj = jnp.dot(attention, w_out, preferred_element_type=jnp.float32).reshape(
        2, 2, local_rows, width
    )
    core = tp_index % 2
    keep = lax.dynamic_index_in_dim(partial_proj, core, axis=1, keepdims=False)
    give = lax.dynamic_index_in_dim(partial_proj, 1 - core, axis=1, keepdims=False)
    half = keep + lax.ppermute(give.astype(jnp.bfloat16), "tp", near_swap).astype(jnp.float32)
    far = tp_index // 2
    keep = lax.dynamic_index_in_dim(half, far, axis=0, keepdims=False)
    give = lax.dynamic_index_in_dim(half, 1 - far, axis=0, keepdims=False)
    projected = keep + lax.ppermute(give.astype(jnp.bfloat16), "tp", far_swap).astype(
        jnp.float32
    )
    attended = (resid.astype(jnp.float32) + projected).astype(jnp.bfloat16)
    widened = attended.astype(jnp.float32)
    meansq = jnp.mean(widened * widened, axis=1, keepdims=True)
    normed = (widened * lax.rsqrt(meansq + 1e-05) * moe_gain[None, :]).astype(jnp.bfloat16)
    local_rows = resid.shape[0]
    top_count = routes.shape[1]
    owned = w_gate_up.shape[0]
    experts_all = owned * seq_count
    capacity = 3 * local_rows * top_count // (2 * experts_all)
    pair_normed = jnp.stack([normed, lax.ppermute(normed, "tp", far_swap)])
    pair_routes = jnp.stack([routes, lax.ppermute(routes, "tp", far_swap)])
    pair_gates = jnp.stack([gates, lax.ppermute(gates, "tp", far_swap)])
    matches = pair_routes[..., None] == jnp.arange(experts_all, dtype=jnp.int32)
    member = jnp.any(matches, axis=2)
    slot = jnp.cumsum(member.astype(jnp.int32), axis=1) - 1
    place = member[..., None] & (slot[..., None] == jnp.arange(capacity, dtype=jnp.int32))
    buffer = jnp.einsum(
        "xiec,xid->excd", place.astype(jnp.bfloat16), pair_normed,
        preferred_element_type=jnp.float32,
    ).astype(jnp.bfloat16)
    buffer = buffer.reshape(seq_count, owned, 2, capacity, width).transpose(1, 0, 2, 3, 4)
    arrived = lax.all_to_all(buffer, "seq", split_axis=1, concat_axis=1, tiled=True)
    near = lax.ppermute(arrived, "tp", near_swap)

    def expert_part(slots):
        projections = jnp.einsum(
            "xnd,xdgf->xngf", slots.reshape(owned, -1, width), w_gate_up,
            preferred_element_type=jnp.float32,
        )
        hidden = (jax.nn.silu(projections[..., 0, :]) * projections[..., 1, :]).astype(
            jnp.bfloat16
        )
        return jnp.einsum(
            "xnf,xfd->xnd", hidden, w_down, preferred_element_type=jnp.float32
        ).astype(jnp.bfloat16)

    from_near = lax.ppermute(expert_part(near), "tp", near_swap)
    reduced = (
        expert_part(arrived).astype(jnp.float32) + from_near.astype(jnp.float32)
    ).astype(jnp.bfloat16)
    returned = lax.all_to_all(
        reduced.reshape(arrived.shape), "seq", split_axis=1, concat_axis=1, tiled=True
    )
    weight_of = jnp.sum(jnp.where(matches, pair_gates[..., None], 0.0), axis=2)
    mix_weights = jnp.where(place, weight_of[..., None], 0.0)
    mixes = jnp.einsum(
        "xiec,xecd->xid",
        mix_weights,
        returned.transpose(2, 1, 0, 3, 4)
        .reshape(2, experts_all, capacity, width)
        .astype(jnp.float32),
        precision=lax.Precision.HIGHEST,
        preferred_element_type=jnp.float32,
    )
    expert_mix = (mixes[0] + lax.ppermute(mixes[1], "tp", far_swap)).astype(jnp.bfloat16)
    return (attended, expert_mix)


def solution(mesh):
    return jax.shard_map(
        shards,
        mesh=mesh,
        in_specs=(
            P("seq", "tp"),
            P("seq", "tp"),
            P("seq", "tp"),
            P(),
            P(("seq", "tp"), None),
            P("tp", None),
            P(),
            P(("seq", "tp"), None),
            P(("seq", "tp"), None),
            P("seq", None, None, "tp"),
            P("seq", "tp", None),
        ),
        out_specs=(P(("seq", "tp"), None), P(("seq", "tp"), None)),
        check_vma=False,
    )
```

```python
import functools
import math

import jax
import jax.numpy as jnp
from jax import lax
from jax.experimental import pallas as pl
from jax.experimental.pallas import tpu as pltpu
from jax.sharding import PartitionSpec as P

HEAD_DIM = 128


def tenant_of(positions, lengths):
    bounds = jnp.cumsum(lengths)
    return jnp.sum((positions[:, None] >= bounds[None, :]).astype(jnp.int32), axis=1)


def spread_kernel(
    blocks, per, back, q_ref, kv_ref, q_out, kv_out, q_send, q_recv, kv_send, kv_recv
):
    me = lax.axis_index("seq")
    tp = lax.axis_index("tp")
    heads = q_ref.shape[0]
    span = back + per
    tries = back // per + 1
    mine = me % blocks

    def send(src, dst, sem, recv, target):
        @pl.when(target == me)
        def _():
            pltpu.make_async_copy(src, dst, sem).start()

        @pl.when(target != me)
        def _():
            pltpu.make_async_remote_copy(
                src_ref=src,
                dst_ref=dst,
                send_sem=sem,
                recv_sem=recv,
                device_id=(target, tp),
                device_id_type=pl.DeviceIdType.MESH,
            ).start()

    def finish_send(src, dst, sem, recv, target):
        @pl.when(target == me)
        def _():
            pltpu.make_async_copy(src, dst, sem).wait()

        @pl.when(target != me)
        def _():
            pltpu.make_async_remote_copy(
                src_ref=src,
                dst_ref=dst,
                send_sem=sem,
                recv_sem=recv,
                device_id=(target, tp),
                device_id_type=pl.DeviceIdType.MESH,
            ).wait_send()

    def finish_recv(src, dst, sem, recv, source):
        @pl.when(source != me)
        def _():
            pltpu.make_async_remote_copy(
                src_ref=src,
                dst_ref=dst,
                send_sem=sem,
                recv_sem=recv,
                device_id=(source, tp),
                device_id_type=pl.DeviceIdType.MESH,
            ).wait_recv()

    plan = []
    for h in range(heads):
        target = h * blocks + me // per
        plan.append((q_ref.at[h], q_out.at[me % per], q_send.at[h], q_recv.at[me % per], target))
        for r in range(tries):
            block = (me + back) // per - r
            slot = (me + back) % per + per * r
            plan.append(
                (
                    kv_ref.at[h],
                    kv_out.at[slot],
                    kv_send.at[h, r],
                    kv_recv.at[slot],
                    h * blocks + block,
                    (block >= 0) & (block < blocks),
                )
            )
    for item in plan:
        valid = item[5] if len(item) > 5 else True

        @pl.when(valid)
        def _():
            send(*item[:5])

    for item in plan:
        valid = item[5] if len(item) > 5 else True

        @pl.when(valid)
        def _():
            finish_send(*item[:5])

    for i in range(per):
        source = per * mine + i
        finish_recv(q_ref.at[0], q_out.at[i], q_send.at[0], q_recv.at[i], source)
    for slot in range(span):
        source = per * mine - back + slot

        @pl.when(source >= 0)
        def _():
            finish_recv(kv_ref.at[0], kv_out.at[slot], kv_send.at[0, 0], kv_recv.at[slot], source)


def spread(q, kv, blocks, per, back):
    heads = q.shape[0]
    span = back + per
    tries = back // per + 1
    return pl.pallas_call(
        functools.partial(spread_kernel, blocks, per, back),
        out_shape=(
            jax.ShapeDtypeStruct((per,) + q.shape[1:], q.dtype),
            jax.ShapeDtypeStruct((span,) + kv.shape[1:], kv.dtype),
        ),
        in_specs=[pl.BlockSpec(memory_space=pl.ANY)] * 2,
        out_specs=(pl.BlockSpec(memory_space=pl.ANY), pl.BlockSpec(memory_space=pl.ANY)),
        scratch_shapes=[
            pltpu.SemaphoreType.DMA((heads,)),
            pltpu.SemaphoreType.DMA((per,)),
            pltpu.SemaphoreType.DMA((heads, tries)),
            pltpu.SemaphoreType.DMA((span,)),
        ],
        compiler_params=pltpu.CompilerParams(has_side_effects=True),
    )(q, kv)


def gather_kernel(blocks, per, att_ref, out_ref, send_sem, recv_sem):
    me = lax.axis_index("seq")
    tp = lax.axis_index("tp")
    heads = out_ref.shape[0]
    head = me // blocks
    mine = me % blocks

    def copy(i, target):
        return pltpu.make_async_remote_copy(
            src_ref=att_ref.at[i],
            dst_ref=out_ref.at[head],
            send_sem=send_sem.at[i],
            recv_sem=recv_sem.at[head],
            device_id=(target, tp),
            device_id_type=pl.DeviceIdType.MESH,
        )

    for i in range(per):
        target = per * mine + i

        @pl.when(target == me)
        def _():
            pltpu.make_async_copy(att_ref.at[i], out_ref.at[head], send_sem.at[i]).start()

        @pl.when(target != me)
        def _():
            copy(i, target).start()

    for i in range(per):
        target = per * mine + i

        @pl.when(target == me)
        def _():
            pltpu.make_async_copy(att_ref.at[i], out_ref.at[head], send_sem.at[i]).wait()

        @pl.when(target != me)
        def _():
            copy(i, target).wait_send()

    for h in range(heads):
        source = h * blocks + me // per

        @pl.when(source != me)
        def _():
            pltpu.make_async_remote_copy(
                src_ref=att_ref.at[0],
                dst_ref=out_ref.at[h],
                send_sem=send_sem.at[0],
                recv_sem=recv_sem.at[h],
                device_id=(source, tp),
                device_id_type=pl.DeviceIdType.MESH,
            ).wait_recv()


def gather_back(att, heads, blocks):
    per = att.shape[0]
    return pl.pallas_call(
        functools.partial(gather_kernel, blocks, per),
        out_shape=jax.ShapeDtypeStruct((heads,) + att.shape[1:], att.dtype),
        in_specs=[pl.BlockSpec(memory_space=pl.ANY)],
        out_specs=pl.BlockSpec(memory_space=pl.ANY),
        scratch_shapes=[pltpu.SemaphoreType.DMA((per,)), pltpu.SemaphoreType.DMA((heads,))],
        compiler_params=pltpu.CompilerParams(has_side_effects=True),
    )(att)


def shards(
    queries, keys, values, lengths, resid, w_out, moe_gain, routes, gates, w_gate_up, w_down
):
    seq_count = lax.axis_size("seq")
    me = lax.axis_index("seq")
    query_rows = queries.shape[0]
    local_heads = queries.shape[1] // HEAD_DIM
    cols = queries.shape[1]
    width = resid.shape[1]
    score_scale = 1.0 / math.sqrt(HEAD_DIM)
    longest = (seq_count * query_rows) // 2
    reach = min(seq_count - 1, -(-(longest - 1) // query_rows))
    blocks = seq_count // local_heads
    per = seq_count // blocks
    back = -(-reach // per) * per
    span = back + per
    head_q = queries.reshape(query_rows, local_heads, HEAD_DIM).transpose(1, 0, 2)
    head_kv = jnp.concatenate(
        [
            keys.reshape(query_rows, local_heads, HEAD_DIM),
            values.reshape(query_rows, local_heads, HEAD_DIM),
        ],
        axis=2,
    ).transpose(1, 0, 2)
    q_in, kv_in = spread(head_q, head_kv, blocks, per, back)
    mine = me % blocks
    query_pos = mine * per * query_rows + jnp.arange(per * query_rows, dtype=jnp.int32)
    key_pos = (mine * per - back) * query_rows + jnp.arange(span * query_rows, dtype=jnp.int32)
    kv_in = kv_in.reshape(span * query_rows, 2 * HEAD_DIM)
    kv_in = jnp.where((key_pos >= 0)[:, None], kv_in, jnp.zeros_like(kv_in))
    query_tenant = tenant_of(query_pos, lengths)
    key_tenant = tenant_of(key_pos, lengths)
    visible = (
        (key_tenant[None, :] == query_tenant[:, None])
        & (key_pos[None, :] <= query_pos[:, None])
        & (key_pos[None, :] >= 0)
    )
    scores = (
        jnp.dot(
            q_in.reshape(per * query_rows, HEAD_DIM),
            kv_in[:, :HEAD_DIM].T,
            preferred_element_type=jnp.float32,
        )
        * score_scale
    )
    scores = jnp.where(visible, scores, -1e30)
    new_max = jnp.max(scores, axis=1, keepdims=True)
    exponent = jnp.where(visible, jnp.exp(scores - new_max), 0.0)
    run_sum = jnp.sum(exponent, axis=1, keepdims=True)
    accumulated = jnp.dot(
        exponent.astype(jnp.bfloat16), kv_in[:, HEAD_DIM:], preferred_element_type=jnp.float32
    )
    head_att = (accumulated / run_sum).astype(jnp.bfloat16).reshape(per, query_rows, HEAD_DIM)
    attention = (
        gather_back(head_att, local_heads, blocks)
        .transpose(1, 0, 2)
        .reshape(query_rows, local_heads * HEAD_DIM)
    )
    tp_index = lax.axis_index("tp")
    near_swap = [(t, t ^ 1) for t in range(lax.axis_size("tp"))]
    far_swap = [(t, t ^ 2) for t in range(lax.axis_size("tp"))]
    local_rows = resid.shape[0]
    partial_proj = jnp.dot(attention, w_out, preferred_element_type=jnp.float32).reshape(
        2, 2, local_rows, width
    )
    core = tp_index % 2
    keep = lax.dynamic_index_in_dim(partial_proj, core, axis=1, keepdims=False)
    give = lax.dynamic_index_in_dim(partial_proj, 1 - core, axis=1, keepdims=False)
    half = keep + lax.ppermute(give.astype(jnp.bfloat16), "tp", near_swap).astype(jnp.float32)
    far = tp_index // 2
    pair_resid = jnp.stack([resid, lax.ppermute(resid, "tp", far_swap)])
    pair_routes = jnp.stack([routes, lax.ppermute(routes, "tp", far_swap)])
    pair_gates = jnp.stack([gates, lax.ppermute(gates, "tp", far_swap)])
    half = half.astype(jnp.bfloat16)
    total = half.astype(jnp.float32) + lax.ppermute(half, "tp", far_swap).astype(jnp.float32)
    pair_proj = jnp.stack(
        [
            lax.dynamic_index_in_dim(total, far, axis=0, keepdims=False),
            lax.dynamic_index_in_dim(total, 1 - far, axis=0, keepdims=False),
        ]
    )
    pair_attended = (pair_resid.astype(jnp.float32) + pair_proj).astype(jnp.bfloat16)
    attended = pair_attended[0]
    widened = pair_attended.astype(jnp.float32)
    meansq = jnp.mean(widened * widened, axis=2, keepdims=True)
    pair_normed = (widened * lax.rsqrt(meansq + 1e-05) * moe_gain).astype(jnp.bfloat16)
    top_count = routes.shape[1]
    owned = w_gate_up.shape[0]
    experts_all = owned * seq_count
    capacity = 3 * local_rows * top_count // (2 * experts_all)
    matches = pair_routes[..., None] == jnp.arange(experts_all, dtype=jnp.int32)
    member = jnp.any(matches, axis=2)
    slot = jnp.cumsum(member.astype(jnp.int32), axis=1) - 1
    place = member[..., None] & (slot[..., None] == jnp.arange(capacity, dtype=jnp.int32))
    buffer = jnp.einsum(
        "xiec,xid->excd", place.astype(jnp.bfloat16), pair_normed,
        preferred_element_type=jnp.float32,
    ).astype(jnp.bfloat16)
    buffer = buffer.reshape(seq_count, owned, 2, capacity, width).transpose(1, 0, 2, 3, 4)
    arrived = lax.all_to_all(buffer, "seq", split_axis=1, concat_axis=1, tiled=True)
    near = lax.ppermute(arrived, "tp", near_swap)

    def expert_part(slots):
        projections = jnp.einsum(
            "xnd,xdgf->xngf", slots.reshape(owned, -1, width), w_gate_up,
            preferred_element_type=jnp.float32,
        )
        hidden = (jax.nn.silu(projections[..., 0, :]) * projections[..., 1, :]).astype(
            jnp.bfloat16
        )
        return jnp.einsum(
            "xnf,xfd->xnd", hidden, w_down, preferred_element_type=jnp.float32
        ).astype(jnp.bfloat16)

    from_near = lax.ppermute(expert_part(near), "tp", near_swap)
    reduced = (
        expert_part(arrived).astype(jnp.float32) + from_near.astype(jnp.float32)
    ).astype(jnp.bfloat16)
    returned = lax.all_to_all(
        reduced.reshape(arrived.shape), "seq", split_axis=1, concat_axis=1, tiled=True
    )
    weight_of = jnp.sum(jnp.where(matches, pair_gates[..., None], 0.0), axis=2)
    mix_weights = jnp.where(place, weight_of[..., None], 0.0)
    mixes = jnp.einsum(
        "xiec,xecd->xid",
        mix_weights,
        returned.transpose(2, 1, 0, 3, 4)
        .reshape(2, experts_all, capacity, width)
        .astype(jnp.float32),
        precision=lax.Precision.HIGHEST,
        preferred_element_type=jnp.float32,
    )
    expert_mix = (mixes[0] + lax.ppermute(mixes[1], "tp", far_swap)).astype(jnp.bfloat16)
    return (attended, expert_mix)


def solution(mesh):
    return jax.shard_map(
        shards,
        mesh=mesh,
        in_specs=(
            P("seq", "tp"),
            P("seq", "tp"),
            P("seq", "tp"),
            P(),
            P(("seq", "tp"), None),
            P("tp", None),
            P(),
            P(("seq", "tp"), None),
            P(("seq", "tp"), None),
            P("seq", None, None, "tp"),
            P("seq", "tp", None),
        ),
        out_specs=(P(("seq", "tp"), None), P(("seq", "tp"), None)),
        check_vma=False,
    )
```

```python
import functools
import math

import jax
import jax.numpy as jnp
from jax import lax
from jax.experimental import pallas as pl
from jax.experimental.pallas import tpu as pltpu
from jax.sharding import PartitionSpec as P

HEAD_DIM = 128


def tenant_of(positions, lengths):
    bounds = jnp.cumsum(lengths)
    return jnp.sum((positions[:, None] >= bounds[None, :]).astype(jnp.int32), axis=1)


def spread_kernel(
    blocks, per, back, q_ref, kv_ref, q_out, kv_out, q_send, q_recv, kv_send, kv_recv
):
    me = lax.axis_index("seq")
    tp = lax.axis_index("tp")
    heads = q_ref.shape[0]
    span = back + per
    tries = back // per + 1
    mine = me % blocks

    def send(src, dst, sem, recv, target):
        @pl.when(target == me)
        def _():
            pltpu.make_async_copy(src, dst, sem).start()

        @pl.when(target != me)
        def _():
            pltpu.make_async_remote_copy(
                src_ref=src,
                dst_ref=dst,
                send_sem=sem,
                recv_sem=recv,
                device_id=(target, tp),
                device_id_type=pl.DeviceIdType.MESH,
            ).start()

    def finish_send(src, dst, sem, recv, target):
        @pl.when(target == me)
        def _():
            pltpu.make_async_copy(src, dst, sem).wait()

        @pl.when(target != me)
        def _():
            pltpu.make_async_remote_copy(
                src_ref=src,
                dst_ref=dst,
                send_sem=sem,
                recv_sem=recv,
                device_id=(target, tp),
                device_id_type=pl.DeviceIdType.MESH,
            ).wait_send()

    def finish_recv(src, dst, sem, recv, source):
        @pl.when(source != me)
        def _():
            pltpu.make_async_remote_copy(
                src_ref=src,
                dst_ref=dst,
                send_sem=sem,
                recv_sem=recv,
                device_id=(source, tp),
                device_id_type=pl.DeviceIdType.MESH,
            ).wait_recv()

    plan = []
    for h in range(heads):
        target = h * blocks + me // per
        plan.append((q_ref.at[h], q_out.at[me % per], q_send.at[h], q_recv.at[me % per], target))
        for r in range(tries):
            block = (me + back) // per - r
            slot = (me + back) % per + per * r
            plan.append(
                (
                    kv_ref.at[h],
                    kv_out.at[slot],
                    kv_send.at[h, r],
                    kv_recv.at[slot],
                    h * blocks + block,
                    (block >= 0) & (block < blocks),
                )
            )
    for item in plan:
        valid = item[5] if len(item) > 5 else True

        @pl.when(valid)
        def _():
            send(*item[:5])

    for item in plan:
        valid = item[5] if len(item) > 5 else True

        @pl.when(valid)
        def _():
            finish_send(*item[:5])

    for i in range(per):
        source = per * mine + i
        finish_recv(q_ref.at[0], q_out.at[i], q_send.at[0], q_recv.at[i], source)
    for slot in range(span):
        source = per * mine - back + slot

        @pl.when(source >= 0)
        def _():
            finish_recv(kv_ref.at[0], kv_out.at[slot], kv_send.at[0, 0], kv_recv.at[slot], source)


def spread(q, kv, blocks, per, back):
    heads = q.shape[0]
    span = back + per
    tries = back // per + 1
    return pl.pallas_call(
        functools.partial(spread_kernel, blocks, per, back),
        out_shape=(
            jax.ShapeDtypeStruct((per,) + q.shape[1:], q.dtype),
            jax.ShapeDtypeStruct((span,) + kv.shape[1:], kv.dtype),
        ),
        in_specs=[pl.BlockSpec(memory_space=pl.ANY)] * 2,
        out_specs=(pl.BlockSpec(memory_space=pl.ANY), pl.BlockSpec(memory_space=pl.ANY)),
        scratch_shapes=[
            pltpu.SemaphoreType.DMA((heads,)),
            pltpu.SemaphoreType.DMA((per,)),
            pltpu.SemaphoreType.DMA((heads, tries)),
            pltpu.SemaphoreType.DMA((span,)),
        ],
        compiler_params=pltpu.CompilerParams(has_side_effects=True),
    )(q, kv)


def gather_kernel(blocks, per, att_ref, out_ref, send_sem, recv_sem):
    me = lax.axis_index("seq")
    tp = lax.axis_index("tp")
    heads = out_ref.shape[0]
    head = me // blocks
    mine = me % blocks

    def copy(i, target):
        return pltpu.make_async_remote_copy(
            src_ref=att_ref.at[i],
            dst_ref=out_ref.at[head],
            send_sem=send_sem.at[i],
            recv_sem=recv_sem.at[head],
            device_id=(target, tp),
            device_id_type=pl.DeviceIdType.MESH,
        )

    for i in range(per):
        target = per * mine + i

        @pl.when(target == me)
        def _():
            pltpu.make_async_copy(att_ref.at[i], out_ref.at[head], send_sem.at[i]).start()

        @pl.when(target != me)
        def _():
            copy(i, target).start()

    for i in range(per):
        target = per * mine + i

        @pl.when(target == me)
        def _():
            pltpu.make_async_copy(att_ref.at[i], out_ref.at[head], send_sem.at[i]).wait()

        @pl.when(target != me)
        def _():
            copy(i, target).wait_send()

    for h in range(heads):
        source = h * blocks + me // per

        @pl.when(source != me)
        def _():
            pltpu.make_async_remote_copy(
                src_ref=att_ref.at[0],
                dst_ref=out_ref.at[h],
                send_sem=send_sem.at[0],
                recv_sem=recv_sem.at[h],
                device_id=(source, tp),
                device_id_type=pl.DeviceIdType.MESH,
            ).wait_recv()


def gather_back(att, heads, blocks):
    per = att.shape[0]
    return pl.pallas_call(
        functools.partial(gather_kernel, blocks, per),
        out_shape=jax.ShapeDtypeStruct((heads,) + att.shape[1:], att.dtype),
        in_specs=[pl.BlockSpec(memory_space=pl.ANY)],
        out_specs=pl.BlockSpec(memory_space=pl.ANY),
        scratch_shapes=[pltpu.SemaphoreType.DMA((per,)), pltpu.SemaphoreType.DMA((heads,))],
        compiler_params=pltpu.CompilerParams(has_side_effects=True),
    )(att)


def attend_kernel(
    blocks, per, back, scale, bounds_ref, q_ref, kv_ref, out_ref,
    q_in, kv_in, att, acc, top, total,
    q_send, q_recv, kv_send, kv_recv, att_send, att_recv,
):
    me = lax.axis_index("seq")
    tp = lax.axis_index("tp")
    heads, rows, head_dim = q_ref.shape
    span = back + per
    tries = back // per + 1
    mine = me % blocks
    head = me // blocks

    def remote(src, dst, send, recv, device):
        return pltpu.make_async_remote_copy(
            src_ref=src, dst_ref=dst, send_sem=send, recv_sem=recv,
            device_id=(device, tp), device_id_type=pl.DeviceIdType.MESH,
        )

    plan = []
    for h in range(heads):
        target = h * blocks + me // per
        plan.append(
            (q_ref.at[h], q_in.at[me % per], q_send.at[h], q_recv.at[me % per], target, True)
        )
        for r in range(tries):
            block = (me + back) // per - r
            slot = (me + back) % per + per * r
            valid = (block >= 0) & (block < blocks)
            plan.append(
                (kv_ref.at[h], kv_in.at[slot], kv_send.at[h, r], kv_recv.at[slot],
                 h * blocks + block, valid)
            )
    for src, dst, send, recv, target, valid in plan:

        @pl.when(valid & (target == me))
        def _():
            pltpu.make_async_copy(src, dst, send).start()

        @pl.when(valid & (target != me))
        def _():
            remote(src, dst, send, recv, target).start()

    for src, dst, send, recv, target, valid in plan:

        @pl.when(valid & (target == me))
        def _():
            pltpu.make_async_copy(src, dst, send).wait()

    for i in range(per):
        source = per * mine + i

        @pl.when(source != me)
        def _():
            remote(q_ref.at[0], q_in.at[i], q_send.at[0], q_recv.at[i], source).wait_recv()

    query = q_in[...].reshape(per * rows, head_dim)
    query_pos = mine * per * rows + lax.broadcasted_iota(jnp.int32, (per * rows, 1), 0)

    def tenant(pos):
        found = jnp.zeros(pos.shape, jnp.int32)
        for k in range(bounds_ref.shape[0]):
            found = found + (pos >= bounds_ref[k]).astype(jnp.int32)
        return found

    query_tenant = tenant(query_pos)

    def scores_of(slot):
        key_pos = (mine * per - back + slot) * rows + lax.broadcasted_iota(
            jnp.int32, (1, rows), 1
        )
        visible = (
            (tenant(key_pos) == query_tenant) & (key_pos <= query_pos) & (key_pos >= 0)
        )
        scores = lax.dot_general(
            query, kv_in[slot, :, :head_dim], (((1,), (1,)), ((), ())),
            preferred_element_type=jnp.float32,
        ) * scale
        return visible, scores

    top[...] = jnp.full(top.shape, -1e30, jnp.float32)
    total[...] = jnp.zeros(total.shape, jnp.float32)
    acc[...] = jnp.zeros(acc.shape, jnp.float32)

    def first_pass(slot, carry):
        source = per * mine - back + slot

        @pl.when(source >= 0)
        def _():
            @pl.when(source != me)
            def _():
                remote(
                    kv_ref.at[0], kv_in.at[slot], kv_send.at[0, 0], kv_recv.at[slot], source
                ).wait_recv()

            visible, scores = scores_of(slot)
            top[...] = jnp.maximum(
                top[...], jnp.max(jnp.where(visible, scores, -1e30), axis=1, keepdims=True)
            )

        return carry

    lax.fori_loop(0, span, first_pass, 0)

    def second_pass(slot, carry):
        source = per * mine - back + slot

        @pl.when(source >= 0)
        def _():
            visible, scores = scores_of(slot)
            weights = jnp.where(visible, jnp.exp(scores - top[...]), 0.0)
            total[...] += jnp.sum(weights, axis=1, keepdims=True)
            acc[...] += jnp.dot(
                weights.astype(jnp.bfloat16), kv_in[slot, :, head_dim:],
                preferred_element_type=jnp.float32,
            )

        return carry

    lax.fori_loop(0, span, second_pass, 0)
    att[...] = (acc[...] / total[...]).astype(att.dtype).reshape(att.shape)

    for i in range(per):
        target = per * mine + i

        @pl.when(target == me)
        def _():
            pltpu.make_async_copy(att.at[i], out_ref.at[head], att_send.at[i]).start()

        @pl.when(target != me)
        def _():
            remote(att.at[i], out_ref.at[head], att_send.at[i], att_recv.at[head], target).start()

    for i in range(per):
        target = per * mine + i

        @pl.when(target == me)
        def _():
            pltpu.make_async_copy(att.at[i], out_ref.at[head], att_send.at[i]).wait()

        @pl.when(target != me)
        def _():
            remote(
                att.at[i], out_ref.at[head], att_send.at[i], att_recv.at[head], target
            ).wait_send()

    for h in range(heads):
        source = h * blocks + me // per

        @pl.when(source != me)
        def _():
            remote(att.at[0], out_ref.at[h], att_send.at[0], att_recv.at[h], source).wait_recv()

    for src, dst, send, recv, target, valid in plan:

        @pl.when(valid & (target != me))
        def _():
            remote(src, dst, send, recv, target).wait_send()


def attend(bounds, q, kv, blocks, back, scale):
    heads, rows, head_dim = q.shape
    per = heads
    span = back + per
    tries = back // per + 1
    return pl.pallas_call(
        functools.partial(attend_kernel, blocks, per, back, scale),
        out_shape=jax.ShapeDtypeStruct(q.shape, q.dtype),
        in_specs=[
            pl.BlockSpec(memory_space=pltpu.SMEM),
            pl.BlockSpec(memory_space=pl.ANY),
            pl.BlockSpec(memory_space=pl.ANY),
        ],
        out_specs=pl.BlockSpec(memory_space=pl.ANY),
        scratch_shapes=[
            pltpu.VMEM((per, rows, head_dim), q.dtype),
            pltpu.VMEM((span,) + kv.shape[1:], kv.dtype),
            pltpu.VMEM((per, rows, head_dim), q.dtype),
            pltpu.VMEM((per * rows, head_dim), jnp.float32),
            pltpu.VMEM((per * rows, 1), jnp.float32),
            pltpu.VMEM((per * rows, 1), jnp.float32),
            pltpu.SemaphoreType.DMA((heads,)),
            pltpu.SemaphoreType.DMA((per,)),
            pltpu.SemaphoreType.DMA((heads, tries)),
            pltpu.SemaphoreType.DMA((span,)),
            pltpu.SemaphoreType.DMA((per,)),
            pltpu.SemaphoreType.DMA((heads,)),
        ],
        compiler_params=pltpu.CompilerParams(has_side_effects=True),
    )(bounds, q, kv)


def shards(
    queries, keys, values, lengths, resid, w_out, moe_gain, routes, gates, w_gate_up, w_down
):
    seq_count = lax.axis_size("seq")
    me = lax.axis_index("seq")
    query_rows = queries.shape[0]
    local_heads = queries.shape[1] // HEAD_DIM
    cols = queries.shape[1]
    width = resid.shape[1]
    score_scale = 1.0 / math.sqrt(HEAD_DIM)
    longest = (seq_count * query_rows) // 2
    reach = min(seq_count - 1, -(-(longest - 1) // query_rows))
    blocks = seq_count // local_heads
    per = seq_count // blocks
    back = -(-reach // per) * per
    span = back + per
    head_q = queries.reshape(query_rows, local_heads, HEAD_DIM).transpose(1, 0, 2)
    head_kv = jnp.concatenate(
        [
            keys.reshape(query_rows, local_heads, HEAD_DIM),
            values.reshape(query_rows, local_heads, HEAD_DIM),
        ],
        axis=2,
    ).transpose(1, 0, 2)
    attention = (
        attend(
            jnp.cumsum(lengths).astype(jnp.int32), head_q, head_kv, blocks, back, score_scale
        )
        .transpose(1, 0, 2)
        .reshape(query_rows, local_heads * HEAD_DIM)
    )
    tp_index = lax.axis_index("tp")
    near_swap = [(t, t ^ 1) for t in range(lax.axis_size("tp"))]
    far_swap = [(t, t ^ 2) for t in range(lax.axis_size("tp"))]
    local_rows = resid.shape[0]
    partial_proj = jnp.dot(attention, w_out, preferred_element_type=jnp.float32).reshape(
        2, 2, local_rows, width
    )
    core = tp_index % 2
    keep = lax.dynamic_index_in_dim(partial_proj, core, axis=1, keepdims=False)
    give = lax.dynamic_index_in_dim(partial_proj, 1 - core, axis=1, keepdims=False)
    half = keep + lax.ppermute(give.astype(jnp.bfloat16), "tp", near_swap).astype(jnp.float32)
    far = tp_index // 2
    pair_resid = jnp.stack([resid, lax.ppermute(resid, "tp", far_swap)])
    pair_routes = jnp.stack([routes, lax.ppermute(routes, "tp", far_swap)])
    pair_gates = jnp.stack([gates, lax.ppermute(gates, "tp", far_swap)])
    half = half.astype(jnp.bfloat16)
    total = half.astype(jnp.float32) + lax.ppermute(half, "tp", far_swap).astype(jnp.float32)
    pair_proj = jnp.stack(
        [
            lax.dynamic_index_in_dim(total, far, axis=0, keepdims=False),
            lax.dynamic_index_in_dim(total, 1 - far, axis=0, keepdims=False),
        ]
    )
    pair_attended = (pair_resid.astype(jnp.float32) + pair_proj).astype(jnp.bfloat16)
    attended = pair_attended[0]
    widened = pair_attended.astype(jnp.float32)
    meansq = jnp.mean(widened * widened, axis=2, keepdims=True)
    pair_normed = (widened * lax.rsqrt(meansq + 1e-05) * moe_gain).astype(jnp.bfloat16)
    top_count = routes.shape[1]
    owned = w_gate_up.shape[0]
    experts_all = owned * seq_count
    capacity = 3 * local_rows * top_count // (2 * experts_all)
    matches = pair_routes[..., None] == jnp.arange(experts_all, dtype=jnp.int32)
    member = jnp.any(matches, axis=2)
    slot = jnp.cumsum(member.astype(jnp.int32), axis=1) - 1
    place = member[..., None] & (slot[..., None] == jnp.arange(capacity, dtype=jnp.int32))
    buffer = jnp.einsum(
        "xiec,xid->excd", place.astype(jnp.bfloat16), pair_normed,
        preferred_element_type=jnp.float32,
    ).astype(jnp.bfloat16)
    buffer = buffer.reshape(seq_count, owned, 2, capacity, width).transpose(1, 0, 2, 3, 4)
    arrived = lax.all_to_all(buffer, "seq", split_axis=1, concat_axis=1, tiled=True)
    near = lax.ppermute(arrived, "tp", near_swap)

    def expert_part(slots):
        projections = jnp.einsum(
            "xnd,xdgf->xngf", slots.reshape(owned, -1, width), w_gate_up,
            preferred_element_type=jnp.float32,
        )
        hidden = (jax.nn.silu(projections[..., 0, :]) * projections[..., 1, :]).astype(
            jnp.bfloat16
        )
        return jnp.einsum(
            "xnf,xfd->xnd", hidden, w_down, preferred_element_type=jnp.float32
        ).astype(jnp.bfloat16)

    from_near = lax.ppermute(expert_part(near), "tp", near_swap)
    reduced = (
        expert_part(arrived).astype(jnp.float32) + from_near.astype(jnp.float32)
    ).astype(jnp.bfloat16)
    returned = lax.all_to_all(
        reduced.reshape(arrived.shape), "seq", split_axis=1, concat_axis=1, tiled=True
    )
    weight_of = jnp.sum(jnp.where(matches, pair_gates[..., None], 0.0), axis=2)
    mix_weights = jnp.where(place, weight_of[..., None], 0.0)
    mixes = jnp.einsum(
        "xiec,xecd->xid",
        mix_weights,
        returned.transpose(2, 1, 0, 3, 4)
        .reshape(2, experts_all, capacity, width)
        .astype(jnp.float32),
        precision=lax.Precision.HIGHEST,
        preferred_element_type=jnp.float32,
    )
    expert_mix = (mixes[0] + lax.ppermute(mixes[1], "tp", far_swap)).astype(jnp.bfloat16)
    return (attended, expert_mix)


def solution(mesh):
    return jax.shard_map(
        shards,
        mesh=mesh,
        in_specs=(
            P("seq", "tp"),
            P("seq", "tp"),
            P("seq", "tp"),
            P(),
            P(("seq", "tp"), None),
            P("tp", None),
            P(),
            P(("seq", "tp"), None),
            P(("seq", "tp"), None),
            P("seq", None, None, "tp"),
            P("seq", "tp", None),
        ),
        out_specs=(P(("seq", "tp"), None), P(("seq", "tp"), None)),
        check_vma=False,
    )
```

```python
import functools
import math

import jax
import jax.numpy as jnp
from jax import lax
from jax.experimental import pallas as pl
from jax.experimental.pallas import tpu as pltpu
from jax.sharding import PartitionSpec as P

HEAD_DIM = 128


def tenant_of(positions, lengths):
    bounds = jnp.cumsum(lengths)
    return jnp.sum((positions[:, None] >= bounds[None, :]).astype(jnp.int32), axis=1)


def spread_kernel(
    blocks, per, back, q_ref, kv_ref, q_out, kv_out, q_send, q_recv, kv_send, kv_recv
):
    me = lax.axis_index("seq")
    tp = lax.axis_index("tp")
    heads = q_ref.shape[0]
    span = back + per
    tries = back // per + 1
    mine = me % blocks

    def send(src, dst, sem, recv, target):
        @pl.when(target == me)
        def _():
            pltpu.make_async_copy(src, dst, sem).start()

        @pl.when(target != me)
        def _():
            pltpu.make_async_remote_copy(
                src_ref=src,
                dst_ref=dst,
                send_sem=sem,
                recv_sem=recv,
                device_id=(target, tp),
                device_id_type=pl.DeviceIdType.MESH,
            ).start()

    def finish_send(src, dst, sem, recv, target):
        @pl.when(target == me)
        def _():
            pltpu.make_async_copy(src, dst, sem).wait()

        @pl.when(target != me)
        def _():
            pltpu.make_async_remote_copy(
                src_ref=src,
                dst_ref=dst,
                send_sem=sem,
                recv_sem=recv,
                device_id=(target, tp),
                device_id_type=pl.DeviceIdType.MESH,
            ).wait_send()

    def finish_recv(src, dst, sem, recv, source):
        @pl.when(source != me)
        def _():
            pltpu.make_async_remote_copy(
                src_ref=src,
                dst_ref=dst,
                send_sem=sem,
                recv_sem=recv,
                device_id=(source, tp),
                device_id_type=pl.DeviceIdType.MESH,
            ).wait_recv()

    plan = []
    for h in range(heads):
        target = h * blocks + me // per
        plan.append((q_ref.at[h], q_out.at[me % per], q_send.at[h], q_recv.at[me % per], target))
        for r in range(tries):
            block = (me + back) // per - r
            slot = (me + back) % per + per * r
            plan.append(
                (
                    kv_ref.at[h],
                    kv_out.at[slot],
                    kv_send.at[h, r],
                    kv_recv.at[slot],
                    h * blocks + block,
                    (block >= 0) & (block < blocks),
                )
            )
    for item in plan:
        valid = item[5] if len(item) > 5 else True

        @pl.when(valid)
        def _():
            send(*item[:5])

    for item in plan:
        valid = item[5] if len(item) > 5 else True

        @pl.when(valid)
        def _():
            finish_send(*item[:5])

    for i in range(per):
        source = per * mine + i
        finish_recv(q_ref.at[0], q_out.at[i], q_send.at[0], q_recv.at[i], source)
    for slot in range(span):
        source = per * mine - back + slot

        @pl.when(source >= 0)
        def _():
            finish_recv(kv_ref.at[0], kv_out.at[slot], kv_send.at[0, 0], kv_recv.at[slot], source)


def spread(q, kv, blocks, per, back):
    heads = q.shape[0]
    span = back + per
    tries = back // per + 1
    return pl.pallas_call(
        functools.partial(spread_kernel, blocks, per, back),
        out_shape=(
            jax.ShapeDtypeStruct((per,) + q.shape[1:], q.dtype),
            jax.ShapeDtypeStruct((span,) + kv.shape[1:], kv.dtype),
        ),
        in_specs=[pl.BlockSpec(memory_space=pl.ANY)] * 2,
        out_specs=(pl.BlockSpec(memory_space=pl.ANY), pl.BlockSpec(memory_space=pl.ANY)),
        scratch_shapes=[
            pltpu.SemaphoreType.DMA((heads,)),
            pltpu.SemaphoreType.DMA((per,)),
            pltpu.SemaphoreType.DMA((heads, tries)),
            pltpu.SemaphoreType.DMA((span,)),
        ],
        compiler_params=pltpu.CompilerParams(has_side_effects=True),
    )(q, kv)


def gather_kernel(blocks, per, att_ref, out_ref, send_sem, recv_sem):
    me = lax.axis_index("seq")
    tp = lax.axis_index("tp")
    heads = out_ref.shape[0]
    head = me // blocks
    mine = me % blocks

    def copy(i, target):
        return pltpu.make_async_remote_copy(
            src_ref=att_ref.at[i],
            dst_ref=out_ref.at[head],
            send_sem=send_sem.at[i],
            recv_sem=recv_sem.at[head],
            device_id=(target, tp),
            device_id_type=pl.DeviceIdType.MESH,
        )

    for i in range(per):
        target = per * mine + i

        @pl.when(target == me)
        def _():
            pltpu.make_async_copy(att_ref.at[i], out_ref.at[head], send_sem.at[i]).start()

        @pl.when(target != me)
        def _():
            copy(i, target).start()

    for i in range(per):
        target = per * mine + i

        @pl.when(target == me)
        def _():
            pltpu.make_async_copy(att_ref.at[i], out_ref.at[head], send_sem.at[i]).wait()

        @pl.when(target != me)
        def _():
            copy(i, target).wait_send()

    for h in range(heads):
        source = h * blocks + me // per

        @pl.when(source != me)
        def _():
            pltpu.make_async_remote_copy(
                src_ref=att_ref.at[0],
                dst_ref=out_ref.at[h],
                send_sem=send_sem.at[0],
                recv_sem=recv_sem.at[h],
                device_id=(source, tp),
                device_id_type=pl.DeviceIdType.MESH,
            ).wait_recv()


def gather_back(att, heads, blocks):
    per = att.shape[0]
    return pl.pallas_call(
        functools.partial(gather_kernel, blocks, per),
        out_shape=jax.ShapeDtypeStruct((heads,) + att.shape[1:], att.dtype),
        in_specs=[pl.BlockSpec(memory_space=pl.ANY)],
        out_specs=pl.BlockSpec(memory_space=pl.ANY),
        scratch_shapes=[pltpu.SemaphoreType.DMA((per,)), pltpu.SemaphoreType.DMA((heads,))],
        compiler_params=pltpu.CompilerParams(has_side_effects=True),
    )(att)


def attend_kernel(
    blocks, per, back, scale, bounds_ref, q_ref, kv_ref, out_ref,
    q_in, kv_in, att, acc, top, total, kept,
    q_send, q_recv, kv_send, kv_recv, att_send, att_recv,
):
    me = lax.axis_index("seq")
    tp = lax.axis_index("tp")
    heads, rows, head_dim = q_ref.shape
    span = back + per
    tries = back // per + 1
    mine = me % blocks
    head = me // blocks

    def remote(src, dst, send, recv, device):
        return pltpu.make_async_remote_copy(
            src_ref=src, dst_ref=dst, send_sem=send, recv_sem=recv,
            device_id=(device, tp), device_id_type=pl.DeviceIdType.MESH,
        )

    plan = []
    for h in range(heads):
        target = h * blocks + me // per
        plan.append(
            (q_ref.at[h], q_in.at[me % per], q_send.at[h], q_recv.at[me % per], target, True)
        )
        for r in range(tries):
            block = (me + back) // per - r
            slot = (me + back) % per + per * r
            valid = (block >= 0) & (block < blocks)
            plan.append(
                (kv_ref.at[h], kv_in.at[slot], kv_send.at[h, r], kv_recv.at[slot],
                 h * blocks + block, valid)
            )
    for src, dst, send, recv, target, valid in plan:

        @pl.when(valid & (target == me))
        def _():
            pltpu.make_async_copy(src, dst, send).start()

        @pl.when(valid & (target != me))
        def _():
            remote(src, dst, send, recv, target).start()

    for src, dst, send, recv, target, valid in plan:

        @pl.when(valid & (target == me))
        def _():
            pltpu.make_async_copy(src, dst, send).wait()

    for i in range(per):
        source = per * mine + i

        @pl.when(source != me)
        def _():
            remote(q_ref.at[0], q_in.at[i], q_send.at[0], q_recv.at[i], source).wait_recv()

    query = q_in[...].reshape(per * rows, head_dim)
    query_pos = mine * per * rows + lax.broadcasted_iota(jnp.int32, (per * rows, 1), 0)
    first = jnp.zeros(query_pos.shape, jnp.int32)
    for k in range(bounds_ref.shape[0]):
        first = jnp.maximum(first, jnp.where(query_pos >= bounds_ref[k], bounds_ref[k], 0))

    top[...] = jnp.full(top.shape, -1e30, jnp.float32)
    total[...] = jnp.zeros(total.shape, jnp.float32)
    acc[...] = jnp.zeros(acc.shape, jnp.float32)

    def first_pass(slot, carry):
        source = per * mine - back + slot

        @pl.when(source >= 0)
        def _():
            @pl.when(source != me)
            def _():
                remote(
                    kv_ref.at[0], kv_in.at[slot], kv_send.at[0, 0], kv_recv.at[slot], source
                ).wait_recv()

            key_pos = source * rows + lax.broadcasted_iota(jnp.int32, (1, rows), 1)
            visible = (key_pos >= first) & (key_pos <= query_pos)
            scores = lax.dot_general(
                query, kv_in[slot, :, :head_dim], (((1,), (1,)), ((), ())),
                preferred_element_type=jnp.float32,
            ) * scale
            scores = jnp.where(visible, scores, -1e30)
            kept[slot] = scores
            top[...] = jnp.maximum(top[...], jnp.max(scores, axis=1, keepdims=True))

        return carry

    lax.fori_loop(0, span, first_pass, 0)

    def second_pass(slot, carry):
        source = per * mine - back + slot

        @pl.when(source >= 0)
        def _():
            weights = jnp.exp(kept[slot] - top[...])
            total[...] += jnp.sum(weights, axis=1, keepdims=True)
            acc[...] += jnp.dot(
                weights.astype(jnp.bfloat16), kv_in[slot, :, head_dim:],
                preferred_element_type=jnp.float32,
            )

        return carry

    lax.fori_loop(0, span, second_pass, 0)
    att[...] = (acc[...] / total[...]).astype(att.dtype).reshape(att.shape)

    for i in range(per):
        target = per * mine + i

        @pl.when(target == me)
        def _():
            pltpu.make_async_copy(att.at[i], out_ref.at[head], att_send.at[i]).start()

        @pl.when(target != me)
        def _():
            remote(att.at[i], out_ref.at[head], att_send.at[i], att_recv.at[head], target).start()

    for i in range(per):
        target = per * mine + i

        @pl.when(target == me)
        def _():
            pltpu.make_async_copy(att.at[i], out_ref.at[head], att_send.at[i]).wait()

        @pl.when(target != me)
        def _():
            remote(
                att.at[i], out_ref.at[head], att_send.at[i], att_recv.at[head], target
            ).wait_send()

    for h in range(heads):
        source = h * blocks + me // per

        @pl.when(source != me)
        def _():
            remote(att.at[0], out_ref.at[h], att_send.at[0], att_recv.at[h], source).wait_recv()

    for src, dst, send, recv, target, valid in plan:

        @pl.when(valid & (target != me))
        def _():
            remote(src, dst, send, recv, target).wait_send()


def attend(bounds, q, kv, blocks, back, scale):
    heads, rows, head_dim = q.shape
    per = heads
    span = back + per
    tries = back // per + 1
    return pl.pallas_call(
        functools.partial(attend_kernel, blocks, per, back, scale),
        out_shape=jax.ShapeDtypeStruct(q.shape, q.dtype),
        in_specs=[
            pl.BlockSpec(memory_space=pltpu.SMEM),
            pl.BlockSpec(memory_space=pl.ANY),
            pl.BlockSpec(memory_space=pl.ANY),
        ],
        out_specs=pl.BlockSpec(memory_space=pl.ANY),
        scratch_shapes=[
            pltpu.VMEM((per, rows, head_dim), q.dtype),
            pltpu.VMEM((span,) + kv.shape[1:], kv.dtype),
            pltpu.VMEM((per, rows, head_dim), q.dtype),
            pltpu.VMEM((per * rows, head_dim), jnp.float32),
            pltpu.VMEM((per * rows, 1), jnp.float32),
            pltpu.VMEM((per * rows, 1), jnp.float32),
            pltpu.VMEM((span, per * rows, rows), jnp.float32),
            pltpu.SemaphoreType.DMA((heads,)),
            pltpu.SemaphoreType.DMA((per,)),
            pltpu.SemaphoreType.DMA((heads, tries)),
            pltpu.SemaphoreType.DMA((span,)),
            pltpu.SemaphoreType.DMA((per,)),
            pltpu.SemaphoreType.DMA((heads,)),
        ],
        compiler_params=pltpu.CompilerParams(has_side_effects=True),
    )(bounds, q, kv)


def shards(
    queries, keys, values, lengths, resid, w_out, moe_gain, routes, gates, w_gate_up, w_down
):
    seq_count = lax.axis_size("seq")
    me = lax.axis_index("seq")
    query_rows = queries.shape[0]
    local_heads = queries.shape[1] // HEAD_DIM
    cols = queries.shape[1]
    width = resid.shape[1]
    score_scale = 1.0 / math.sqrt(HEAD_DIM)
    longest = (seq_count * query_rows) // 2
    reach = min(seq_count - 1, -(-(longest - 1) // query_rows))
    blocks = seq_count // local_heads
    per = seq_count // blocks
    back = -(-reach // per) * per
    span = back + per
    head_q = queries.reshape(query_rows, local_heads, HEAD_DIM).transpose(1, 0, 2)
    head_kv = jnp.concatenate(
        [
            keys.reshape(query_rows, local_heads, HEAD_DIM),
            values.reshape(query_rows, local_heads, HEAD_DIM),
        ],
        axis=2,
    ).transpose(1, 0, 2)
    attention = (
        attend(
            jnp.cumsum(lengths).astype(jnp.int32), head_q, head_kv, blocks, back, score_scale
        )
        .transpose(1, 0, 2)
        .reshape(query_rows, local_heads * HEAD_DIM)
    )
    tp_index = lax.axis_index("tp")
    near_swap = [(t, t ^ 1) for t in range(lax.axis_size("tp"))]
    far_swap = [(t, t ^ 2) for t in range(lax.axis_size("tp"))]
    local_rows = resid.shape[0]
    partial_proj = jnp.dot(attention, w_out, preferred_element_type=jnp.float32).reshape(
        2, 2, local_rows, width
    )
    core = tp_index % 2
    keep = lax.dynamic_index_in_dim(partial_proj, core, axis=1, keepdims=False)
    give = lax.dynamic_index_in_dim(partial_proj, 1 - core, axis=1, keepdims=False)
    half = keep + lax.ppermute(give.astype(jnp.bfloat16), "tp", near_swap).astype(jnp.float32)
    far = tp_index // 2
    pair_resid = jnp.stack([resid, lax.ppermute(resid, "tp", far_swap)])
    pair_routes = jnp.stack([routes, lax.ppermute(routes, "tp", far_swap)])
    pair_gates = jnp.stack([gates, lax.ppermute(gates, "tp", far_swap)])
    half = half.astype(jnp.bfloat16)
    total = half.astype(jnp.float32) + lax.ppermute(half, "tp", far_swap).astype(jnp.float32)
    pair_proj = jnp.stack(
        [
            lax.dynamic_index_in_dim(total, far, axis=0, keepdims=False),
            lax.dynamic_index_in_dim(total, 1 - far, axis=0, keepdims=False),
        ]
    )
    pair_attended = (pair_resid.astype(jnp.float32) + pair_proj).astype(jnp.bfloat16)
    attended = pair_attended[0]
    widened = pair_attended.astype(jnp.float32)
    meansq = jnp.mean(widened * widened, axis=2, keepdims=True)
    pair_normed = (widened * lax.rsqrt(meansq + 1e-05) * moe_gain).astype(jnp.bfloat16)
    top_count = routes.shape[1]
    owned = w_gate_up.shape[0]
    experts_all = owned * seq_count
    capacity = 3 * local_rows * top_count // (2 * experts_all)
    matches = pair_routes[..., None] == jnp.arange(experts_all, dtype=jnp.int32)
    member = jnp.any(matches, axis=2)
    slot = jnp.cumsum(member.astype(jnp.int32), axis=1) - 1
    place = member[..., None] & (slot[..., None] == jnp.arange(capacity, dtype=jnp.int32))
    buffer = jnp.einsum(
        "xiec,xid->excd", place.astype(jnp.bfloat16), pair_normed,
        preferred_element_type=jnp.float32,
    ).astype(jnp.bfloat16)
    buffer = buffer.reshape(seq_count, owned, 2, capacity, width).transpose(1, 0, 2, 3, 4)
    arrived = lax.all_to_all(buffer, "seq", split_axis=1, concat_axis=1, tiled=True)
    near = lax.ppermute(arrived, "tp", near_swap)

    def expert_part(slots):
        projections = jnp.einsum(
            "xnd,xdgf->xngf", slots.reshape(owned, -1, width), w_gate_up,
            preferred_element_type=jnp.float32,
        )
        hidden = (jax.nn.silu(projections[..., 0, :]) * projections[..., 1, :]).astype(
            jnp.bfloat16
        )
        return jnp.einsum(
            "xnf,xfd->xnd", hidden, w_down, preferred_element_type=jnp.float32
        ).astype(jnp.bfloat16)

    from_near = lax.ppermute(expert_part(near), "tp", near_swap)
    reduced = (
        expert_part(arrived).astype(jnp.float32) + from_near.astype(jnp.float32)
    ).astype(jnp.bfloat16)
    returned = lax.all_to_all(
        reduced.reshape(arrived.shape), "seq", split_axis=1, concat_axis=1, tiled=True
    )
    weight_of = jnp.sum(jnp.where(matches, pair_gates[..., None], 0.0), axis=2)
    mix_weights = jnp.where(place, weight_of[..., None], 0.0)
    mixes = jnp.einsum(
        "xiec,xecd->xid",
        mix_weights,
        returned.transpose(2, 1, 0, 3, 4)
        .reshape(2, experts_all, capacity, width)
        .astype(jnp.float32),
        precision=lax.Precision.HIGHEST,
        preferred_element_type=jnp.float32,
    )
    expert_mix = (mixes[0] + lax.ppermute(mixes[1], "tp", far_swap)).astype(jnp.bfloat16)
    return (attended, expert_mix)


def solution(mesh):
    return jax.shard_map(
        shards,
        mesh=mesh,
        in_specs=(
            P("seq", "tp"),
            P("seq", "tp"),
            P("seq", "tp"),
            P(),
            P(("seq", "tp"), None),
            P("tp", None),
            P(),
            P(("seq", "tp"), None),
            P(("seq", "tp"), None),
            P("seq", None, None, "tp"),
            P("seq", "tp", None),
        ),
        out_specs=(P(("seq", "tp"), None), P(("seq", "tp"), None)),
        check_vma=False,
    )
```

```python
import functools
import math

import jax
import jax.numpy as jnp
from jax import lax
from jax.experimental import pallas as pl
from jax.experimental.pallas import tpu as pltpu
from jax.sharding import PartitionSpec as P

HEAD_DIM = 128


def tenant_of(positions, lengths):
    bounds = jnp.cumsum(lengths)
    return jnp.sum((positions[:, None] >= bounds[None, :]).astype(jnp.int32), axis=1)


def spread_kernel(
    blocks, per, back, q_ref, kv_ref, q_out, kv_out, q_send, q_recv, kv_send, kv_recv
):
    me = lax.axis_index("seq")
    tp = lax.axis_index("tp")
    heads = q_ref.shape[0]
    span = back + per
    tries = back // per + 1
    mine = me % blocks

    def send(src, dst, sem, recv, target):
        @pl.when(target == me)
        def _():
            pltpu.make_async_copy(src, dst, sem).start()

        @pl.when(target != me)
        def _():
            pltpu.make_async_remote_copy(
                src_ref=src,
                dst_ref=dst,
                send_sem=sem,
                recv_sem=recv,
                device_id=(target, tp),
                device_id_type=pl.DeviceIdType.MESH,
            ).start()

    def finish_send(src, dst, sem, recv, target):
        @pl.when(target == me)
        def _():
            pltpu.make_async_copy(src, dst, sem).wait()

        @pl.when(target != me)
        def _():
            pltpu.make_async_remote_copy(
                src_ref=src,
                dst_ref=dst,
                send_sem=sem,
                recv_sem=recv,
                device_id=(target, tp),
                device_id_type=pl.DeviceIdType.MESH,
            ).wait_send()

    def finish_recv(src, dst, sem, recv, source):
        @pl.when(source != me)
        def _():
            pltpu.make_async_remote_copy(
                src_ref=src,
                dst_ref=dst,
                send_sem=sem,
                recv_sem=recv,
                device_id=(source, tp),
                device_id_type=pl.DeviceIdType.MESH,
            ).wait_recv()

    plan = []
    for h in range(heads):
        target = h * blocks + me // per
        plan.append((q_ref.at[h], q_out.at[me % per], q_send.at[h], q_recv.at[me % per], target))
        for r in range(tries):
            block = (me + back) // per - r
            slot = (me + back) % per + per * r
            plan.append(
                (
                    kv_ref.at[h],
                    kv_out.at[slot],
                    kv_send.at[h, r],
                    kv_recv.at[slot],
                    h * blocks + block,
                    (block >= 0) & (block < blocks),
                )
            )
    for item in plan:
        valid = item[5] if len(item) > 5 else True

        @pl.when(valid)
        def _():
            send(*item[:5])

    for item in plan:
        valid = item[5] if len(item) > 5 else True

        @pl.when(valid)
        def _():
            finish_send(*item[:5])

    for i in range(per):
        source = per * mine + i
        finish_recv(q_ref.at[0], q_out.at[i], q_send.at[0], q_recv.at[i], source)
    for slot in range(span):
        source = per * mine - back + slot

        @pl.when(source >= 0)
        def _():
            finish_recv(kv_ref.at[0], kv_out.at[slot], kv_send.at[0, 0], kv_recv.at[slot], source)


def spread(q, kv, blocks, per, back):
    heads = q.shape[0]
    span = back + per
    tries = back // per + 1
    return pl.pallas_call(
        functools.partial(spread_kernel, blocks, per, back),
        out_shape=(
            jax.ShapeDtypeStruct((per,) + q.shape[1:], q.dtype),
            jax.ShapeDtypeStruct((span,) + kv.shape[1:], kv.dtype),
        ),
        in_specs=[pl.BlockSpec(memory_space=pl.ANY)] * 2,
        out_specs=(pl.BlockSpec(memory_space=pl.ANY), pl.BlockSpec(memory_space=pl.ANY)),
        scratch_shapes=[
            pltpu.SemaphoreType.DMA((heads,)),
            pltpu.SemaphoreType.DMA((per,)),
            pltpu.SemaphoreType.DMA((heads, tries)),
            pltpu.SemaphoreType.DMA((span,)),
        ],
        compiler_params=pltpu.CompilerParams(has_side_effects=True),
    )(q, kv)


def gather_kernel(blocks, per, att_ref, out_ref, send_sem, recv_sem):
    me = lax.axis_index("seq")
    tp = lax.axis_index("tp")
    heads = out_ref.shape[0]
    head = me // blocks
    mine = me % blocks

    def copy(i, target):
        return pltpu.make_async_remote_copy(
            src_ref=att_ref.at[i],
            dst_ref=out_ref.at[head],
            send_sem=send_sem.at[i],
            recv_sem=recv_sem.at[head],
            device_id=(target, tp),
            device_id_type=pl.DeviceIdType.MESH,
        )

    for i in range(per):
        target = per * mine + i

        @pl.when(target == me)
        def _():
            pltpu.make_async_copy(att_ref.at[i], out_ref.at[head], send_sem.at[i]).start()

        @pl.when(target != me)
        def _():
            copy(i, target).start()

    for i in range(per):
        target = per * mine + i

        @pl.when(target == me)
        def _():
            pltpu.make_async_copy(att_ref.at[i], out_ref.at[head], send_sem.at[i]).wait()

        @pl.when(target != me)
        def _():
            copy(i, target).wait_send()

    for h in range(heads):
        source = h * blocks + me // per

        @pl.when(source != me)
        def _():
            pltpu.make_async_remote_copy(
                src_ref=att_ref.at[0],
                dst_ref=out_ref.at[h],
                send_sem=send_sem.at[0],
                recv_sem=recv_sem.at[h],
                device_id=(source, tp),
                device_id_type=pl.DeviceIdType.MESH,
            ).wait_recv()


def gather_back(att, heads, blocks):
    per = att.shape[0]
    return pl.pallas_call(
        functools.partial(gather_kernel, blocks, per),
        out_shape=jax.ShapeDtypeStruct((heads,) + att.shape[1:], att.dtype),
        in_specs=[pl.BlockSpec(memory_space=pl.ANY)],
        out_specs=pl.BlockSpec(memory_space=pl.ANY),
        scratch_shapes=[pltpu.SemaphoreType.DMA((per,)), pltpu.SemaphoreType.DMA((heads,))],
        compiler_params=pltpu.CompilerParams(has_side_effects=True),
    )(att)


def attend_kernel(
    blocks, per, back, scale, bounds_ref, q_ref, kv_ref, out_ref,
    q_in, kv_in, att, acc, top, total, kept,
    q_send, q_recv, kv_send, kv_recv, att_send, att_recv,
):
    me = lax.axis_index("seq")
    tp = lax.axis_index("tp")
    heads, rows, head_dim = q_ref.shape
    span = back + per
    tries = back // per + 1
    mine = me % blocks
    head = me // blocks

    def remote(src, dst, send, recv, device):
        return pltpu.make_async_remote_copy(
            src_ref=src, dst_ref=dst, send_sem=send, recv_sem=recv,
            device_id=(device, tp), device_id_type=pl.DeviceIdType.MESH,
        )

    plan = []
    for h in range(heads):
        target = h * blocks + me // per
        plan.append(
            (q_ref.at[h], q_in.at[me % per], q_send.at[h], q_recv.at[me % per], target, True)
        )
        for r in range(tries):
            block = (me + back) // per - r
            slot = (me + back) % per + per * r
            valid = (block >= 0) & (block < blocks)
            plan.append(
                (kv_ref.at[h], kv_in.at[slot], kv_send.at[h, r], kv_recv.at[slot],
                 h * blocks + block, valid)
            )
    for src, dst, send, recv, target, valid in plan:

        @pl.when(valid & (target == me))
        def _():
            pltpu.make_async_copy(src, dst, send).start()

        @pl.when(valid & (target != me))
        def _():
            remote(src, dst, send, recv, target).start()

    for src, dst, send, recv, target, valid in plan:

        @pl.when(valid & (target == me))
        def _():
            pltpu.make_async_copy(src, dst, send).wait()

    for i in range(per):
        source = per * mine + i

        @pl.when(source != me)
        def _():
            remote(q_ref.at[0], q_in.at[i], q_send.at[0], q_recv.at[i], source).wait_recv()

    query = q_in[...].reshape(per * rows, head_dim)
    query_pos = mine * per * rows + lax.broadcasted_iota(jnp.int32, (per * rows, 1), 0)
    first = jnp.zeros(query_pos.shape, jnp.int32)
    for k in range(bounds_ref.shape[0]):
        first = jnp.maximum(first, jnp.where(query_pos >= bounds_ref[k], bounds_ref[k], 0))

    top[...] = jnp.full(top.shape, -1e30, jnp.float32)
    total[...] = jnp.zeros(total.shape, jnp.float32)
    acc[...] = jnp.zeros(acc.shape, jnp.float32)

    def first_pass(slot, carry):
        source = per * mine - back + slot

        @pl.when(source >= 0)
        def _():
            @pl.when(source != me)
            def _():
                remote(
                    kv_ref.at[0], kv_in.at[slot], kv_send.at[0, 0], kv_recv.at[slot], source
                ).wait_recv()

            key_pos = source * rows + lax.broadcasted_iota(jnp.int32, (1, rows), 1)
            visible = (key_pos >= first) & (key_pos <= query_pos)
            scores = lax.dot_general(
                query, kv_in[slot, :, :head_dim], (((1,), (1,)), ((), ())),
                preferred_element_type=jnp.float32,
            ) * scale
            scores = jnp.where(visible, scores, -1e30)
            kept[slot] = scores
            top[...] = jnp.maximum(top[...], jnp.max(scores, axis=1, keepdims=True))

        return carry

    lax.fori_loop(0, span, first_pass, 0)

    def second_pass(slot, carry):
        source = per * mine - back + slot

        @pl.when(source >= 0)
        def _():
            weights = jnp.exp(kept[slot] - top[...])
            total[...] += jnp.sum(weights, axis=1, keepdims=True)
            acc[...] += jnp.dot(
                weights.astype(jnp.bfloat16), kv_in[slot, :, head_dim:],
                preferred_element_type=jnp.float32,
            )

        return carry

    lax.fori_loop(0, span, second_pass, 0)
    att[...] = (acc[...] / total[...]).astype(att.dtype).reshape(att.shape)

    for i in range(per):
        target = per * mine + i

        @pl.when(target == me)
        def _():
            pltpu.make_async_copy(att.at[i], out_ref.at[head], att_send.at[i]).start()

        @pl.when(target != me)
        def _():
            remote(att.at[i], out_ref.at[head], att_send.at[i], att_recv.at[head], target).start()

    for i in range(per):
        target = per * mine + i

        @pl.when(target == me)
        def _():
            pltpu.make_async_copy(att.at[i], out_ref.at[head], att_send.at[i]).wait()

        @pl.when(target != me)
        def _():
            remote(
                att.at[i], out_ref.at[head], att_send.at[i], att_recv.at[head], target
            ).wait_send()

    for h in range(heads):
        source = h * blocks + me // per

        @pl.when(source != me)
        def _():
            remote(att.at[0], out_ref.at[h], att_send.at[0], att_recv.at[h], source).wait_recv()

    for src, dst, send, recv, target, valid in plan:

        @pl.when(valid & (target != me))
        def _():
            remote(src, dst, send, recv, target).wait_send()


def attend(bounds, q, kv, blocks, back, scale):
    heads, rows, head_dim = q.shape
    per = heads
    span = back + per
    tries = back // per + 1
    return pl.pallas_call(
        functools.partial(attend_kernel, blocks, per, back, scale),
        out_shape=jax.ShapeDtypeStruct(q.shape, q.dtype),
        in_specs=[
            pl.BlockSpec(memory_space=pltpu.SMEM),
            pl.BlockSpec(memory_space=pl.ANY),
            pl.BlockSpec(memory_space=pl.ANY),
        ],
        out_specs=pl.BlockSpec(memory_space=pl.ANY),
        scratch_shapes=[
            pltpu.VMEM((per, rows, head_dim), q.dtype),
            pltpu.VMEM((span,) + kv.shape[1:], kv.dtype),
            pltpu.VMEM((per, rows, head_dim), q.dtype),
            pltpu.VMEM((per * rows, head_dim), jnp.float32),
            pltpu.VMEM((per * rows, 1), jnp.float32),
            pltpu.VMEM((per * rows, 1), jnp.float32),
            pltpu.VMEM((span, per * rows, rows), jnp.float32),
            pltpu.SemaphoreType.DMA((heads,)),
            pltpu.SemaphoreType.DMA((per,)),
            pltpu.SemaphoreType.DMA((heads, tries)),
            pltpu.SemaphoreType.DMA((span,)),
            pltpu.SemaphoreType.DMA((per,)),
            pltpu.SemaphoreType.DMA((heads,)),
        ],
        compiler_params=pltpu.CompilerParams(has_side_effects=True),
    )(bounds, q, kv)


def shards(
    queries, keys, values, lengths, resid, w_out, moe_gain, routes, gates, w_gate_up, w_down
):
    seq_count = lax.axis_size("seq")
    me = lax.axis_index("seq")
    query_rows = queries.shape[0]
    local_heads = queries.shape[1] // HEAD_DIM
    cols = queries.shape[1]
    width = resid.shape[1]
    score_scale = 1.0 / math.sqrt(HEAD_DIM)
    longest = (seq_count * query_rows) // 2
    reach = min(seq_count - 1, -(-(longest - 1) // query_rows))
    blocks = seq_count // local_heads
    per = seq_count // blocks
    back = -(-reach // per) * per
    span = back + per
    head_q = queries.reshape(query_rows, local_heads, HEAD_DIM).transpose(1, 0, 2)
    head_kv = jnp.concatenate(
        [
            keys.reshape(query_rows, local_heads, HEAD_DIM),
            values.reshape(query_rows, local_heads, HEAD_DIM),
        ],
        axis=2,
    ).transpose(1, 0, 2)
    attention = (
        attend(
            jnp.cumsum(lengths).astype(jnp.int32), head_q, head_kv, blocks, back, score_scale
        )
        .transpose(1, 0, 2)
        .reshape(query_rows, local_heads * HEAD_DIM)
    )
    tp_index = lax.axis_index("tp")
    near_swap = [(t, t ^ 1) for t in range(lax.axis_size("tp"))]
    far_swap = [(t, t ^ 2) for t in range(lax.axis_size("tp"))]
    local_rows = resid.shape[0]
    partial_proj = jnp.dot(attention, w_out, preferred_element_type=jnp.float32).reshape(
        2, 2, local_rows, width
    )
    core = tp_index % 2
    keep = lax.dynamic_index_in_dim(partial_proj, core, axis=1, keepdims=False)
    give = lax.dynamic_index_in_dim(partial_proj, 1 - core, axis=1, keepdims=False)
    half = keep + lax.ppermute(give.astype(jnp.bfloat16), "tp", near_swap).astype(jnp.float32)
    far = tp_index // 2
    pair_resid = jnp.stack([resid, lax.ppermute(resid, "tp", far_swap)])
    pair_routes = jnp.stack([routes, lax.ppermute(routes, "tp", far_swap)])
    pair_gates = jnp.stack([gates, lax.ppermute(gates, "tp", far_swap)])
    half = half.astype(jnp.bfloat16)
    total = half.astype(jnp.float32) + lax.ppermute(half, "tp", far_swap).astype(jnp.float32)
    pair_proj = jnp.stack(
        [
            lax.dynamic_index_in_dim(total, far, axis=0, keepdims=False),
            lax.dynamic_index_in_dim(total, 1 - far, axis=0, keepdims=False),
        ]
    )
    pair_attended = (pair_resid.astype(jnp.float32) + pair_proj).astype(jnp.bfloat16)
    attended = pair_attended[0]
    widened = pair_attended.astype(jnp.float32)
    meansq = jnp.mean(widened * widened, axis=2, keepdims=True)
    pair_normed = (widened * lax.rsqrt(meansq + 1e-05) * moe_gain).astype(jnp.bfloat16)
    top_count = routes.shape[1]
    owned = w_gate_up.shape[0]
    experts_all = owned * seq_count
    capacity = 3 * local_rows * top_count // (2 * experts_all)
    matches = pair_routes[..., None] == jnp.arange(experts_all, dtype=jnp.int32)
    member = jnp.any(matches, axis=2)
    slot = jnp.cumsum(member.astype(jnp.int32), axis=1) - 1
    place = member[..., None] & (slot[..., None] == jnp.arange(capacity, dtype=jnp.int32))
    halves = pair_normed.shape[0]
    same_half = jnp.eye(halves, dtype=jnp.bool_)
    dispatch = (
        place.reshape(halves, local_rows, seq_count, owned, capacity)
        .transpose(2, 0, 4, 3, 1)[:, :, :, :, None, :]
        & same_half[None, :, None, None, :, None]
    ).reshape(-1, halves * local_rows)
    buffer = jnp.dot(
        dispatch.astype(jnp.bfloat16),
        pair_normed.reshape(halves * local_rows, width),
        preferred_element_type=jnp.float32,
    ).astype(jnp.bfloat16).reshape(seq_count, halves, capacity, owned, width)
    arrived = lax.all_to_all(buffer, "seq", split_axis=0, concat_axis=0, tiled=True)
    near = lax.ppermute(arrived, "tp", near_swap)

    def expert_part(slots):
        projections = jnp.einsum(
            "szcxd,xdgf->szcxgf", slots, w_gate_up, preferred_element_type=jnp.float32
        )
        hidden = (jax.nn.silu(projections[..., 0, :]) * projections[..., 1, :]).astype(
            jnp.bfloat16
        )
        return jnp.einsum(
            "szcxf,xfd->szcxd", hidden, w_down, preferred_element_type=jnp.float32
        ).astype(jnp.bfloat16)

    from_near = lax.ppermute(expert_part(near), "tp", near_swap)
    reduced = (
        expert_part(arrived).astype(jnp.float32) + from_near.astype(jnp.float32)
    ).astype(jnp.bfloat16)
    returned = lax.all_to_all(reduced, "seq", split_axis=0, concat_axis=0, tiled=True)
    weight_of = jnp.sum(jnp.where(matches, pair_gates[..., None], 0.0), axis=2)
    mix_weights = jnp.where(place, weight_of[..., None], 0.0)
    combine = jnp.where(
        same_half[:, None, None, :, None, None],
        mix_weights.reshape(halves, local_rows, seq_count, owned, capacity)
        .transpose(0, 1, 2, 4, 3)[:, :, :, None, :, :],
        0.0,
    ).reshape(halves * local_rows, -1)
    mixes = jnp.dot(
        combine,
        returned.reshape(-1, width).astype(jnp.float32),
        precision=lax.Precision.HIGHEST,
        preferred_element_type=jnp.float32,
    ).reshape(halves, local_rows, width)
    expert_mix = (mixes[0] + lax.ppermute(mixes[1], "tp", far_swap)).astype(jnp.bfloat16)
    return (attended, expert_mix)


def solution(mesh):
    return jax.shard_map(
        shards,
        mesh=mesh,
        in_specs=(
            P("seq", "tp"),
            P("seq", "tp"),
            P("seq", "tp"),
            P(),
            P(("seq", "tp"), None),
            P("tp", None),
            P(),
            P(("seq", "tp"), None),
            P(("seq", "tp"), None),
            P("seq", None, None, "tp"),
            P("seq", "tp", None),
        ),
        out_specs=(P(("seq", "tp"), None), P(("seq", "tp"), None)),
        check_vma=False,
    )
```

```python
import functools
import math

import jax
import jax.numpy as jnp
from jax import lax
from jax.experimental import pallas as pl
from jax.experimental.pallas import tpu as pltpu
from jax.sharding import PartitionSpec as P

HEAD_DIM = 128


def tenant_of(positions, lengths):
    bounds = jnp.cumsum(lengths)
    return jnp.sum((positions[:, None] >= bounds[None, :]).astype(jnp.int32), axis=1)


def spread_kernel(
    blocks, per, back, q_ref, kv_ref, q_out, kv_out, q_send, q_recv, kv_send, kv_recv
):
    me = lax.axis_index("seq")
    tp = lax.axis_index("tp")
    heads = q_ref.shape[0]
    span = back + per
    tries = back // per + 1
    mine = me % blocks

    def send(src, dst, sem, recv, target):
        @pl.when(target == me)
        def _():
            pltpu.make_async_copy(src, dst, sem).start()

        @pl.when(target != me)
        def _():
            pltpu.make_async_remote_copy(
                src_ref=src,
                dst_ref=dst,
                send_sem=sem,
                recv_sem=recv,
                device_id=(target, tp),
                device_id_type=pl.DeviceIdType.MESH,
            ).start()

    def finish_send(src, dst, sem, recv, target):
        @pl.when(target == me)
        def _():
            pltpu.make_async_copy(src, dst, sem).wait()

        @pl.when(target != me)
        def _():
            pltpu.make_async_remote_copy(
                src_ref=src,
                dst_ref=dst,
                send_sem=sem,
                recv_sem=recv,
                device_id=(target, tp),
                device_id_type=pl.DeviceIdType.MESH,
            ).wait_send()

    def finish_recv(src, dst, sem, recv, source):
        @pl.when(source != me)
        def _():
            pltpu.make_async_remote_copy(
                src_ref=src,
                dst_ref=dst,
                send_sem=sem,
                recv_sem=recv,
                device_id=(source, tp),
                device_id_type=pl.DeviceIdType.MESH,
            ).wait_recv()

    plan = []
    for h in range(heads):
        target = h * blocks + me // per
        plan.append((q_ref.at[h], q_out.at[me % per], q_send.at[h], q_recv.at[me % per], target))
        for r in range(tries):
            block = (me + back) // per - r
            slot = (me + back) % per + per * r
            plan.append(
                (
                    kv_ref.at[h],
                    kv_out.at[slot],
                    kv_send.at[h, r],
                    kv_recv.at[slot],
                    h * blocks + block,
                    (block >= 0) & (block < blocks),
                )
            )
    for item in plan:
        valid = item[5] if len(item) > 5 else True

        @pl.when(valid)
        def _():
            send(*item[:5])

    for item in plan:
        valid = item[5] if len(item) > 5 else True

        @pl.when(valid)
        def _():
            finish_send(*item[:5])

    for i in range(per):
        source = per * mine + i
        finish_recv(q_ref.at[0], q_out.at[i], q_send.at[0], q_recv.at[i], source)
    for slot in range(span):
        source = per * mine - back + slot

        @pl.when(source >= 0)
        def _():
            finish_recv(kv_ref.at[0], kv_out.at[slot], kv_send.at[0, 0], kv_recv.at[slot], source)


def spread(q, kv, blocks, per, back):
    heads = q.shape[0]
    span = back + per
    tries = back // per + 1
    return pl.pallas_call(
        functools.partial(spread_kernel, blocks, per, back),
        out_shape=(
            jax.ShapeDtypeStruct((per,) + q.shape[1:], q.dtype),
            jax.ShapeDtypeStruct((span,) + kv.shape[1:], kv.dtype),
        ),
        in_specs=[pl.BlockSpec(memory_space=pl.ANY)] * 2,
        out_specs=(pl.BlockSpec(memory_space=pl.ANY), pl.BlockSpec(memory_space=pl.ANY)),
        scratch_shapes=[
            pltpu.SemaphoreType.DMA((heads,)),
            pltpu.SemaphoreType.DMA((per,)),
            pltpu.SemaphoreType.DMA((heads, tries)),
            pltpu.SemaphoreType.DMA((span,)),
        ],
        compiler_params=pltpu.CompilerParams(has_side_effects=True),
    )(q, kv)


def gather_kernel(blocks, per, att_ref, out_ref, send_sem, recv_sem):
    me = lax.axis_index("seq")
    tp = lax.axis_index("tp")
    heads = out_ref.shape[0]
    head = me // blocks
    mine = me % blocks

    def copy(i, target):
        return pltpu.make_async_remote_copy(
            src_ref=att_ref.at[i],
            dst_ref=out_ref.at[head],
            send_sem=send_sem.at[i],
            recv_sem=recv_sem.at[head],
            device_id=(target, tp),
            device_id_type=pl.DeviceIdType.MESH,
        )

    for i in range(per):
        target = per * mine + i

        @pl.when(target == me)
        def _():
            pltpu.make_async_copy(att_ref.at[i], out_ref.at[head], send_sem.at[i]).start()

        @pl.when(target != me)
        def _():
            copy(i, target).start()

    for i in range(per):
        target = per * mine + i

        @pl.when(target == me)
        def _():
            pltpu.make_async_copy(att_ref.at[i], out_ref.at[head], send_sem.at[i]).wait()

        @pl.when(target != me)
        def _():
            copy(i, target).wait_send()

    for h in range(heads):
        source = h * blocks + me // per

        @pl.when(source != me)
        def _():
            pltpu.make_async_remote_copy(
                src_ref=att_ref.at[0],
                dst_ref=out_ref.at[h],
                send_sem=send_sem.at[0],
                recv_sem=recv_sem.at[h],
                device_id=(source, tp),
                device_id_type=pl.DeviceIdType.MESH,
            ).wait_recv()


def gather_back(att, heads, blocks):
    per = att.shape[0]
    return pl.pallas_call(
        functools.partial(gather_kernel, blocks, per),
        out_shape=jax.ShapeDtypeStruct((heads,) + att.shape[1:], att.dtype),
        in_specs=[pl.BlockSpec(memory_space=pl.ANY)],
        out_specs=pl.BlockSpec(memory_space=pl.ANY),
        scratch_shapes=[pltpu.SemaphoreType.DMA((per,)), pltpu.SemaphoreType.DMA((heads,))],
        compiler_params=pltpu.CompilerParams(has_side_effects=True),
    )(att)


def attend_kernel(
    blocks, per, back, scale, bounds_ref, q_ref, kv_ref, out_ref,
    q_in, kv_in, att, acc, top, total, kept,
    q_send, q_recv, kv_send, kv_recv, att_send, att_recv,
):
    me = lax.axis_index("seq")
    tp = lax.axis_index("tp")
    heads, rows, head_dim = q_ref.shape
    span = back + per
    tries = back // per + 1
    mine = me % blocks
    head = me // blocks

    def remote(src, dst, send, recv, device):
        return pltpu.make_async_remote_copy(
            src_ref=src, dst_ref=dst, send_sem=send, recv_sem=recv,
            device_id=(device, tp), device_id_type=pl.DeviceIdType.MESH,
        )

    plan = []
    for h in range(heads):
        target = h * blocks + me // per
        plan.append(
            (q_ref.at[h], q_in.at[me % per], q_send.at[h], q_recv.at[me % per], target, True)
        )
        for r in range(tries):
            block = (me + back) // per - r
            slot = (me + back) % per + per * r
            valid = (block >= 0) & (block < blocks)
            plan.append(
                (kv_ref.at[h], kv_in.at[slot], kv_send.at[h, r], kv_recv.at[slot],
                 h * blocks + block, valid)
            )
    for src, dst, send, recv, target, valid in plan:

        @pl.when(valid & (target == me))
        def _():
            pltpu.make_async_copy(src, dst, send).start()

        @pl.when(valid & (target != me))
        def _():
            remote(src, dst, send, recv, target).start()

    for src, dst, send, recv, target, valid in plan:

        @pl.when(valid & (target == me))
        def _():
            pltpu.make_async_copy(src, dst, send).wait()

    for i in range(per):
        source = per * mine + i

        @pl.when(source != me)
        def _():
            remote(q_ref.at[0], q_in.at[i], q_send.at[0], q_recv.at[i], source).wait_recv()

    query = q_in[...].reshape(per * rows, head_dim)
    query_pos = mine * per * rows + lax.broadcasted_iota(jnp.int32, (per * rows, 1), 0)
    first = jnp.zeros(query_pos.shape, jnp.int32)
    for k in range(bounds_ref.shape[0]):
        first = jnp.maximum(first, jnp.where(query_pos >= bounds_ref[k], bounds_ref[k], 0))

    top[...] = jnp.full(top.shape, -1e30, jnp.float32)
    total[...] = jnp.zeros(total.shape, jnp.float32)
    acc[...] = jnp.zeros(acc.shape, jnp.float32)

    def first_pass(slot, carry):
        source = per * mine - back + slot

        @pl.when(source >= 0)
        def _():
            @pl.when(source != me)
            def _():
                remote(
                    kv_ref.at[0], kv_in.at[slot], kv_send.at[0, 0], kv_recv.at[slot], source
                ).wait_recv()

            key_pos = source * rows + lax.broadcasted_iota(jnp.int32, (1, rows), 1)
            visible = (key_pos >= first) & (key_pos <= query_pos)
            scores = lax.dot_general(
                query, kv_in[slot, :, :head_dim], (((1,), (1,)), ((), ())),
                preferred_element_type=jnp.float32,
            ) * scale
            scores = jnp.where(visible, scores, -1e30)
            kept[slot] = scores
            top[...] = jnp.maximum(top[...], jnp.max(scores, axis=1, keepdims=True))

        return carry

    lax.fori_loop(0, span, first_pass, 0)

    def second_pass(slot, carry):
        source = per * mine - back + slot

        @pl.when(source >= 0)
        def _():
            weights = jnp.exp(kept[slot] - top[...])
            total[...] += jnp.sum(weights, axis=1, keepdims=True)
            acc[...] += jnp.dot(
                weights.astype(jnp.bfloat16), kv_in[slot, :, head_dim:],
                preferred_element_type=jnp.float32,
            )

        return carry

    lax.fori_loop(0, span, second_pass, 0)
    att[...] = (acc[...] / total[...]).astype(att.dtype).reshape(att.shape)

    for i in range(per):
        target = per * mine + i

        @pl.when(target == me)
        def _():
            pltpu.make_async_copy(att.at[i], out_ref.at[head], att_send.at[i]).start()

        @pl.when(target != me)
        def _():
            remote(att.at[i], out_ref.at[head], att_send.at[i], att_recv.at[head], target).start()

    for i in range(per):
        target = per * mine + i

        @pl.when(target == me)
        def _():
            pltpu.make_async_copy(att.at[i], out_ref.at[head], att_send.at[i]).wait()

        @pl.when(target != me)
        def _():
            remote(
                att.at[i], out_ref.at[head], att_send.at[i], att_recv.at[head], target
            ).wait_send()

    for h in range(heads):
        source = h * blocks + me // per

        @pl.when(source != me)
        def _():
            remote(att.at[0], out_ref.at[h], att_send.at[0], att_recv.at[h], source).wait_recv()

    for src, dst, send, recv, target, valid in plan:

        @pl.when(valid & (target != me))
        def _():
            remote(src, dst, send, recv, target).wait_send()


def attend(bounds, q, kv, blocks, back, scale):
    heads, rows, head_dim = q.shape
    per = heads
    span = back + per
    tries = back // per + 1
    return pl.pallas_call(
        functools.partial(attend_kernel, blocks, per, back, scale),
        out_shape=jax.ShapeDtypeStruct(q.shape, q.dtype),
        in_specs=[
            pl.BlockSpec(memory_space=pltpu.SMEM),
            pl.BlockSpec(memory_space=pl.ANY),
            pl.BlockSpec(memory_space=pl.ANY),
        ],
        out_specs=pl.BlockSpec(memory_space=pl.ANY),
        scratch_shapes=[
            pltpu.VMEM((per, rows, head_dim), q.dtype),
            pltpu.VMEM((span,) + kv.shape[1:], kv.dtype),
            pltpu.VMEM((per, rows, head_dim), q.dtype),
            pltpu.VMEM((per * rows, head_dim), jnp.float32),
            pltpu.VMEM((per * rows, 1), jnp.float32),
            pltpu.VMEM((per * rows, 1), jnp.float32),
            pltpu.VMEM((span, per * rows, rows), jnp.float32),
            pltpu.SemaphoreType.DMA((heads,)),
            pltpu.SemaphoreType.DMA((per,)),
            pltpu.SemaphoreType.DMA((heads, tries)),
            pltpu.SemaphoreType.DMA((span,)),
            pltpu.SemaphoreType.DMA((per,)),
            pltpu.SemaphoreType.DMA((heads,)),
        ],
        compiler_params=pltpu.CompilerParams(has_side_effects=True),
    )(bounds, q, kv)


def shards(
    queries, keys, values, lengths, resid, w_out, moe_gain, routes, gates, w_gate_up, w_down
):
    seq_count = lax.axis_size("seq")
    me = lax.axis_index("seq")
    query_rows = queries.shape[0]
    local_heads = queries.shape[1] // HEAD_DIM
    cols = queries.shape[1]
    width = resid.shape[1]
    score_scale = 1.0 / math.sqrt(HEAD_DIM)
    longest = (seq_count * query_rows) // 2
    reach = min(seq_count - 1, -(-(longest - 1) // query_rows))
    blocks = seq_count // local_heads
    per = seq_count // blocks
    back = -(-reach // per) * per
    span = back + per
    head_q = queries.reshape(query_rows, local_heads, HEAD_DIM).transpose(1, 0, 2)
    head_kv = jnp.concatenate(
        [
            keys.reshape(query_rows, local_heads, HEAD_DIM),
            values.reshape(query_rows, local_heads, HEAD_DIM),
        ],
        axis=2,
    ).transpose(1, 0, 2)
    attention = (
        attend(
            jnp.cumsum(lengths).astype(jnp.int32), head_q, head_kv, blocks, back, score_scale
        )
        .transpose(1, 0, 2)
        .reshape(query_rows, local_heads * HEAD_DIM)
    )
    tp_index = lax.axis_index("tp")
    near_swap = [(t, t ^ 1) for t in range(lax.axis_size("tp"))]
    far_swap = [(t, t ^ 2) for t in range(lax.axis_size("tp"))]
    local_rows = resid.shape[0]
    partial_proj = jnp.dot(attention, w_out, preferred_element_type=jnp.float32).reshape(
        2, 2, local_rows, width
    )
    core = tp_index % 2
    keep = lax.dynamic_index_in_dim(partial_proj, core, axis=1, keepdims=False)
    give = lax.dynamic_index_in_dim(partial_proj, 1 - core, axis=1, keepdims=False)
    half = keep + lax.ppermute(give.astype(jnp.bfloat16), "tp", near_swap).astype(jnp.float32)
    far = tp_index // 2
    pair_resid = jnp.stack([resid, lax.ppermute(resid, "tp", far_swap)])
    pair_routes = jnp.stack([routes, lax.ppermute(routes, "tp", far_swap)])
    pair_gates = jnp.stack([gates, lax.ppermute(gates, "tp", far_swap)])
    half = half.astype(jnp.bfloat16)
    total = half.astype(jnp.float32) + lax.ppermute(half, "tp", far_swap).astype(jnp.float32)
    pair_proj = jnp.stack(
        [
            lax.dynamic_index_in_dim(total, far, axis=0, keepdims=False),
            lax.dynamic_index_in_dim(total, 1 - far, axis=0, keepdims=False),
        ]
    )
    pair_attended = (pair_resid.astype(jnp.float32) + pair_proj).astype(jnp.bfloat16)
    attended = pair_attended[0]
    widened = pair_attended.astype(jnp.float32)
    meansq = jnp.mean(widened * widened, axis=2, keepdims=True)
    pair_normed = (widened * lax.rsqrt(meansq + 1e-05) * moe_gain).astype(jnp.bfloat16)
    top_count = routes.shape[1]
    owned = w_gate_up.shape[0]
    experts_all = owned * seq_count
    capacity = 3 * local_rows * top_count // (2 * experts_all)
    matches = pair_routes[..., None] == jnp.arange(experts_all, dtype=jnp.int32)
    member = jnp.any(matches, axis=2)
    slot = jnp.cumsum(member.astype(jnp.int32), axis=1) - 1
    place = member[..., None] & (slot[..., None] == jnp.arange(capacity, dtype=jnp.int32))
    buffer = jnp.einsum(
        "xiec,xid->excd", place.astype(jnp.bfloat16), pair_normed,
        preferred_element_type=jnp.float32,
    ).astype(jnp.bfloat16)
    buffer = buffer.reshape(seq_count, owned, 2, capacity, width).transpose(1, 0, 2, 3, 4)
    arrived = lax.all_to_all(buffer, "seq", split_axis=1, concat_axis=1, tiled=True)
    near = lax.ppermute(arrived, "tp", near_swap)

    def expert_part(slots):
        projections = jnp.einsum(
            "xnd,xdgf->xngf", slots.reshape(owned, -1, width), w_gate_up,
            preferred_element_type=jnp.float32,
        )
        hidden = (jax.nn.silu(projections[..., 0, :]) * projections[..., 1, :]).astype(
            jnp.bfloat16
        )
        return jnp.einsum(
            "xnf,xfd->xnd", hidden, w_down, preferred_element_type=jnp.float32
        ).astype(jnp.bfloat16)

    from_near = lax.ppermute(expert_part(near), "tp", near_swap)
    reduced = (
        expert_part(arrived).astype(jnp.float32) + from_near.astype(jnp.float32)
    ).astype(jnp.bfloat16)
    returned = lax.all_to_all(
        reduced.reshape(arrived.shape), "seq", split_axis=1, concat_axis=1, tiled=True
    )
    weight_of = jnp.sum(jnp.where(matches, pair_gates[..., None], 0.0), axis=2)
    mix_weights = jnp.where(place, weight_of[..., None], 0.0)
    mixes = jnp.einsum(
        "xiec,xecd->xid",
        mix_weights.astype(jnp.bfloat16),
        returned.transpose(2, 1, 0, 3, 4).reshape(2, experts_all, capacity, width),
        preferred_element_type=jnp.float32,
    )
    from_far = lax.ppermute(mixes[1].astype(jnp.bfloat16), "tp", far_swap)
    expert_mix = (mixes[0] + from_far.astype(jnp.float32)).astype(jnp.bfloat16)
    return (attended, expert_mix)


def solution(mesh):
    return jax.shard_map(
        shards,
        mesh=mesh,
        in_specs=(
            P("seq", "tp"),
            P("seq", "tp"),
            P("seq", "tp"),
            P(),
            P(("seq", "tp"), None),
            P("tp", None),
            P(),
            P(("seq", "tp"), None),
            P(("seq", "tp"), None),
            P("seq", None, None, "tp"),
            P("seq", "tp", None),
        ),
        out_specs=(P(("seq", "tp"), None), P(("seq", "tp"), None)),
        check_vma=False,
    )
```

```python
import functools
import math

import jax
import jax.numpy as jnp
from jax import lax
from jax.experimental import pallas as pl
from jax.experimental.pallas import tpu as pltpu
from jax.sharding import PartitionSpec as P

HEAD_DIM = 128


def tenant_of(positions, lengths):
    bounds = jnp.cumsum(lengths)
    return jnp.sum((positions[:, None] >= bounds[None, :]).astype(jnp.int32), axis=1)


def spread_kernel(
    blocks, per, back, q_ref, kv_ref, q_out, kv_out, q_send, q_recv, kv_send, kv_recv
):
    me = lax.axis_index("seq")
    tp = lax.axis_index("tp")
    heads = q_ref.shape[0]
    span = back + per
    tries = back // per + 1
    mine = me % blocks

    def send(src, dst, sem, recv, target):
        @pl.when(target == me)
        def _():
            pltpu.make_async_copy(src, dst, sem).start()

        @pl.when(target != me)
        def _():
            pltpu.make_async_remote_copy(
                src_ref=src,
                dst_ref=dst,
                send_sem=sem,
                recv_sem=recv,
                device_id=(target, tp),
                device_id_type=pl.DeviceIdType.MESH,
            ).start()

    def finish_send(src, dst, sem, recv, target):
        @pl.when(target == me)
        def _():
            pltpu.make_async_copy(src, dst, sem).wait()

        @pl.when(target != me)
        def _():
            pltpu.make_async_remote_copy(
                src_ref=src,
                dst_ref=dst,
                send_sem=sem,
                recv_sem=recv,
                device_id=(target, tp),
                device_id_type=pl.DeviceIdType.MESH,
            ).wait_send()

    def finish_recv(src, dst, sem, recv, source):
        @pl.when(source != me)
        def _():
            pltpu.make_async_remote_copy(
                src_ref=src,
                dst_ref=dst,
                send_sem=sem,
                recv_sem=recv,
                device_id=(source, tp),
                device_id_type=pl.DeviceIdType.MESH,
            ).wait_recv()

    plan = []
    for h in range(heads):
        target = h * blocks + me // per
        plan.append((q_ref.at[h], q_out.at[me % per], q_send.at[h], q_recv.at[me % per], target))
        for r in range(tries):
            block = (me + back) // per - r
            slot = (me + back) % per + per * r
            plan.append(
                (
                    kv_ref.at[h],
                    kv_out.at[slot],
                    kv_send.at[h, r],
                    kv_recv.at[slot],
                    h * blocks + block,
                    (block >= 0) & (block < blocks),
                )
            )
    for item in plan:
        valid = item[5] if len(item) > 5 else True

        @pl.when(valid)
        def _():
            send(*item[:5])

    for item in plan:
        valid = item[5] if len(item) > 5 else True

        @pl.when(valid)
        def _():
            finish_send(*item[:5])

    for i in range(per):
        source = per * mine + i
        finish_recv(q_ref.at[0], q_out.at[i], q_send.at[0], q_recv.at[i], source)
    for slot in range(span):
        source = per * mine - back + slot

        @pl.when(source >= 0)
        def _():
            finish_recv(kv_ref.at[0], kv_out.at[slot], kv_send.at[0, 0], kv_recv.at[slot], source)


def spread(q, kv, blocks, per, back):
    heads = q.shape[0]
    span = back + per
    tries = back // per + 1
    return pl.pallas_call(
        functools.partial(spread_kernel, blocks, per, back),
        out_shape=(
            jax.ShapeDtypeStruct((per,) + q.shape[1:], q.dtype),
            jax.ShapeDtypeStruct((span,) + kv.shape[1:], kv.dtype),
        ),
        in_specs=[pl.BlockSpec(memory_space=pl.ANY)] * 2,
        out_specs=(pl.BlockSpec(memory_space=pl.ANY), pl.BlockSpec(memory_space=pl.ANY)),
        scratch_shapes=[
            pltpu.SemaphoreType.DMA((heads,)),
            pltpu.SemaphoreType.DMA((per,)),
            pltpu.SemaphoreType.DMA((heads, tries)),
            pltpu.SemaphoreType.DMA((span,)),
        ],
        compiler_params=pltpu.CompilerParams(has_side_effects=True),
    )(q, kv)


def gather_kernel(blocks, per, att_ref, out_ref, send_sem, recv_sem):
    me = lax.axis_index("seq")
    tp = lax.axis_index("tp")
    heads = out_ref.shape[0]
    head = me // blocks
    mine = me % blocks

    def copy(i, target):
        return pltpu.make_async_remote_copy(
            src_ref=att_ref.at[i],
            dst_ref=out_ref.at[head],
            send_sem=send_sem.at[i],
            recv_sem=recv_sem.at[head],
            device_id=(target, tp),
            device_id_type=pl.DeviceIdType.MESH,
        )

    for i in range(per):
        target = per * mine + i

        @pl.when(target == me)
        def _():
            pltpu.make_async_copy(att_ref.at[i], out_ref.at[head], send_sem.at[i]).start()

        @pl.when(target != me)
        def _():
            copy(i, target).start()

    for i in range(per):
        target = per * mine + i

        @pl.when(target == me)
        def _():
            pltpu.make_async_copy(att_ref.at[i], out_ref.at[head], send_sem.at[i]).wait()

        @pl.when(target != me)
        def _():
            copy(i, target).wait_send()

    for h in range(heads):
        source = h * blocks + me // per

        @pl.when(source != me)
        def _():
            pltpu.make_async_remote_copy(
                src_ref=att_ref.at[0],
                dst_ref=out_ref.at[h],
                send_sem=send_sem.at[0],
                recv_sem=recv_sem.at[h],
                device_id=(source, tp),
                device_id_type=pl.DeviceIdType.MESH,
            ).wait_recv()


def gather_back(att, heads, blocks):
    per = att.shape[0]
    return pl.pallas_call(
        functools.partial(gather_kernel, blocks, per),
        out_shape=jax.ShapeDtypeStruct((heads,) + att.shape[1:], att.dtype),
        in_specs=[pl.BlockSpec(memory_space=pl.ANY)],
        out_specs=pl.BlockSpec(memory_space=pl.ANY),
        scratch_shapes=[pltpu.SemaphoreType.DMA((per,)), pltpu.SemaphoreType.DMA((heads,))],
        compiler_params=pltpu.CompilerParams(has_side_effects=True),
    )(att)


def attend_kernel(
    blocks, per, back, scale, bounds_ref, q_ref, kv_ref, out_ref,
    q_in, kv_in, att, acc, top, total, kept,
    q_send, q_recv, kv_send, kv_recv, att_send, att_recv,
):
    me = lax.axis_index("seq")
    tp = lax.axis_index("tp")
    heads, rows, head_dim = q_ref.shape
    span = back + per
    tries = back // per + 1
    mine = me % blocks
    head = me // blocks

    def remote(src, dst, send, recv, device):
        return pltpu.make_async_remote_copy(
            src_ref=src, dst_ref=dst, send_sem=send, recv_sem=recv,
            device_id=(device, tp), device_id_type=pl.DeviceIdType.MESH,
        )

    plan = []
    for h in range(heads):
        target = h * blocks + me // per
        plan.append(
            (q_ref.at[h], q_in.at[me % per], q_send.at[h], q_recv.at[me % per], target, True)
        )
        for r in range(tries):
            block = (me + back) // per - r
            slot = (me + back) % per + per * r
            valid = (block >= 0) & (block < blocks)
            plan.append(
                (kv_ref.at[h], kv_in.at[slot], kv_send.at[h, r], kv_recv.at[slot],
                 h * blocks + block, valid)
            )
    for src, dst, send, recv, target, valid in plan:

        @pl.when(valid & (target == me))
        def _():
            pltpu.make_async_copy(src, dst, send).start()

        @pl.when(valid & (target != me))
        def _():
            remote(src, dst, send, recv, target).start()

    for src, dst, send, recv, target, valid in plan:

        @pl.when(valid & (target == me))
        def _():
            pltpu.make_async_copy(src, dst, send).wait()

    for i in range(per):
        source = per * mine + i

        @pl.when(source != me)
        def _():
            remote(q_ref.at[0], q_in.at[i], q_send.at[0], q_recv.at[i], source).wait_recv()

    query = q_in[...].reshape(per * rows, head_dim)
    query_pos = mine * per * rows + lax.broadcasted_iota(jnp.int32, (per * rows, 1), 0)
    first = jnp.zeros(query_pos.shape, jnp.int32)
    for k in range(bounds_ref.shape[0]):
        first = jnp.maximum(first, jnp.where(query_pos >= bounds_ref[k], bounds_ref[k], 0))

    top[...] = jnp.full(top.shape, -1e30, jnp.float32)
    total[...] = jnp.zeros(total.shape, jnp.float32)
    acc[...] = jnp.zeros(acc.shape, jnp.float32)

    def first_pass(slot, carry):
        source = per * mine - back + slot

        @pl.when(source >= 0)
        def _():
            @pl.when(source != me)
            def _():
                remote(
                    kv_ref.at[0], kv_in.at[slot], kv_send.at[0, 0], kv_recv.at[slot], source
                ).wait_recv()

            key_pos = source * rows + lax.broadcasted_iota(jnp.int32, (1, rows), 1)
            visible = (key_pos >= first) & (key_pos <= query_pos)
            scores = lax.dot_general(
                query, kv_in[slot, :, :head_dim], (((1,), (1,)), ((), ())),
                preferred_element_type=jnp.float32,
            ) * scale
            scores = jnp.where(visible, scores, -1e30)
            kept[slot] = scores
            top[...] = jnp.maximum(top[...], jnp.max(scores, axis=1, keepdims=True))

        return carry

    lax.fori_loop(0, span, first_pass, 0)

    def second_pass(slot, carry):
        source = per * mine - back + slot

        @pl.when(source >= 0)
        def _():
            weights = jnp.exp(kept[slot] - top[...])
            total[...] += jnp.sum(weights, axis=1, keepdims=True)
            acc[...] += jnp.dot(
                weights.astype(jnp.bfloat16), kv_in[slot, :, head_dim:],
                preferred_element_type=jnp.float32,
            )

        return carry

    lax.fori_loop(0, span, second_pass, 0)
    att[...] = (acc[...] / total[...]).astype(att.dtype).reshape(att.shape)

    for i in range(per):
        target = per * mine + i

        @pl.when(target == me)
        def _():
            pltpu.make_async_copy(att.at[i], out_ref.at[head], att_send.at[i]).start()

        @pl.when(target != me)
        def _():
            remote(att.at[i], out_ref.at[head], att_send.at[i], att_recv.at[head], target).start()

    for i in range(per):
        target = per * mine + i

        @pl.when(target == me)
        def _():
            pltpu.make_async_copy(att.at[i], out_ref.at[head], att_send.at[i]).wait()

        @pl.when(target != me)
        def _():
            remote(
                att.at[i], out_ref.at[head], att_send.at[i], att_recv.at[head], target
            ).wait_send()

    for h in range(heads):
        source = h * blocks + me // per

        @pl.when(source != me)
        def _():
            remote(att.at[0], out_ref.at[h], att_send.at[0], att_recv.at[h], source).wait_recv()

    for src, dst, send, recv, target, valid in plan:

        @pl.when(valid & (target != me))
        def _():
            remote(src, dst, send, recv, target).wait_send()


def attend(bounds, q, kv, blocks, back, scale):
    heads, rows, head_dim = q.shape
    per = heads
    span = back + per
    tries = back // per + 1
    return pl.pallas_call(
        functools.partial(attend_kernel, blocks, per, back, scale),
        out_shape=jax.ShapeDtypeStruct(q.shape, q.dtype),
        in_specs=[
            pl.BlockSpec(memory_space=pltpu.SMEM),
            pl.BlockSpec(memory_space=pl.ANY),
            pl.BlockSpec(memory_space=pl.ANY),
        ],
        out_specs=pl.BlockSpec(memory_space=pl.ANY),
        scratch_shapes=[
            pltpu.VMEM((per, rows, head_dim), q.dtype),
            pltpu.VMEM((span,) + kv.shape[1:], kv.dtype),
            pltpu.VMEM((per, rows, head_dim), q.dtype),
            pltpu.VMEM((per * rows, head_dim), jnp.float32),
            pltpu.VMEM((per * rows, 1), jnp.float32),
            pltpu.VMEM((per * rows, 1), jnp.float32),
            pltpu.VMEM((span, per * rows, rows), jnp.float32),
            pltpu.SemaphoreType.DMA((heads,)),
            pltpu.SemaphoreType.DMA((per,)),
            pltpu.SemaphoreType.DMA((heads, tries)),
            pltpu.SemaphoreType.DMA((span,)),
            pltpu.SemaphoreType.DMA((per,)),
            pltpu.SemaphoreType.DMA((heads,)),
        ],
        compiler_params=pltpu.CompilerParams(has_side_effects=True),
    )(bounds, q, kv)


def shards(
    queries, keys, values, lengths, resid, w_out, moe_gain, routes, gates, w_gate_up, w_down
):
    seq_count = lax.axis_size("seq")
    me = lax.axis_index("seq")
    query_rows = queries.shape[0]
    local_heads = queries.shape[1] // HEAD_DIM
    cols = queries.shape[1]
    width = resid.shape[1]
    score_scale = 1.0 / math.sqrt(HEAD_DIM)
    longest = (seq_count * query_rows) // 2
    reach = min(seq_count - 1, -(-(longest - 1) // query_rows))
    blocks = seq_count // local_heads
    per = seq_count // blocks
    back = -(-reach // per) * per
    span = back + per
    head_q = queries.reshape(query_rows, local_heads, HEAD_DIM).transpose(1, 0, 2)
    head_kv = jnp.concatenate(
        [
            keys.reshape(query_rows, local_heads, HEAD_DIM),
            values.reshape(query_rows, local_heads, HEAD_DIM),
        ],
        axis=2,
    ).transpose(1, 0, 2)
    attention = (
        attend(
            jnp.cumsum(lengths).astype(jnp.int32), head_q, head_kv, blocks, back, score_scale
        )
        .transpose(1, 0, 2)
        .reshape(query_rows, local_heads * HEAD_DIM)
    )
    tp_index = lax.axis_index("tp")
    near_swap = [(t, t ^ 1) for t in range(lax.axis_size("tp"))]
    far_swap = [(t, t ^ 2) for t in range(lax.axis_size("tp"))]
    local_rows = resid.shape[0]
    partial_proj = jnp.dot(attention, w_out, preferred_element_type=jnp.float32).reshape(
        2, 2, local_rows, width
    )
    core = tp_index % 2
    keep = lax.dynamic_index_in_dim(partial_proj, core, axis=1, keepdims=False)
    give = lax.dynamic_index_in_dim(partial_proj, 1 - core, axis=1, keepdims=False)
    half = keep + lax.ppermute(give.astype(jnp.bfloat16), "tp", near_swap).astype(jnp.float32)
    far = tp_index // 2
    pair_resid = jnp.stack([resid, lax.ppermute(resid, "tp", far_swap)])
    pair_routes = jnp.stack([routes, lax.ppermute(routes, "tp", far_swap)])
    pair_gates = jnp.stack([gates, lax.ppermute(gates, "tp", far_swap)])
    half = half.astype(jnp.bfloat16)
    total = half.astype(jnp.float32) + lax.ppermute(half, "tp", far_swap).astype(jnp.float32)
    pair_proj = jnp.stack(
        [
            lax.dynamic_index_in_dim(total, far, axis=0, keepdims=False),
            lax.dynamic_index_in_dim(total, 1 - far, axis=0, keepdims=False),
        ]
    )
    pair_attended = (pair_resid.astype(jnp.float32) + pair_proj).astype(jnp.bfloat16)
    attended = pair_attended[0]
    widened = pair_attended.astype(jnp.float32)
    meansq = jnp.mean(widened * widened, axis=2, keepdims=True)
    pair_normed = (widened * lax.rsqrt(meansq + 1e-05) * moe_gain).astype(jnp.bfloat16)
    top_count = routes.shape[1]
    owned = w_gate_up.shape[0]
    experts_all = owned * seq_count
    capacity = 3 * local_rows * top_count // (2 * experts_all)
    matches = pair_routes[..., None] == jnp.arange(experts_all, dtype=jnp.int32)
    member = jnp.any(matches, axis=2)
    slot = jnp.cumsum(member.astype(jnp.int32), axis=1) - 1
    place = member[..., None] & (slot[..., None] == jnp.arange(capacity, dtype=jnp.int32))
    buffer = jnp.einsum(
        "xiec,xid->excd", place.astype(jnp.bfloat16), pair_normed,
        preferred_element_type=jnp.bfloat16,
    )
    buffer = buffer.reshape(seq_count, owned, 2, capacity, width).transpose(1, 0, 2, 3, 4)
    arrived = lax.all_to_all(buffer, "seq", split_axis=1, concat_axis=1, tiled=True)
    near = lax.ppermute(arrived, "tp", near_swap)

    def expert_part(slots):
        projections = jnp.einsum(
            "xnd,xdgf->xngf", slots.reshape(owned, -1, width), w_gate_up,
            preferred_element_type=jnp.float32,
        )
        hidden = (jax.nn.silu(projections[..., 0, :]) * projections[..., 1, :]).astype(
            jnp.bfloat16
        )
        return jnp.einsum(
            "xnf,xfd->xnd", hidden, w_down, preferred_element_type=jnp.float32
        ).astype(jnp.bfloat16)

    from_near = lax.ppermute(expert_part(near), "tp", near_swap)
    reduced = (
        expert_part(arrived).astype(jnp.float32) + from_near.astype(jnp.float32)
    ).astype(jnp.bfloat16)
    returned = lax.all_to_all(
        reduced.reshape(arrived.shape), "seq", split_axis=1, concat_axis=1, tiled=True
    )
    weight_of = jnp.sum(jnp.where(matches, pair_gates[..., None], 0.0), axis=2)
    mix_weights = jnp.where(place, weight_of[..., None], 0.0)
    mixes = jnp.einsum(
        "xiec,xecd->xid",
        mix_weights.astype(jnp.bfloat16),
        returned.transpose(2, 1, 0, 3, 4).reshape(2, experts_all, capacity, width),
        preferred_element_type=jnp.float32,
    )
    from_far = lax.ppermute(mixes[1].astype(jnp.bfloat16), "tp", far_swap)
    expert_mix = (mixes[0] + from_far.astype(jnp.float32)).astype(jnp.bfloat16)
    return (attended, expert_mix)


def solution(mesh):
    return jax.shard_map(
        shards,
        mesh=mesh,
        in_specs=(
            P("seq", "tp"),
            P("seq", "tp"),
            P("seq", "tp"),
            P(),
            P(("seq", "tp"), None),
            P("tp", None),
            P(),
            P(("seq", "tp"), None),
            P(("seq", "tp"), None),
            P("seq", None, None, "tp"),
            P("seq", "tp", None),
        ),
        out_specs=(P(("seq", "tp"), None), P(("seq", "tp"), None)),
        check_vma=False,
    )
```

```python
import functools
import math

import jax
import jax.numpy as jnp
from jax import lax
from jax.experimental import pallas as pl
from jax.experimental.pallas import tpu as pltpu
from jax.sharding import PartitionSpec as P

HEAD_DIM = 128


def tenant_of(positions, lengths):
    bounds = jnp.cumsum(lengths)
    return jnp.sum((positions[:, None] >= bounds[None, :]).astype(jnp.int32), axis=1)


def spread_kernel(
    blocks, per, back, q_ref, kv_ref, q_out, kv_out, q_send, q_recv, kv_send, kv_recv
):
    me = lax.axis_index("seq")
    tp = lax.axis_index("tp")
    heads = q_ref.shape[0]
    span = back + per
    tries = back // per + 1
    mine = me % blocks

    def send(src, dst, sem, recv, target):
        @pl.when(target == me)
        def _():
            pltpu.make_async_copy(src, dst, sem).start()

        @pl.when(target != me)
        def _():
            pltpu.make_async_remote_copy(
                src_ref=src,
                dst_ref=dst,
                send_sem=sem,
                recv_sem=recv,
                device_id=(target, tp),
                device_id_type=pl.DeviceIdType.MESH,
            ).start()

    def finish_send(src, dst, sem, recv, target):
        @pl.when(target == me)
        def _():
            pltpu.make_async_copy(src, dst, sem).wait()

        @pl.when(target != me)
        def _():
            pltpu.make_async_remote_copy(
                src_ref=src,
                dst_ref=dst,
                send_sem=sem,
                recv_sem=recv,
                device_id=(target, tp),
                device_id_type=pl.DeviceIdType.MESH,
            ).wait_send()

    def finish_recv(src, dst, sem, recv, source):
        @pl.when(source != me)
        def _():
            pltpu.make_async_remote_copy(
                src_ref=src,
                dst_ref=dst,
                send_sem=sem,
                recv_sem=recv,
                device_id=(source, tp),
                device_id_type=pl.DeviceIdType.MESH,
            ).wait_recv()

    plan = []
    for h in range(heads):
        target = h * blocks + me // per
        plan.append((q_ref.at[h], q_out.at[me % per], q_send.at[h], q_recv.at[me % per], target))
        for r in range(tries):
            block = (me + back) // per - r
            slot = (me + back) % per + per * r
            plan.append(
                (
                    kv_ref.at[h],
                    kv_out.at[slot],
                    kv_send.at[h, r],
                    kv_recv.at[slot],
                    h * blocks + block,
                    (block >= 0) & (block < blocks),
                )
            )
    for item in plan:
        valid = item[5] if len(item) > 5 else True

        @pl.when(valid)
        def _():
            send(*item[:5])

    for item in plan:
        valid = item[5] if len(item) > 5 else True

        @pl.when(valid)
        def _():
            finish_send(*item[:5])

    for i in range(per):
        source = per * mine + i
        finish_recv(q_ref.at[0], q_out.at[i], q_send.at[0], q_recv.at[i], source)
    for slot in range(span):
        source = per * mine - back + slot

        @pl.when(source >= 0)
        def _():
            finish_recv(kv_ref.at[0], kv_out.at[slot], kv_send.at[0, 0], kv_recv.at[slot], source)


def spread(q, kv, blocks, per, back):
    heads = q.shape[0]
    span = back + per
    tries = back // per + 1
    return pl.pallas_call(
        functools.partial(spread_kernel, blocks, per, back),
        out_shape=(
            jax.ShapeDtypeStruct((per,) + q.shape[1:], q.dtype),
            jax.ShapeDtypeStruct((span,) + kv.shape[1:], kv.dtype),
        ),
        in_specs=[pl.BlockSpec(memory_space=pl.ANY)] * 2,
        out_specs=(pl.BlockSpec(memory_space=pl.ANY), pl.BlockSpec(memory_space=pl.ANY)),
        scratch_shapes=[
            pltpu.SemaphoreType.DMA((heads,)),
            pltpu.SemaphoreType.DMA((per,)),
            pltpu.SemaphoreType.DMA((heads, tries)),
            pltpu.SemaphoreType.DMA((span,)),
        ],
        compiler_params=pltpu.CompilerParams(has_side_effects=True),
    )(q, kv)


def gather_kernel(blocks, per, att_ref, out_ref, send_sem, recv_sem):
    me = lax.axis_index("seq")
    tp = lax.axis_index("tp")
    heads = out_ref.shape[0]
    head = me // blocks
    mine = me % blocks

    def copy(i, target):
        return pltpu.make_async_remote_copy(
            src_ref=att_ref.at[i],
            dst_ref=out_ref.at[head],
            send_sem=send_sem.at[i],
            recv_sem=recv_sem.at[head],
            device_id=(target, tp),
            device_id_type=pl.DeviceIdType.MESH,
        )

    for i in range(per):
        target = per * mine + i

        @pl.when(target == me)
        def _():
            pltpu.make_async_copy(att_ref.at[i], out_ref.at[head], send_sem.at[i]).start()

        @pl.when(target != me)
        def _():
            copy(i, target).start()

    for i in range(per):
        target = per * mine + i

        @pl.when(target == me)
        def _():
            pltpu.make_async_copy(att_ref.at[i], out_ref.at[head], send_sem.at[i]).wait()

        @pl.when(target != me)
        def _():
            copy(i, target).wait_send()

    for h in range(heads):
        source = h * blocks + me // per

        @pl.when(source != me)
        def _():
            pltpu.make_async_remote_copy(
                src_ref=att_ref.at[0],
                dst_ref=out_ref.at[h],
                send_sem=send_sem.at[0],
                recv_sem=recv_sem.at[h],
                device_id=(source, tp),
                device_id_type=pl.DeviceIdType.MESH,
            ).wait_recv()


def gather_back(att, heads, blocks):
    per = att.shape[0]
    return pl.pallas_call(
        functools.partial(gather_kernel, blocks, per),
        out_shape=jax.ShapeDtypeStruct((heads,) + att.shape[1:], att.dtype),
        in_specs=[pl.BlockSpec(memory_space=pl.ANY)],
        out_specs=pl.BlockSpec(memory_space=pl.ANY),
        scratch_shapes=[pltpu.SemaphoreType.DMA((per,)), pltpu.SemaphoreType.DMA((heads,))],
        compiler_params=pltpu.CompilerParams(has_side_effects=True),
    )(att)


def attend_kernel(
    blocks, per, back, scale, bounds_ref, q_ref, kv_ref, out_ref,
    q_in, kv_in, att, acc, top, total, kept,
    q_send, q_recv, kv_send, kv_recv, att_send, att_recv,
):
    me = lax.axis_index("seq")
    tp = lax.axis_index("tp")
    heads, rows, head_dim = q_ref.shape
    span = back + per
    tries = back // per + 1
    mine = me % blocks
    head = me // blocks

    def remote(src, dst, send, recv, device):
        return pltpu.make_async_remote_copy(
            src_ref=src, dst_ref=dst, send_sem=send, recv_sem=recv,
            device_id=(device, tp), device_id_type=pl.DeviceIdType.MESH,
        )

    plan = []
    for h in range(heads):
        target = h * blocks + me // per
        plan.append(
            (q_ref.at[h], q_in.at[me % per], q_send.at[h], q_recv.at[me % per], target, True)
        )
        for r in range(tries):
            block = (me + back) // per - r
            slot = (me + back) % per + per * r
            valid = (block >= 0) & (block < blocks)
            plan.append(
                (kv_ref.at[h], kv_in.at[slot], kv_send.at[h, r], kv_recv.at[slot],
                 h * blocks + block, valid)
            )
    for src, dst, send, recv, target, valid in plan:

        @pl.when(valid & (target == me))
        def _():
            pltpu.make_async_copy(src, dst, send).start()

        @pl.when(valid & (target != me))
        def _():
            remote(src, dst, send, recv, target).start()

    for src, dst, send, recv, target, valid in plan:

        @pl.when(valid & (target == me))
        def _():
            pltpu.make_async_copy(src, dst, send).wait()

    for i in range(per):
        source = per * mine + i

        @pl.when(source != me)
        def _():
            remote(q_ref.at[0], q_in.at[i], q_send.at[0], q_recv.at[i], source).wait_recv()

    query = q_in[...].reshape(per * rows, head_dim)
    query_pos = mine * per * rows + lax.broadcasted_iota(jnp.int32, (per * rows, 1), 0)
    first = jnp.zeros(query_pos.shape, jnp.int32)
    for k in range(bounds_ref.shape[0]):
        first = jnp.maximum(first, jnp.where(query_pos >= bounds_ref[k], bounds_ref[k], 0))

    top[...] = jnp.full(top.shape, -1e30, jnp.float32)
    total[...] = jnp.zeros(total.shape, jnp.float32)
    acc[...] = jnp.zeros(acc.shape, jnp.float32)

    def first_pass(slot, carry):
        source = per * mine - back + slot

        @pl.when(source >= 0)
        def _():
            @pl.when(source != me)
            def _():
                remote(
                    kv_ref.at[0], kv_in.at[slot], kv_send.at[0, 0], kv_recv.at[slot], source
                ).wait_recv()

            key_pos = source * rows + lax.broadcasted_iota(jnp.int32, (1, rows), 1)
            visible = (key_pos >= first) & (key_pos <= query_pos)
            scores = lax.dot_general(
                query, kv_in[slot, :, :head_dim], (((1,), (1,)), ((), ())),
                preferred_element_type=jnp.float32,
            ) * scale
            scores = jnp.where(visible, scores, -1e30)
            kept[slot] = scores
            top[...] = jnp.maximum(top[...], jnp.max(scores, axis=1, keepdims=True))

        return carry

    lax.fori_loop(0, span, first_pass, 0)

    def second_pass(slot, carry):
        source = per * mine - back + slot

        @pl.when(source >= 0)
        def _():
            weights = jnp.exp(kept[slot] - top[...])
            total[...] += jnp.sum(weights, axis=1, keepdims=True)
            acc[...] += jnp.dot(
                weights.astype(jnp.bfloat16), kv_in[slot, :, head_dim:],
                preferred_element_type=jnp.float32,
            )

        return carry

    lax.fori_loop(0, span, second_pass, 0)
    att[...] = (acc[...] / total[...]).astype(att.dtype).reshape(att.shape)

    for i in range(per):
        target = per * mine + i

        @pl.when(target == me)
        def _():
            pltpu.make_async_copy(att.at[i], out_ref.at[head], att_send.at[i]).start()

        @pl.when(target != me)
        def _():
            remote(att.at[i], out_ref.at[head], att_send.at[i], att_recv.at[head], target).start()

    for i in range(per):
        target = per * mine + i

        @pl.when(target == me)
        def _():
            pltpu.make_async_copy(att.at[i], out_ref.at[head], att_send.at[i]).wait()

        @pl.when(target != me)
        def _():
            remote(
                att.at[i], out_ref.at[head], att_send.at[i], att_recv.at[head], target
            ).wait_send()

    for h in range(heads):
        source = h * blocks + me // per

        @pl.when(source != me)
        def _():
            remote(att.at[0], out_ref.at[h], att_send.at[0], att_recv.at[h], source).wait_recv()

    for src, dst, send, recv, target, valid in plan:

        @pl.when(valid & (target != me))
        def _():
            remote(src, dst, send, recv, target).wait_send()


def attend(bounds, q, kv, blocks, back, scale):
    heads, rows, head_dim = q.shape
    per = heads
    span = back + per
    tries = back // per + 1
    return pl.pallas_call(
        functools.partial(attend_kernel, blocks, per, back, scale),
        out_shape=jax.ShapeDtypeStruct(q.shape, q.dtype),
        in_specs=[
            pl.BlockSpec(memory_space=pltpu.SMEM),
            pl.BlockSpec(memory_space=pl.ANY),
            pl.BlockSpec(memory_space=pl.ANY),
        ],
        out_specs=pl.BlockSpec(memory_space=pl.ANY),
        scratch_shapes=[
            pltpu.VMEM((per, rows, head_dim), q.dtype),
            pltpu.VMEM((span,) + kv.shape[1:], kv.dtype),
            pltpu.VMEM((per, rows, head_dim), q.dtype),
            pltpu.VMEM((per * rows, head_dim), jnp.float32),
            pltpu.VMEM((per * rows, 1), jnp.float32),
            pltpu.VMEM((per * rows, 1), jnp.float32),
            pltpu.VMEM((span, per * rows, rows), jnp.float32),
            pltpu.SemaphoreType.DMA((heads,)),
            pltpu.SemaphoreType.DMA((per,)),
            pltpu.SemaphoreType.DMA((heads, tries)),
            pltpu.SemaphoreType.DMA((span,)),
            pltpu.SemaphoreType.DMA((per,)),
            pltpu.SemaphoreType.DMA((heads,)),
        ],
        compiler_params=pltpu.CompilerParams(has_side_effects=True),
    )(bounds, q, kv)


def shards(
    queries, keys, values, lengths, resid, w_out, moe_gain, routes, gates, w_gate_up, w_down
):
    seq_count = lax.axis_size("seq")
    me = lax.axis_index("seq")
    query_rows = queries.shape[0]
    local_heads = queries.shape[1] // HEAD_DIM
    cols = queries.shape[1]
    width = resid.shape[1]
    score_scale = 1.0 / math.sqrt(HEAD_DIM)
    longest = (seq_count * query_rows) // 2
    reach = min(seq_count - 1, -(-(longest - 1) // query_rows))
    blocks = seq_count // local_heads
    per = seq_count // blocks
    back = -(-reach // per) * per
    span = back + per
    head_q = queries.reshape(query_rows, local_heads, HEAD_DIM).transpose(1, 0, 2)
    head_kv = jnp.concatenate(
        [
            keys.reshape(query_rows, local_heads, HEAD_DIM),
            values.reshape(query_rows, local_heads, HEAD_DIM),
        ],
        axis=2,
    ).transpose(1, 0, 2)
    far_swap = [(t, t ^ 2) for t in range(lax.axis_size("tp"))]
    far_resid, far_routes, far_gates, head_q, head_kv = lax.optimization_barrier(
        (
            lax.ppermute(resid, "tp", far_swap),
            lax.ppermute(routes, "tp", far_swap),
            lax.ppermute(gates, "tp", far_swap),
            head_q,
            head_kv,
        )
    )
    attention = (
        attend(
            jnp.cumsum(lengths).astype(jnp.int32), head_q, head_kv, blocks, back, score_scale
        )
        .transpose(1, 0, 2)
        .reshape(query_rows, local_heads * HEAD_DIM)
    )
    tp_index = lax.axis_index("tp")
    near_swap = [(t, t ^ 1) for t in range(lax.axis_size("tp"))]
    far_swap = [(t, t ^ 2) for t in range(lax.axis_size("tp"))]
    local_rows = resid.shape[0]
    partial_proj = jnp.dot(attention, w_out, preferred_element_type=jnp.float32).reshape(
        2, 2, local_rows, width
    )
    core = tp_index % 2
    keep = lax.dynamic_index_in_dim(partial_proj, core, axis=1, keepdims=False)
    give = lax.dynamic_index_in_dim(partial_proj, 1 - core, axis=1, keepdims=False)
    half = keep + lax.ppermute(give.astype(jnp.bfloat16), "tp", near_swap).astype(jnp.float32)
    far = tp_index // 2
    pair_resid = jnp.stack([resid, far_resid])
    pair_routes = jnp.stack([routes, far_routes])
    pair_gates = jnp.stack([gates, far_gates])
    half = half.astype(jnp.bfloat16)
    total = half.astype(jnp.float32) + lax.ppermute(half, "tp", far_swap).astype(jnp.float32)
    pair_proj = jnp.stack(
        [
            lax.dynamic_index_in_dim(total, far, axis=0, keepdims=False),
            lax.dynamic_index_in_dim(total, 1 - far, axis=0, keepdims=False),
        ]
    )
    pair_attended = (pair_resid.astype(jnp.float32) + pair_proj).astype(jnp.bfloat16)
    attended = pair_attended[0]
    widened = pair_attended.astype(jnp.float32)
    meansq = jnp.mean(widened * widened, axis=2, keepdims=True)
    pair_normed = (widened * lax.rsqrt(meansq + 1e-05) * moe_gain).astype(jnp.bfloat16)
    top_count = routes.shape[1]
    owned = w_gate_up.shape[0]
    experts_all = owned * seq_count
    capacity = 3 * local_rows * top_count // (2 * experts_all)
    matches = pair_routes[..., None] == jnp.arange(experts_all, dtype=jnp.int32)
    member = jnp.any(matches, axis=2)
    slot = jnp.cumsum(member.astype(jnp.int32), axis=1) - 1
    place = member[..., None] & (slot[..., None] == jnp.arange(capacity, dtype=jnp.int32))
    buffer = jnp.einsum(
        "xiec,xid->excd", place.astype(jnp.bfloat16), pair_normed,
        preferred_element_type=jnp.bfloat16,
    )
    buffer = buffer.reshape(seq_count, owned, 2, capacity, width).transpose(1, 0, 2, 3, 4)
    arrived = lax.all_to_all(buffer, "seq", split_axis=1, concat_axis=1, tiled=True)
    near = lax.ppermute(arrived, "tp", near_swap)

    def expert_part(slots):
        projections = jnp.einsum(
            "xnd,xdgf->xngf", slots.reshape(owned, -1, width), w_gate_up,
            preferred_element_type=jnp.float32,
        )
        hidden = (jax.nn.silu(projections[..., 0, :]) * projections[..., 1, :]).astype(
            jnp.bfloat16
        )
        return jnp.einsum(
            "xnf,xfd->xnd", hidden, w_down, preferred_element_type=jnp.float32
        ).astype(jnp.bfloat16)

    from_near = lax.ppermute(expert_part(near), "tp", near_swap)
    reduced = (
        expert_part(arrived).astype(jnp.float32) + from_near.astype(jnp.float32)
    ).astype(jnp.bfloat16)
    returned = lax.all_to_all(
        reduced.reshape(arrived.shape), "seq", split_axis=1, concat_axis=1, tiled=True
    )
    weight_of = jnp.sum(jnp.where(matches, pair_gates[..., None], 0.0), axis=2)
    mix_weights = jnp.where(place, weight_of[..., None], 0.0)
    mixes = jnp.einsum(
        "xiec,xecd->xid",
        mix_weights.astype(jnp.bfloat16),
        returned.transpose(2, 1, 0, 3, 4).reshape(2, experts_all, capacity, width),
        preferred_element_type=jnp.float32,
    )
    from_far = lax.ppermute(mixes[1].astype(jnp.bfloat16), "tp", far_swap)
    expert_mix = (mixes[0] + from_far.astype(jnp.float32)).astype(jnp.bfloat16)
    return (attended, expert_mix)


def solution(mesh):
    return jax.shard_map(
        shards,
        mesh=mesh,
        in_specs=(
            P("seq", "tp"),
            P("seq", "tp"),
            P("seq", "tp"),
            P(),
            P(("seq", "tp"), None),
            P("tp", None),
            P(),
            P(("seq", "tp"), None),
            P(("seq", "tp"), None),
            P("seq", None, None, "tp"),
            P("seq", "tp", None),
        ),
        out_specs=(P(("seq", "tp"), None), P(("seq", "tp"), None)),
        check_vma=False,
    )
```

```python
import functools
import math

import jax
import jax.numpy as jnp
from jax import lax
from jax.experimental import pallas as pl
from jax.experimental.pallas import tpu as pltpu
from jax.sharding import PartitionSpec as P

HEAD_DIM = 128


def tenant_of(positions, lengths):
    bounds = jnp.cumsum(lengths)
    return jnp.sum((positions[:, None] >= bounds[None, :]).astype(jnp.int32), axis=1)


def spread_kernel(
    blocks, per, back, q_ref, kv_ref, q_out, kv_out, q_send, q_recv, kv_send, kv_recv
):
    me = lax.axis_index("seq")
    tp = lax.axis_index("tp")
    heads = q_ref.shape[0]
    span = back + per
    tries = back // per + 1
    mine = me % blocks

    def send(src, dst, sem, recv, target):
        @pl.when(target == me)
        def _():
            pltpu.make_async_copy(src, dst, sem).start()

        @pl.when(target != me)
        def _():
            pltpu.make_async_remote_copy(
                src_ref=src,
                dst_ref=dst,
                send_sem=sem,
                recv_sem=recv,
                device_id=(target, tp),
                device_id_type=pl.DeviceIdType.MESH,
            ).start()

    def finish_send(src, dst, sem, recv, target):
        @pl.when(target == me)
        def _():
            pltpu.make_async_copy(src, dst, sem).wait()

        @pl.when(target != me)
        def _():
            pltpu.make_async_remote_copy(
                src_ref=src,
                dst_ref=dst,
                send_sem=sem,
                recv_sem=recv,
                device_id=(target, tp),
                device_id_type=pl.DeviceIdType.MESH,
            ).wait_send()

    def finish_recv(src, dst, sem, recv, source):
        @pl.when(source != me)
        def _():
            pltpu.make_async_remote_copy(
                src_ref=src,
                dst_ref=dst,
                send_sem=sem,
                recv_sem=recv,
                device_id=(source, tp),
                device_id_type=pl.DeviceIdType.MESH,
            ).wait_recv()

    plan = []
    for h in range(heads):
        target = h * blocks + me // per
        plan.append((q_ref.at[h], q_out.at[me % per], q_send.at[h], q_recv.at[me % per], target))
        for r in range(tries):
            block = (me + back) // per - r
            slot = (me + back) % per + per * r
            plan.append(
                (
                    kv_ref.at[h],
                    kv_out.at[slot],
                    kv_send.at[h, r],
                    kv_recv.at[slot],
                    h * blocks + block,
                    (block >= 0) & (block < blocks),
                )
            )
    for item in plan:
        valid = item[5] if len(item) > 5 else True

        @pl.when(valid)
        def _():
            send(*item[:5])

    for item in plan:
        valid = item[5] if len(item) > 5 else True

        @pl.when(valid)
        def _():
            finish_send(*item[:5])

    for i in range(per):
        source = per * mine + i
        finish_recv(q_ref.at[0], q_out.at[i], q_send.at[0], q_recv.at[i], source)
    for slot in range(span):
        source = per * mine - back + slot

        @pl.when(source >= 0)
        def _():
            finish_recv(kv_ref.at[0], kv_out.at[slot], kv_send.at[0, 0], kv_recv.at[slot], source)


def spread(q, kv, blocks, per, back):
    heads = q.shape[0]
    span = back + per
    tries = back // per + 1
    return pl.pallas_call(
        functools.partial(spread_kernel, blocks, per, back),
        out_shape=(
            jax.ShapeDtypeStruct((per,) + q.shape[1:], q.dtype),
            jax.ShapeDtypeStruct((span,) + kv.shape[1:], kv.dtype),
        ),
        in_specs=[pl.BlockSpec(memory_space=pl.ANY)] * 2,
        out_specs=(pl.BlockSpec(memory_space=pl.ANY), pl.BlockSpec(memory_space=pl.ANY)),
        scratch_shapes=[
            pltpu.SemaphoreType.DMA((heads,)),
            pltpu.SemaphoreType.DMA((per,)),
            pltpu.SemaphoreType.DMA((heads, tries)),
            pltpu.SemaphoreType.DMA((span,)),
        ],
        compiler_params=pltpu.CompilerParams(has_side_effects=True),
    )(q, kv)


def gather_kernel(blocks, per, att_ref, out_ref, send_sem, recv_sem):
    me = lax.axis_index("seq")
    tp = lax.axis_index("tp")
    heads = out_ref.shape[0]
    head = me // blocks
    mine = me % blocks

    def copy(i, target):
        return pltpu.make_async_remote_copy(
            src_ref=att_ref.at[i],
            dst_ref=out_ref.at[head],
            send_sem=send_sem.at[i],
            recv_sem=recv_sem.at[head],
            device_id=(target, tp),
            device_id_type=pl.DeviceIdType.MESH,
        )

    for i in range(per):
        target = per * mine + i

        @pl.when(target == me)
        def _():
            pltpu.make_async_copy(att_ref.at[i], out_ref.at[head], send_sem.at[i]).start()

        @pl.when(target != me)
        def _():
            copy(i, target).start()

    for i in range(per):
        target = per * mine + i

        @pl.when(target == me)
        def _():
            pltpu.make_async_copy(att_ref.at[i], out_ref.at[head], send_sem.at[i]).wait()

        @pl.when(target != me)
        def _():
            copy(i, target).wait_send()

    for h in range(heads):
        source = h * blocks + me // per

        @pl.when(source != me)
        def _():
            pltpu.make_async_remote_copy(
                src_ref=att_ref.at[0],
                dst_ref=out_ref.at[h],
                send_sem=send_sem.at[0],
                recv_sem=recv_sem.at[h],
                device_id=(source, tp),
                device_id_type=pl.DeviceIdType.MESH,
            ).wait_recv()


def gather_back(att, heads, blocks):
    per = att.shape[0]
    return pl.pallas_call(
        functools.partial(gather_kernel, blocks, per),
        out_shape=jax.ShapeDtypeStruct((heads,) + att.shape[1:], att.dtype),
        in_specs=[pl.BlockSpec(memory_space=pl.ANY)],
        out_specs=pl.BlockSpec(memory_space=pl.ANY),
        scratch_shapes=[pltpu.SemaphoreType.DMA((per,)), pltpu.SemaphoreType.DMA((heads,))],
        compiler_params=pltpu.CompilerParams(has_side_effects=True),
    )(att)


def attend_kernel(
    blocks, per, back, scale, bounds_ref, q_ref, kv_ref, out_ref,
    q_in, kv_in, att, acc, top, total, kept,
    q_send, q_recv, kv_send, kv_recv, att_send, att_recv,
):
    me = lax.axis_index("seq")
    tp = lax.axis_index("tp")
    heads, rows, head_dim = q_ref.shape
    span = back + per
    tries = back // per + 1
    mine = me % blocks
    head = me // blocks

    def remote(src, dst, send, recv, device):
        return pltpu.make_async_remote_copy(
            src_ref=src, dst_ref=dst, send_sem=send, recv_sem=recv,
            device_id=(device, tp), device_id_type=pl.DeviceIdType.MESH,
        )

    plan = []
    for h in range(heads):
        target = h * blocks + me // per
        plan.append(
            (q_ref.at[h], q_in.at[me % per], q_send.at[h], q_recv.at[me % per], target, True)
        )
        for r in range(tries):
            block = (me + back) // per - r
            slot = (me + back) % per + per * r
            valid = (block >= 0) & (block < blocks)
            plan.append(
                (kv_ref.at[h], kv_in.at[slot], kv_send.at[h, r], kv_recv.at[slot],
                 h * blocks + block, valid)
            )
    for src, dst, send, recv, target, valid in plan:

        @pl.when(valid & (target == me))
        def _():
            pltpu.make_async_copy(src, dst, send).start()

        @pl.when(valid & (target != me))
        def _():
            remote(src, dst, send, recv, target).start()

    for src, dst, send, recv, target, valid in plan:

        @pl.when(valid & (target == me))
        def _():
            pltpu.make_async_copy(src, dst, send).wait()

    for i in range(per):
        source = per * mine + i

        @pl.when(source != me)
        def _():
            remote(q_ref.at[0], q_in.at[i], q_send.at[0], q_recv.at[i], source).wait_recv()

    query = q_in[...].reshape(per * rows, head_dim)
    query_pos = mine * per * rows + lax.broadcasted_iota(jnp.int32, (per * rows, 1), 0)
    first = jnp.zeros(query_pos.shape, jnp.int32)
    for k in range(bounds_ref.shape[0]):
        first = jnp.maximum(first, jnp.where(query_pos >= bounds_ref[k], bounds_ref[k], 0))

    top[...] = jnp.full(top.shape, -1e30, jnp.float32)
    total[...] = jnp.zeros(total.shape, jnp.float32)
    acc[...] = jnp.zeros(acc.shape, jnp.float32)

    def first_pass(slot, carry):
        source = per * mine - back + slot

        @pl.when(source >= 0)
        def _():
            @pl.when(source != me)
            def _():
                remote(
                    kv_ref.at[0], kv_in.at[slot], kv_send.at[0, 0], kv_recv.at[slot], source
                ).wait_recv()

            key_pos = source * rows + lax.broadcasted_iota(jnp.int32, (1, rows), 1)
            visible = (key_pos >= first) & (key_pos <= query_pos)
            scores = lax.dot_general(
                query, kv_in[slot, :, :head_dim], (((1,), (1,)), ((), ())),
                preferred_element_type=jnp.float32,
            ) * scale
            scores = jnp.where(visible, scores, -1e30)
            kept[slot] = scores
            top[...] = jnp.maximum(top[...], jnp.max(scores, axis=1, keepdims=True))

        return carry

    lax.fori_loop(0, span, first_pass, 0)

    def second_pass(slot, carry):
        source = per * mine - back + slot

        @pl.when(source >= 0)
        def _():
            weights = jnp.exp(kept[slot] - top[...])
            total[...] += jnp.sum(weights, axis=1, keepdims=True)
            acc[...] += jnp.dot(
                weights.astype(jnp.bfloat16), kv_in[slot, :, head_dim:],
                preferred_element_type=jnp.float32,
            )

        return carry

    lax.fori_loop(0, span, second_pass, 0)
    att[...] = (acc[...] / total[...]).astype(att.dtype).reshape(att.shape)

    for i in range(per):
        target = per * mine + i

        @pl.when(target == me)
        def _():
            pltpu.make_async_copy(att.at[i], out_ref.at[head], att_send.at[i]).start()

        @pl.when(target != me)
        def _():
            remote(att.at[i], out_ref.at[head], att_send.at[i], att_recv.at[head], target).start()

    for i in range(per):
        target = per * mine + i

        @pl.when(target == me)
        def _():
            pltpu.make_async_copy(att.at[i], out_ref.at[head], att_send.at[i]).wait()

        @pl.when(target != me)
        def _():
            remote(
                att.at[i], out_ref.at[head], att_send.at[i], att_recv.at[head], target
            ).wait_send()

    for h in range(heads):
        source = h * blocks + me // per

        @pl.when(source != me)
        def _():
            remote(att.at[0], out_ref.at[h], att_send.at[0], att_recv.at[h], source).wait_recv()

    for src, dst, send, recv, target, valid in plan:

        @pl.when(valid & (target != me))
        def _():
            remote(src, dst, send, recv, target).wait_send()


def attend(bounds, q, kv, blocks, back, scale):
    heads, rows, head_dim = q.shape
    per = heads
    span = back + per
    tries = back // per + 1
    return pl.pallas_call(
        functools.partial(attend_kernel, blocks, per, back, scale),
        out_shape=jax.ShapeDtypeStruct(q.shape, q.dtype),
        in_specs=[
            pl.BlockSpec(memory_space=pltpu.SMEM),
            pl.BlockSpec(memory_space=pl.ANY),
            pl.BlockSpec(memory_space=pl.ANY),
        ],
        out_specs=pl.BlockSpec(memory_space=pl.ANY),
        scratch_shapes=[
            pltpu.VMEM((per, rows, head_dim), q.dtype),
            pltpu.VMEM((span,) + kv.shape[1:], kv.dtype),
            pltpu.VMEM((per, rows, head_dim), q.dtype),
            pltpu.VMEM((per * rows, head_dim), jnp.float32),
            pltpu.VMEM((per * rows, 1), jnp.float32),
            pltpu.VMEM((per * rows, 1), jnp.float32),
            pltpu.VMEM((span, per * rows, rows), jnp.float32),
            pltpu.SemaphoreType.DMA((heads,)),
            pltpu.SemaphoreType.DMA((per,)),
            pltpu.SemaphoreType.DMA((heads, tries)),
            pltpu.SemaphoreType.DMA((span,)),
            pltpu.SemaphoreType.DMA((per,)),
            pltpu.SemaphoreType.DMA((heads,)),
        ],
        compiler_params=pltpu.CompilerParams(has_side_effects=True),
    )(bounds, q, kv)


def shards(
    queries, keys, values, lengths, resid, w_out, moe_gain, routes, gates, w_gate_up, w_down
):
    seq_count = lax.axis_size("seq")
    me = lax.axis_index("seq")
    query_rows = queries.shape[0]
    local_heads = queries.shape[1] // HEAD_DIM
    cols = queries.shape[1]
    width = resid.shape[1]
    score_scale = 1.0 / math.sqrt(HEAD_DIM)
    longest = (seq_count * query_rows) // 2
    reach = min(seq_count - 1, -(-(longest - 1) // query_rows))
    blocks = seq_count // local_heads
    per = seq_count // blocks
    back = -(-reach // per) * per
    span = back + per
    head_q = queries.reshape(query_rows, local_heads, HEAD_DIM).transpose(1, 0, 2)
    head_kv = jnp.concatenate(
        [
            keys.reshape(query_rows, local_heads, HEAD_DIM),
            values.reshape(query_rows, local_heads, HEAD_DIM),
        ],
        axis=2,
    ).transpose(1, 0, 2)
    attention = (
        attend(
            jnp.cumsum(lengths).astype(jnp.int32), head_q, head_kv, blocks, back, score_scale
        )
        .transpose(1, 0, 2)
        .reshape(query_rows, local_heads * HEAD_DIM)
    )
    tp_index = lax.axis_index("tp")
    near_swap = [(t, t ^ 1) for t in range(lax.axis_size("tp"))]
    far_swap = [(t, t ^ 2) for t in range(lax.axis_size("tp"))]
    local_rows = resid.shape[0]
    partial_proj = jnp.dot(attention, w_out, preferred_element_type=jnp.float32).reshape(
        2, 2, local_rows, width
    )
    core = tp_index % 2
    keep = lax.dynamic_index_in_dim(partial_proj, core, axis=1, keepdims=False)
    give = lax.dynamic_index_in_dim(partial_proj, 1 - core, axis=1, keepdims=False)
    half = keep + lax.ppermute(give.astype(jnp.bfloat16), "tp", near_swap).astype(jnp.float32)
    far = tp_index // 2
    half = half.astype(jnp.bfloat16)
    extra = jnp.zeros((3 * local_rows, 128), jnp.bfloat16)
    extra = extra.at[2 * local_rows:, : routes.shape[1]].set(routes.astype(jnp.bfloat16))
    extra = extra.at[2 * local_rows:, routes.shape[1] : 2 * routes.shape[1]].set(
        gates.astype(jnp.bfloat16)
    )
    payload = jnp.concatenate(
        [jnp.concatenate([half.reshape(2 * local_rows, width), resid], axis=0), extra], axis=1
    )
    arrived_far = lax.ppermute(payload, "tp", far_swap)
    far_half = arrived_far[: 2 * local_rows, :width].reshape(half.shape)
    pair_resid = jnp.stack([resid, arrived_far[2 * local_rows :, :width]])
    far_tail = arrived_far[2 * local_rows :, width:]
    pair_routes = jnp.stack([routes, far_tail[:, : routes.shape[1]].astype(jnp.int32)])
    pair_gates = jnp.stack(
        [gates, far_tail[:, routes.shape[1] : 2 * routes.shape[1]].astype(jnp.float32)]
    )
    total = half.astype(jnp.float32) + far_half.astype(jnp.float32)
    pair_proj = jnp.stack(
        [
            lax.dynamic_index_in_dim(total, far, axis=0, keepdims=False),
            lax.dynamic_index_in_dim(total, 1 - far, axis=0, keepdims=False),
        ]
    )
    pair_attended = (pair_resid.astype(jnp.float32) + pair_proj).astype(jnp.bfloat16)
    attended = pair_attended[0]
    widened = pair_attended.astype(jnp.float32)
    meansq = jnp.mean(widened * widened, axis=2, keepdims=True)
    pair_normed = (widened * lax.rsqrt(meansq + 1e-05) * moe_gain).astype(jnp.bfloat16)
    top_count = routes.shape[1]
    owned = w_gate_up.shape[0]
    experts_all = owned * seq_count
    capacity = 3 * local_rows * top_count // (2 * experts_all)
    matches = pair_routes[..., None] == jnp.arange(experts_all, dtype=jnp.int32)
    member = jnp.any(matches, axis=2)
    slot = jnp.cumsum(member.astype(jnp.int32), axis=1) - 1
    place = member[..., None] & (slot[..., None] == jnp.arange(capacity, dtype=jnp.int32))
    buffer = jnp.einsum(
        "xiec,xid->excd", place.astype(jnp.bfloat16), pair_normed,
        preferred_element_type=jnp.float32,
    ).astype(jnp.bfloat16)
    buffer = buffer.reshape(seq_count, owned, 2, capacity, width).transpose(1, 0, 2, 3, 4)
    arrived = lax.all_to_all(buffer, "seq", split_axis=1, concat_axis=1, tiled=True)
    near = lax.ppermute(arrived, "tp", near_swap)

    def expert_part(slots):
        projections = jnp.einsum(
            "xnd,xdgf->xngf", slots.reshape(owned, -1, width), w_gate_up,
            preferred_element_type=jnp.float32,
        )
        hidden = (jax.nn.silu(projections[..., 0, :]) * projections[..., 1, :]).astype(
            jnp.bfloat16
        )
        return jnp.einsum(
            "xnf,xfd->xnd", hidden, w_down, preferred_element_type=jnp.float32
        ).astype(jnp.bfloat16)

    from_near = lax.ppermute(expert_part(near), "tp", near_swap)
    reduced = (
        expert_part(arrived).astype(jnp.float32) + from_near.astype(jnp.float32)
    ).astype(jnp.bfloat16)
    returned = lax.all_to_all(
        reduced.reshape(arrived.shape), "seq", split_axis=1, concat_axis=1, tiled=True
    )
    weight_of = jnp.sum(jnp.where(matches, pair_gates[..., None], 0.0), axis=2)
    mix_weights = jnp.where(place, weight_of[..., None], 0.0)
    mixes = jnp.einsum(
        "xiec,xecd->xid",
        mix_weights.astype(jnp.bfloat16),
        returned.transpose(2, 1, 0, 3, 4).reshape(2, experts_all, capacity, width),
        preferred_element_type=jnp.float32,
    )
    from_far = lax.ppermute(mixes[1].astype(jnp.bfloat16), "tp", far_swap)
    expert_mix = (mixes[0] + from_far.astype(jnp.float32)).astype(jnp.bfloat16)
    return (attended, expert_mix)


def solution(mesh):
    return jax.shard_map(
        shards,
        mesh=mesh,
        in_specs=(
            P("seq", "tp"),
            P("seq", "tp"),
            P("seq", "tp"),
            P(),
            P(("seq", "tp"), None),
            P("tp", None),
            P(),
            P(("seq", "tp"), None),
            P(("seq", "tp"), None),
            P("seq", None, None, "tp"),
            P("seq", "tp", None),
        ),
        out_specs=(P(("seq", "tp"), None), P(("seq", "tp"), None)),
        check_vma=False,
    )
```

```python
import functools
import math

import jax
import jax.numpy as jnp
from jax import lax
from jax.experimental import pallas as pl
from jax.experimental.pallas import tpu as pltpu
from jax.sharding import PartitionSpec as P

HEAD_DIM = 128


def tenant_of(positions, lengths):
    bounds = jnp.cumsum(lengths)
    return jnp.sum((positions[:, None] >= bounds[None, :]).astype(jnp.int32), axis=1)


def spread_kernel(
    blocks, per, back, q_ref, kv_ref, q_out, kv_out, q_send, q_recv, kv_send, kv_recv
):
    me = lax.axis_index("seq")
    tp = lax.axis_index("tp")
    heads = q_ref.shape[0]
    span = back + per
    tries = back // per + 1
    mine = me % blocks

    def send(src, dst, sem, recv, target):
        @pl.when(target == me)
        def _():
            pltpu.make_async_copy(src, dst, sem).start()

        @pl.when(target != me)
        def _():
            pltpu.make_async_remote_copy(
                src_ref=src,
                dst_ref=dst,
                send_sem=sem,
                recv_sem=recv,
                device_id=(target, tp),
                device_id_type=pl.DeviceIdType.MESH,
            ).start()

    def finish_send(src, dst, sem, recv, target):
        @pl.when(target == me)
        def _():
            pltpu.make_async_copy(src, dst, sem).wait()

        @pl.when(target != me)
        def _():
            pltpu.make_async_remote_copy(
                src_ref=src,
                dst_ref=dst,
                send_sem=sem,
                recv_sem=recv,
                device_id=(target, tp),
                device_id_type=pl.DeviceIdType.MESH,
            ).wait_send()

    def finish_recv(src, dst, sem, recv, source):
        @pl.when(source != me)
        def _():
            pltpu.make_async_remote_copy(
                src_ref=src,
                dst_ref=dst,
                send_sem=sem,
                recv_sem=recv,
                device_id=(source, tp),
                device_id_type=pl.DeviceIdType.MESH,
            ).wait_recv()

    plan = []
    for h in range(heads):
        target = h * blocks + me // per
        plan.append((q_ref.at[h], q_out.at[me % per], q_send.at[h], q_recv.at[me % per], target))
        for r in range(tries):
            block = (me + back) // per - r
            slot = (me + back) % per + per * r
            plan.append(
                (
                    kv_ref.at[h],
                    kv_out.at[slot],
                    kv_send.at[h, r],
                    kv_recv.at[slot],
                    h * blocks + block,
                    (block >= 0) & (block < blocks),
                )
            )
    for item in plan:
        valid = item[5] if len(item) > 5 else True

        @pl.when(valid)
        def _():
            send(*item[:5])

    for item in plan:
        valid = item[5] if len(item) > 5 else True

        @pl.when(valid)
        def _():
            finish_send(*item[:5])

    for i in range(per):
        source = per * mine + i
        finish_recv(q_ref.at[0], q_out.at[i], q_send.at[0], q_recv.at[i], source)
    for slot in range(span):
        source = per * mine - back + slot

        @pl.when(source >= 0)
        def _():
            finish_recv(kv_ref.at[0], kv_out.at[slot], kv_send.at[0, 0], kv_recv.at[slot], source)


def spread(q, kv, blocks, per, back):
    heads = q.shape[0]
    span = back + per
    tries = back // per + 1
    return pl.pallas_call(
        functools.partial(spread_kernel, blocks, per, back),
        out_shape=(
            jax.ShapeDtypeStruct((per,) + q.shape[1:], q.dtype),
            jax.ShapeDtypeStruct((span,) + kv.shape[1:], kv.dtype),
        ),
        in_specs=[pl.BlockSpec(memory_space=pl.ANY)] * 2,
        out_specs=(pl.BlockSpec(memory_space=pl.ANY), pl.BlockSpec(memory_space=pl.ANY)),
        scratch_shapes=[
            pltpu.SemaphoreType.DMA((heads,)),
            pltpu.SemaphoreType.DMA((per,)),
            pltpu.SemaphoreType.DMA((heads, tries)),
            pltpu.SemaphoreType.DMA((span,)),
        ],
        compiler_params=pltpu.CompilerParams(has_side_effects=True),
    )(q, kv)


def gather_kernel(blocks, per, att_ref, out_ref, send_sem, recv_sem):
    me = lax.axis_index("seq")
    tp = lax.axis_index("tp")
    heads = out_ref.shape[0]
    head = me // blocks
    mine = me % blocks

    def copy(i, target):
        return pltpu.make_async_remote_copy(
            src_ref=att_ref.at[i],
            dst_ref=out_ref.at[head],
            send_sem=send_sem.at[i],
            recv_sem=recv_sem.at[head],
            device_id=(target, tp),
            device_id_type=pl.DeviceIdType.MESH,
        )

    for i in range(per):
        target = per * mine + i

        @pl.when(target == me)
        def _():
            pltpu.make_async_copy(att_ref.at[i], out_ref.at[head], send_sem.at[i]).start()

        @pl.when(target != me)
        def _():
            copy(i, target).start()

    for i in range(per):
        target = per * mine + i

        @pl.when(target == me)
        def _():
            pltpu.make_async_copy(att_ref.at[i], out_ref.at[head], send_sem.at[i]).wait()

        @pl.when(target != me)
        def _():
            copy(i, target).wait_send()

    for h in range(heads):
        source = h * blocks + me // per

        @pl.when(source != me)
        def _():
            pltpu.make_async_remote_copy(
                src_ref=att_ref.at[0],
                dst_ref=out_ref.at[h],
                send_sem=send_sem.at[0],
                recv_sem=recv_sem.at[h],
                device_id=(source, tp),
                device_id_type=pl.DeviceIdType.MESH,
            ).wait_recv()


def gather_back(att, heads, blocks):
    per = att.shape[0]
    return pl.pallas_call(
        functools.partial(gather_kernel, blocks, per),
        out_shape=jax.ShapeDtypeStruct((heads,) + att.shape[1:], att.dtype),
        in_specs=[pl.BlockSpec(memory_space=pl.ANY)],
        out_specs=pl.BlockSpec(memory_space=pl.ANY),
        scratch_shapes=[pltpu.SemaphoreType.DMA((per,)), pltpu.SemaphoreType.DMA((heads,))],
        compiler_params=pltpu.CompilerParams(has_side_effects=True),
    )(att)


def attend_kernel(
    blocks, per, back, scale, bounds_ref, q_ref, kv_ref, out_ref,
    q_in, kv_in, att, acc, top, total, kept,
    q_send, q_recv, kv_send, kv_recv, att_send, att_recv,
):
    me = lax.axis_index("seq")
    tp = lax.axis_index("tp")
    heads, rows, head_dim = q_ref.shape
    span = back + per
    tries = back // per + 1
    mine = me % blocks
    head = me // blocks

    def remote(src, dst, send, recv, device):
        return pltpu.make_async_remote_copy(
            src_ref=src, dst_ref=dst, send_sem=send, recv_sem=recv,
            device_id=(device, tp), device_id_type=pl.DeviceIdType.MESH,
        )

    plan = []
    for h in range(heads):
        target = h * blocks + me // per
        plan.append(
            (q_ref.at[h], q_in.at[me % per], q_send.at[h], q_recv.at[me % per], target, True)
        )
        for r in range(tries):
            block = (me + back) // per - r
            slot = (me + back) % per + per * r
            valid = (block >= 0) & (block < blocks)
            plan.append(
                (kv_ref.at[h], kv_in.at[slot], kv_send.at[h, r], kv_recv.at[slot],
                 h * blocks + block, valid)
            )
    for src, dst, send, recv, target, valid in plan:

        @pl.when(valid & (target == me))
        def _():
            pltpu.make_async_copy(src, dst, send).start()

        @pl.when(valid & (target != me))
        def _():
            remote(src, dst, send, recv, target).start()

    for src, dst, send, recv, target, valid in plan:

        @pl.when(valid & (target == me))
        def _():
            pltpu.make_async_copy(src, dst, send).wait()

    for i in range(per):
        source = per * mine + i

        @pl.when(source != me)
        def _():
            remote(q_ref.at[0], q_in.at[i], q_send.at[0], q_recv.at[i], source).wait_recv()

    query = q_in[...].reshape(per * rows, head_dim)
    query_pos = mine * per * rows + lax.broadcasted_iota(jnp.int32, (per * rows, 1), 0)
    first = jnp.zeros(query_pos.shape, jnp.int32)
    for k in range(bounds_ref.shape[0]):
        first = jnp.maximum(first, jnp.where(query_pos >= bounds_ref[k], bounds_ref[k], 0))

    top[...] = jnp.full(top.shape, -1e30, jnp.float32)
    total[...] = jnp.zeros(total.shape, jnp.float32)
    acc[...] = jnp.zeros(acc.shape, jnp.float32)

    def first_pass(slot, carry):
        source = per * mine - back + slot

        @pl.when(source >= 0)
        def _():
            @pl.when(source != me)
            def _():
                remote(
                    kv_ref.at[0], kv_in.at[slot], kv_send.at[0, 0], kv_recv.at[slot], source
                ).wait_recv()

            key_pos = source * rows + lax.broadcasted_iota(jnp.int32, (1, rows), 1)
            visible = (key_pos >= first) & (key_pos <= query_pos)
            scores = lax.dot_general(
                query, kv_in[slot, :, :head_dim], (((1,), (1,)), ((), ())),
                preferred_element_type=jnp.float32,
            ) * scale
            scores = jnp.where(visible, scores, -1e30)
            kept[slot] = scores
            top[...] = jnp.maximum(top[...], jnp.max(scores, axis=1, keepdims=True))

        return carry

    lax.fori_loop(0, span, first_pass, 0)

    def second_pass(slot, carry):
        source = per * mine - back + slot

        @pl.when(source >= 0)
        def _():
            weights = jnp.exp(kept[slot] - top[...])
            total[...] += jnp.sum(weights, axis=1, keepdims=True)
            acc[...] += jnp.dot(
                weights.astype(jnp.bfloat16), kv_in[slot, :, head_dim:],
                preferred_element_type=jnp.float32,
            )

        return carry

    lax.fori_loop(0, span, second_pass, 0)
    att[...] = (acc[...] / total[...]).astype(att.dtype).reshape(att.shape)

    for i in range(per):
        target = per * mine + i

        @pl.when(target == me)
        def _():
            pltpu.make_async_copy(att.at[i], out_ref.at[head], att_send.at[i]).start()

        @pl.when(target != me)
        def _():
            remote(att.at[i], out_ref.at[head], att_send.at[i], att_recv.at[head], target).start()

    for i in range(per):
        target = per * mine + i

        @pl.when(target == me)
        def _():
            pltpu.make_async_copy(att.at[i], out_ref.at[head], att_send.at[i]).wait()

        @pl.when(target != me)
        def _():
            remote(
                att.at[i], out_ref.at[head], att_send.at[i], att_recv.at[head], target
            ).wait_send()

    for h in range(heads):
        source = h * blocks + me // per

        @pl.when(source != me)
        def _():
            remote(att.at[0], out_ref.at[h], att_send.at[0], att_recv.at[h], source).wait_recv()

    for src, dst, send, recv, target, valid in plan:

        @pl.when(valid & (target != me))
        def _():
            remote(src, dst, send, recv, target).wait_send()


def attend(bounds, q, kv, blocks, back, scale):
    heads, rows, head_dim = q.shape
    per = heads
    span = back + per
    tries = back // per + 1
    return pl.pallas_call(
        functools.partial(attend_kernel, blocks, per, back, scale),
        out_shape=jax.ShapeDtypeStruct(q.shape, q.dtype),
        in_specs=[
            pl.BlockSpec(memory_space=pltpu.SMEM),
            pl.BlockSpec(memory_space=pl.ANY),
            pl.BlockSpec(memory_space=pl.ANY),
        ],
        out_specs=pl.BlockSpec(memory_space=pl.ANY),
        scratch_shapes=[
            pltpu.VMEM((per, rows, head_dim), q.dtype),
            pltpu.VMEM((span,) + kv.shape[1:], kv.dtype),
            pltpu.VMEM((per, rows, head_dim), q.dtype),
            pltpu.VMEM((per * rows, head_dim), jnp.float32),
            pltpu.VMEM((per * rows, 1), jnp.float32),
            pltpu.VMEM((per * rows, 1), jnp.float32),
            pltpu.VMEM((span, per * rows, rows), jnp.float32),
            pltpu.SemaphoreType.DMA((heads,)),
            pltpu.SemaphoreType.DMA((per,)),
            pltpu.SemaphoreType.DMA((heads, tries)),
            pltpu.SemaphoreType.DMA((span,)),
            pltpu.SemaphoreType.DMA((per,)),
            pltpu.SemaphoreType.DMA((heads,)),
        ],
        compiler_params=pltpu.CompilerParams(has_side_effects=True),
    )(bounds, q, kv)


def shards(
    queries, keys, values, lengths, resid, w_out, moe_gain, routes, gates, w_gate_up, w_down
):
    seq_count = lax.axis_size("seq")
    me = lax.axis_index("seq")
    query_rows = queries.shape[0]
    local_heads = queries.shape[1] // HEAD_DIM
    cols = queries.shape[1]
    width = resid.shape[1]
    score_scale = 1.0 / math.sqrt(HEAD_DIM)
    longest = (seq_count * query_rows) // 2
    reach = min(seq_count - 1, -(-(longest - 1) // query_rows))
    blocks = seq_count // local_heads
    per = seq_count // blocks
    back = -(-reach // per) * per
    span = back + per
    head_q = queries.reshape(query_rows, local_heads, HEAD_DIM).transpose(1, 0, 2)
    head_kv = jnp.concatenate(
        [
            keys.reshape(query_rows, local_heads, HEAD_DIM),
            values.reshape(query_rows, local_heads, HEAD_DIM),
        ],
        axis=2,
    ).transpose(1, 0, 2)
    attention = (
        attend(
            jnp.cumsum(lengths).astype(jnp.int32), head_q, head_kv, blocks, back, score_scale
        )
        .transpose(1, 0, 2)
        .reshape(query_rows, local_heads * HEAD_DIM)
    )
    tp_index = lax.axis_index("tp")
    near_swap = [(t, t ^ 1) for t in range(lax.axis_size("tp"))]
    far_swap = [(t, t ^ 2) for t in range(lax.axis_size("tp"))]
    local_rows = resid.shape[0]
    partial_proj = jnp.dot(attention, w_out, preferred_element_type=jnp.float32).reshape(
        2, 2, local_rows, width
    )
    core = tp_index % 2
    keep = lax.dynamic_index_in_dim(partial_proj, core, axis=1, keepdims=False)
    give = lax.dynamic_index_in_dim(partial_proj, 1 - core, axis=1, keepdims=False)
    half = keep + lax.ppermute(give.astype(jnp.bfloat16), "tp", near_swap).astype(jnp.float32)
    far = tp_index // 2
    pair_resid = jnp.stack([resid, lax.ppermute(resid, "tp", far_swap)])
    pair_routes = jnp.stack([routes, lax.ppermute(routes, "tp", far_swap)])
    pair_gates = jnp.stack([gates, lax.ppermute(gates, "tp", far_swap)])
    half = half.astype(jnp.bfloat16)
    total = half.astype(jnp.float32) + lax.ppermute(half, "tp", far_swap).astype(jnp.float32)
    pair_proj = jnp.stack(
        [
            lax.dynamic_index_in_dim(total, far, axis=0, keepdims=False),
            lax.dynamic_index_in_dim(total, 1 - far, axis=0, keepdims=False),
        ]
    )
    pair_attended = (pair_resid.astype(jnp.float32) + pair_proj).astype(jnp.bfloat16)
    attended = pair_attended[0]
    widened = pair_attended.astype(jnp.float32)
    meansq = jnp.mean(widened * widened, axis=2, keepdims=True)
    pair_normed = (widened * lax.rsqrt(meansq + 1e-05) * moe_gain).astype(jnp.bfloat16)
    top_count = routes.shape[1]
    owned = w_gate_up.shape[0]
    experts_all = owned * seq_count
    capacity = 3 * local_rows * top_count // (2 * experts_all)
    matches = pair_routes[..., None] == jnp.arange(experts_all, dtype=jnp.int32)
    member = jnp.any(matches, axis=2)
    slot = jnp.cumsum(member.astype(jnp.int32), axis=1) - 1
    place = member[..., None] & (slot[..., None] == jnp.arange(capacity, dtype=jnp.int32))
    buffer = jnp.einsum(
        "xiec,xid->excd", place.astype(jnp.bfloat16), pair_normed,
        preferred_element_type=jnp.float32,
    ).astype(jnp.bfloat16)
    buffer = buffer.reshape(seq_count, owned, 2, capacity, width).transpose(1, 0, 2, 3, 4)
    arrived = lax.all_to_all(buffer, "seq", split_axis=1, concat_axis=1, tiled=True)
    near = lax.ppermute(arrived, "tp", near_swap)

    def expert_part(slots):
        projections = jnp.einsum(
            "xnd,xdgf->xngf", slots.reshape(owned, -1, width), w_gate_up,
            preferred_element_type=jnp.float32,
        )
        hidden = (jax.nn.silu(projections[..., 0, :]) * projections[..., 1, :]).astype(
            jnp.bfloat16
        )
        return jnp.einsum(
            "xnf,xfd->xnd", hidden, w_down, preferred_element_type=jnp.float32
        ).astype(jnp.bfloat16)

    own_part, near = lax.optimization_barrier((expert_part(arrived), near))
    from_near = lax.ppermute(expert_part(near), "tp", near_swap)
    reduced = (own_part.astype(jnp.float32) + from_near.astype(jnp.float32)).astype(
        jnp.bfloat16
    )
    returned = lax.all_to_all(
        reduced.reshape(arrived.shape), "seq", split_axis=1, concat_axis=1, tiled=True
    )
    weight_of = jnp.sum(jnp.where(matches, pair_gates[..., None], 0.0), axis=2)
    mix_weights = jnp.where(place, weight_of[..., None], 0.0)
    mixes = jnp.einsum(
        "xiec,xecd->xid",
        mix_weights.astype(jnp.bfloat16),
        returned.transpose(2, 1, 0, 3, 4).reshape(2, experts_all, capacity, width),
        preferred_element_type=jnp.float32,
    )
    from_far = lax.ppermute(mixes[1].astype(jnp.bfloat16), "tp", far_swap)
    expert_mix = (mixes[0] + from_far.astype(jnp.float32)).astype(jnp.bfloat16)
    return (attended, expert_mix)


def solution(mesh):
    return jax.shard_map(
        shards,
        mesh=mesh,
        in_specs=(
            P("seq", "tp"),
            P("seq", "tp"),
            P("seq", "tp"),
            P(),
            P(("seq", "tp"), None),
            P("tp", None),
            P(),
            P(("seq", "tp"), None),
            P(("seq", "tp"), None),
            P("seq", None, None, "tp"),
            P("seq", "tp", None),
        ),
        out_specs=(P(("seq", "tp"), None), P(("seq", "tp"), None)),
        check_vma=False,
    )
```

```python
import functools
import math

import jax
import jax.numpy as jnp
from jax import lax
from jax.experimental import pallas as pl
from jax.experimental.pallas import tpu as pltpu
from jax.sharding import PartitionSpec as P

HEAD_DIM = 128


def tenant_of(positions, lengths):
    bounds = jnp.cumsum(lengths)
    return jnp.sum((positions[:, None] >= bounds[None, :]).astype(jnp.int32), axis=1)


def spread_kernel(
    blocks, per, back, q_ref, kv_ref, q_out, kv_out, q_send, q_recv, kv_send, kv_recv
):
    me = lax.axis_index("seq")
    tp = lax.axis_index("tp")
    heads = q_ref.shape[0]
    span = back + per
    tries = back // per + 1
    mine = me % blocks

    def send(src, dst, sem, recv, target):
        @pl.when(target == me)
        def _():
            pltpu.make_async_copy(src, dst, sem).start()

        @pl.when(target != me)
        def _():
            pltpu.make_async_remote_copy(
                src_ref=src,
                dst_ref=dst,
                send_sem=sem,
                recv_sem=recv,
                device_id=(target, tp),
                device_id_type=pl.DeviceIdType.MESH,
            ).start()

    def finish_send(src, dst, sem, recv, target):
        @pl.when(target == me)
        def _():
            pltpu.make_async_copy(src, dst, sem).wait()

        @pl.when(target != me)
        def _():
            pltpu.make_async_remote_copy(
                src_ref=src,
                dst_ref=dst,
                send_sem=sem,
                recv_sem=recv,
                device_id=(target, tp),
                device_id_type=pl.DeviceIdType.MESH,
            ).wait_send()

    def finish_recv(src, dst, sem, recv, source):
        @pl.when(source != me)
        def _():
            pltpu.make_async_remote_copy(
                src_ref=src,
                dst_ref=dst,
                send_sem=sem,
                recv_sem=recv,
                device_id=(source, tp),
                device_id_type=pl.DeviceIdType.MESH,
            ).wait_recv()

    plan = []
    for h in range(heads):
        target = h * blocks + me // per
        plan.append((q_ref.at[h], q_out.at[me % per], q_send.at[h], q_recv.at[me % per], target))
        for r in range(tries):
            block = (me + back) // per - r
            slot = (me + back) % per + per * r
            plan.append(
                (
                    kv_ref.at[h],
                    kv_out.at[slot],
                    kv_send.at[h, r],
                    kv_recv.at[slot],
                    h * blocks + block,
                    (block >= 0) & (block < blocks),
                )
            )
    for item in plan:
        valid = item[5] if len(item) > 5 else True

        @pl.when(valid)
        def _():
            send(*item[:5])

    for item in plan:
        valid = item[5] if len(item) > 5 else True

        @pl.when(valid)
        def _():
            finish_send(*item[:5])

    for i in range(per):
        source = per * mine + i
        finish_recv(q_ref.at[0], q_out.at[i], q_send.at[0], q_recv.at[i], source)
    for slot in range(span):
        source = per * mine - back + slot

        @pl.when(source >= 0)
        def _():
            finish_recv(kv_ref.at[0], kv_out.at[slot], kv_send.at[0, 0], kv_recv.at[slot], source)


def spread(q, kv, blocks, per, back):
    heads = q.shape[0]
    span = back + per
    tries = back // per + 1
    return pl.pallas_call(
        functools.partial(spread_kernel, blocks, per, back),
        out_shape=(
            jax.ShapeDtypeStruct((per,) + q.shape[1:], q.dtype),
            jax.ShapeDtypeStruct((span,) + kv.shape[1:], kv.dtype),
        ),
        in_specs=[pl.BlockSpec(memory_space=pl.ANY)] * 2,
        out_specs=(pl.BlockSpec(memory_space=pl.ANY), pl.BlockSpec(memory_space=pl.ANY)),
        scratch_shapes=[
            pltpu.SemaphoreType.DMA((heads,)),
            pltpu.SemaphoreType.DMA((per,)),
            pltpu.SemaphoreType.DMA((heads, tries)),
            pltpu.SemaphoreType.DMA((span,)),
        ],
        compiler_params=pltpu.CompilerParams(has_side_effects=True),
    )(q, kv)


def gather_kernel(blocks, per, att_ref, out_ref, send_sem, recv_sem):
    me = lax.axis_index("seq")
    tp = lax.axis_index("tp")
    heads = out_ref.shape[0]
    head = me // blocks
    mine = me % blocks

    def copy(i, target):
        return pltpu.make_async_remote_copy(
            src_ref=att_ref.at[i],
            dst_ref=out_ref.at[head],
            send_sem=send_sem.at[i],
            recv_sem=recv_sem.at[head],
            device_id=(target, tp),
            device_id_type=pl.DeviceIdType.MESH,
        )

    for i in range(per):
        target = per * mine + i

        @pl.when(target == me)
        def _():
            pltpu.make_async_copy(att_ref.at[i], out_ref.at[head], send_sem.at[i]).start()

        @pl.when(target != me)
        def _():
            copy(i, target).start()

    for i in range(per):
        target = per * mine + i

        @pl.when(target == me)
        def _():
            pltpu.make_async_copy(att_ref.at[i], out_ref.at[head], send_sem.at[i]).wait()

        @pl.when(target != me)
        def _():
            copy(i, target).wait_send()

    for h in range(heads):
        source = h * blocks + me // per

        @pl.when(source != me)
        def _():
            pltpu.make_async_remote_copy(
                src_ref=att_ref.at[0],
                dst_ref=out_ref.at[h],
                send_sem=send_sem.at[0],
                recv_sem=recv_sem.at[h],
                device_id=(source, tp),
                device_id_type=pl.DeviceIdType.MESH,
            ).wait_recv()


def gather_back(att, heads, blocks):
    per = att.shape[0]
    return pl.pallas_call(
        functools.partial(gather_kernel, blocks, per),
        out_shape=jax.ShapeDtypeStruct((heads,) + att.shape[1:], att.dtype),
        in_specs=[pl.BlockSpec(memory_space=pl.ANY)],
        out_specs=pl.BlockSpec(memory_space=pl.ANY),
        scratch_shapes=[pltpu.SemaphoreType.DMA((per,)), pltpu.SemaphoreType.DMA((heads,))],
        compiler_params=pltpu.CompilerParams(has_side_effects=True),
    )(att)


def attend_kernel(
    blocks, per, back, scale, bounds_ref, q_ref, kv_ref, out_ref,
    q_in, kv_in, att, acc, top, total, kept,
    q_send, q_recv, kv_send, kv_recv, att_send, att_recv,
):
    me = lax.axis_index("seq")
    tp = lax.axis_index("tp")
    heads, rows, head_dim = q_ref.shape
    span = back + per
    tries = back // per + 1
    mine = me % blocks
    head = me // blocks

    def remote(src, dst, send, recv, device):
        return pltpu.make_async_remote_copy(
            src_ref=src, dst_ref=dst, send_sem=send, recv_sem=recv,
            device_id=(device, tp), device_id_type=pl.DeviceIdType.MESH,
        )

    plan = []
    for h in range(heads):
        target = h * blocks + me // per
        plan.append(
            (q_ref.at[h], q_in.at[me % per], q_send.at[h], q_recv.at[me % per], target, True)
        )
        for r in range(tries):
            block = (me + back) // per - r
            slot = (me + back) % per + per * r
            valid = (block >= 0) & (block < blocks)
            plan.append(
                (kv_ref.at[h], kv_in.at[slot], kv_send.at[h, r], kv_recv.at[slot],
                 h * blocks + block, valid)
            )
    for src, dst, send, recv, target, valid in plan:

        @pl.when(valid & (target == me))
        def _():
            pltpu.make_async_copy(src, dst, send).start()

        @pl.when(valid & (target != me))
        def _():
            remote(src, dst, send, recv, target).start()

    for src, dst, send, recv, target, valid in plan:

        @pl.when(valid & (target == me))
        def _():
            pltpu.make_async_copy(src, dst, send).wait()

    for i in range(per):
        source = per * mine + i

        @pl.when(source != me)
        def _():
            remote(q_ref.at[0], q_in.at[i], q_send.at[0], q_recv.at[i], source).wait_recv()

    query = q_in[...].reshape(per * rows, head_dim)
    query_pos = mine * per * rows + lax.broadcasted_iota(jnp.int32, (per * rows, 1), 0)
    first = jnp.zeros(query_pos.shape, jnp.int32)
    for k in range(bounds_ref.shape[0]):
        first = jnp.maximum(first, jnp.where(query_pos >= bounds_ref[k], bounds_ref[k], 0))

    top[...] = jnp.full(top.shape, -1e30, jnp.float32)
    total[...] = jnp.zeros(total.shape, jnp.float32)
    acc[...] = jnp.zeros(acc.shape, jnp.float32)

    def first_pass(slot, carry):
        source = per * mine - back + slot

        @pl.when(source >= 0)
        def _():
            @pl.when(source != me)
            def _():
                remote(
                    kv_ref.at[0], kv_in.at[slot], kv_send.at[0, 0], kv_recv.at[slot], source
                ).wait_recv()

            key_pos = source * rows + lax.broadcasted_iota(jnp.int32, (1, rows), 1)
            visible = (key_pos >= first) & (key_pos <= query_pos)
            scores = lax.dot_general(
                query, kv_in[slot, :, :head_dim], (((1,), (1,)), ((), ())),
                preferred_element_type=jnp.float32,
            ) * scale
            scores = jnp.where(visible, scores, -1e30)
            kept[slot] = scores
            top[...] = jnp.maximum(top[...], jnp.max(scores, axis=1, keepdims=True))

        return carry

    lax.fori_loop(0, span, first_pass, 0)

    def second_pass(slot, carry):
        source = per * mine - back + slot

        @pl.when(source >= 0)
        def _():
            weights = jnp.exp(kept[slot] - top[...])
            total[...] += jnp.sum(weights, axis=1, keepdims=True)
            acc[...] += jnp.dot(
                weights.astype(jnp.bfloat16), kv_in[slot, :, head_dim:],
                preferred_element_type=jnp.float32,
            )

        return carry

    lax.fori_loop(0, span, second_pass, 0)
    att[...] = (acc[...] / total[...]).astype(att.dtype).reshape(att.shape)

    for i in range(per):
        target = per * mine + i

        @pl.when(target == me)
        def _():
            pltpu.make_async_copy(att.at[i], out_ref.at[head], att_send.at[i]).start()

        @pl.when(target != me)
        def _():
            remote(att.at[i], out_ref.at[head], att_send.at[i], att_recv.at[head], target).start()

    for i in range(per):
        target = per * mine + i

        @pl.when(target == me)
        def _():
            pltpu.make_async_copy(att.at[i], out_ref.at[head], att_send.at[i]).wait()

        @pl.when(target != me)
        def _():
            remote(
                att.at[i], out_ref.at[head], att_send.at[i], att_recv.at[head], target
            ).wait_send()

    for h in range(heads):
        source = h * blocks + me // per

        @pl.when(source != me)
        def _():
            remote(att.at[0], out_ref.at[h], att_send.at[0], att_recv.at[h], source).wait_recv()

    for src, dst, send, recv, target, valid in plan:

        @pl.when(valid & (target != me))
        def _():
            remote(src, dst, send, recv, target).wait_send()


def attend(bounds, q, kv, blocks, back, scale):
    heads, rows, head_dim = q.shape
    per = heads
    span = back + per
    tries = back // per + 1
    return pl.pallas_call(
        functools.partial(attend_kernel, blocks, per, back, scale),
        out_shape=jax.ShapeDtypeStruct(q.shape, q.dtype),
        in_specs=[
            pl.BlockSpec(memory_space=pltpu.SMEM),
            pl.BlockSpec(memory_space=pl.ANY),
            pl.BlockSpec(memory_space=pl.ANY),
        ],
        out_specs=pl.BlockSpec(memory_space=pl.ANY),
        scratch_shapes=[
            pltpu.VMEM((per, rows, head_dim), q.dtype),
            pltpu.VMEM((span,) + kv.shape[1:], kv.dtype),
            pltpu.VMEM((per, rows, head_dim), q.dtype),
            pltpu.VMEM((per * rows, head_dim), jnp.float32),
            pltpu.VMEM((per * rows, 1), jnp.float32),
            pltpu.VMEM((per * rows, 1), jnp.float32),
            pltpu.VMEM((span, per * rows, rows), jnp.float32),
            pltpu.SemaphoreType.DMA((heads,)),
            pltpu.SemaphoreType.DMA((per,)),
            pltpu.SemaphoreType.DMA((heads, tries)),
            pltpu.SemaphoreType.DMA((span,)),
            pltpu.SemaphoreType.DMA((per,)),
            pltpu.SemaphoreType.DMA((heads,)),
        ],
        compiler_params=pltpu.CompilerParams(has_side_effects=True),
    )(bounds, q, kv)


def shards(
    queries, keys, values, lengths, resid, w_out, moe_gain, routes, gates, w_gate_up, w_down
):
    seq_count = lax.axis_size("seq")
    me = lax.axis_index("seq")
    query_rows = queries.shape[0]
    local_heads = queries.shape[1] // HEAD_DIM
    cols = queries.shape[1]
    width = resid.shape[1]
    score_scale = 1.0 / math.sqrt(HEAD_DIM)
    longest = (seq_count * query_rows) // 2
    reach = min(seq_count - 1, -(-(longest - 1) // query_rows))
    blocks = seq_count // local_heads
    per = seq_count // blocks
    back = -(-reach // per) * per
    span = back + per
    head_q = queries.reshape(query_rows, local_heads, HEAD_DIM).transpose(1, 0, 2)
    head_kv = jnp.concatenate(
        [
            keys.reshape(query_rows, local_heads, HEAD_DIM),
            values.reshape(query_rows, local_heads, HEAD_DIM),
        ],
        axis=2,
    ).transpose(1, 0, 2)
    attention = (
        attend(
            jnp.cumsum(lengths).astype(jnp.int32), head_q, head_kv, blocks, back, score_scale
        )
        .transpose(1, 0, 2)
        .reshape(query_rows, local_heads * HEAD_DIM)
    )
    tp_index = lax.axis_index("tp")
    near_swap = [(t, t ^ 1) for t in range(lax.axis_size("tp"))]
    far_swap = [(t, t ^ 2) for t in range(lax.axis_size("tp"))]
    local_rows = resid.shape[0]
    partial_proj = jnp.dot(attention, w_out, preferred_element_type=jnp.float32).reshape(
        2, 2, local_rows, width
    )
    core = tp_index % 2
    keep = lax.dynamic_index_in_dim(partial_proj, core, axis=1, keepdims=False)
    give = lax.dynamic_index_in_dim(partial_proj, 1 - core, axis=1, keepdims=False)
    half = keep + lax.ppermute(give.astype(jnp.bfloat16), "tp", near_swap).astype(jnp.float32)
    far = tp_index // 2
    pair_resid = jnp.stack([resid, lax.ppermute(resid, "tp", far_swap)])
    pair_routes = jnp.stack([routes, lax.ppermute(routes, "tp", far_swap)])
    pair_gates = jnp.stack([gates, lax.ppermute(gates, "tp", far_swap)])
    half = half.astype(jnp.bfloat16)
    total = half.astype(jnp.float32) + lax.ppermute(half, "tp", far_swap).astype(jnp.float32)
    pair_proj = jnp.stack(
        [
            lax.dynamic_index_in_dim(total, far, axis=0, keepdims=False),
            lax.dynamic_index_in_dim(total, 1 - far, axis=0, keepdims=False),
        ]
    )
    pair_attended = (pair_resid.astype(jnp.float32) + pair_proj).astype(jnp.bfloat16)
    attended = pair_attended[0]
    widened = pair_attended.astype(jnp.float32)
    meansq = jnp.mean(widened * widened, axis=2, keepdims=True)
    pair_normed = (widened * lax.rsqrt(meansq + 1e-05) * moe_gain).astype(jnp.bfloat16)
    top_count = routes.shape[1]
    owned = w_gate_up.shape[0]
    experts_all = owned * seq_count
    capacity = 3 * local_rows * top_count // (2 * experts_all)
    matches = pair_routes[..., None] == jnp.arange(experts_all, dtype=jnp.int32)
    member = jnp.any(matches, axis=2)
    slot = jnp.cumsum(member.astype(jnp.int32), axis=1) - 1
    place = member[..., None] & (slot[..., None] == jnp.arange(capacity, dtype=jnp.int32))
    buffer = jnp.einsum(
        "xiec,xid->excd", place.astype(jnp.bfloat16), pair_normed,
        preferred_element_type=jnp.float32,
    ).astype(jnp.bfloat16)
    buffer = buffer.reshape(seq_count, owned, 2, capacity, width).transpose(1, 0, 2, 3, 4)
    arrived = lax.all_to_all(buffer, "seq", split_axis=1, concat_axis=1, tiled=True)
    near_gate_up = lax.ppermute(w_gate_up, "tp", near_swap)
    near_down = lax.ppermute(w_down, "tp", near_swap)

    def expert_part(slots, gate_up, down):
        projections = jnp.einsum(
            "xnd,xdgf->xngf", slots.reshape(owned, -1, width), gate_up,
            preferred_element_type=jnp.float32,
        )
        hidden = (jax.nn.silu(projections[..., 0, :]) * projections[..., 1, :]).astype(
            jnp.bfloat16
        )
        return jnp.einsum(
            "xnf,xfd->xnd", hidden, down, preferred_element_type=jnp.float32
        ).astype(jnp.bfloat16)

    reduced = (
        expert_part(arrived, w_gate_up, w_down).astype(jnp.float32)
        + expert_part(arrived, near_gate_up, near_down).astype(jnp.float32)
    ).astype(jnp.bfloat16)
    returned = lax.all_to_all(
        reduced.reshape(arrived.shape), "seq", split_axis=1, concat_axis=1, tiled=True
    )
    weight_of = jnp.sum(jnp.where(matches, pair_gates[..., None], 0.0), axis=2)
    mix_weights = jnp.where(place, weight_of[..., None], 0.0)
    mixes = jnp.einsum(
        "xiec,xecd->xid",
        mix_weights.astype(jnp.bfloat16),
        returned.transpose(2, 1, 0, 3, 4).reshape(2, experts_all, capacity, width),
        preferred_element_type=jnp.float32,
    )
    from_far = lax.ppermute(mixes[1].astype(jnp.bfloat16), "tp", far_swap)
    expert_mix = (mixes[0] + from_far.astype(jnp.float32)).astype(jnp.bfloat16)
    return (attended, expert_mix)


def solution(mesh):
    return jax.shard_map(
        shards,
        mesh=mesh,
        in_specs=(
            P("seq", "tp"),
            P("seq", "tp"),
            P("seq", "tp"),
            P(),
            P(("seq", "tp"), None),
            P("tp", None),
            P(),
            P(("seq", "tp"), None),
            P(("seq", "tp"), None),
            P("seq", None, None, "tp"),
            P("seq", "tp", None),
        ),
        out_specs=(P(("seq", "tp"), None), P(("seq", "tp"), None)),
        check_vma=False,
    )
```

```python
import functools
import math

import jax
import jax.numpy as jnp
from jax import lax
from jax.experimental import pallas as pl
from jax.experimental.pallas import tpu as pltpu
from jax.sharding import PartitionSpec as P

HEAD_DIM = 128


def tenant_of(positions, lengths):
    bounds = jnp.cumsum(lengths)
    return jnp.sum((positions[:, None] >= bounds[None, :]).astype(jnp.int32), axis=1)


def spread_kernel(
    blocks, per, back, q_ref, kv_ref, q_out, kv_out, q_send, q_recv, kv_send, kv_recv
):
    me = lax.axis_index("seq")
    tp = lax.axis_index("tp")
    heads = q_ref.shape[0]
    span = back + per
    tries = back // per + 1
    mine = me % blocks

    def send(src, dst, sem, recv, target):
        @pl.when(target == me)
        def _():
            pltpu.make_async_copy(src, dst, sem).start()

        @pl.when(target != me)
        def _():
            pltpu.make_async_remote_copy(
                src_ref=src,
                dst_ref=dst,
                send_sem=sem,
                recv_sem=recv,
                device_id=(target, tp),
                device_id_type=pl.DeviceIdType.MESH,
            ).start()

    def finish_send(src, dst, sem, recv, target):
        @pl.when(target == me)
        def _():
            pltpu.make_async_copy(src, dst, sem).wait()

        @pl.when(target != me)
        def _():
            pltpu.make_async_remote_copy(
                src_ref=src,
                dst_ref=dst,
                send_sem=sem,
                recv_sem=recv,
                device_id=(target, tp),
                device_id_type=pl.DeviceIdType.MESH,
            ).wait_send()

    def finish_recv(src, dst, sem, recv, source):
        @pl.when(source != me)
        def _():
            pltpu.make_async_remote_copy(
                src_ref=src,
                dst_ref=dst,
                send_sem=sem,
                recv_sem=recv,
                device_id=(source, tp),
                device_id_type=pl.DeviceIdType.MESH,
            ).wait_recv()

    plan = []
    for h in range(heads):
        target = h * blocks + me // per
        plan.append((q_ref.at[h], q_out.at[me % per], q_send.at[h], q_recv.at[me % per], target))
        for r in range(tries):
            block = (me + back) // per - r
            slot = (me + back) % per + per * r
            plan.append(
                (
                    kv_ref.at[h],
                    kv_out.at[slot],
                    kv_send.at[h, r],
                    kv_recv.at[slot],
                    h * blocks + block,
                    (block >= 0) & (block < blocks),
                )
            )
    for item in plan:
        valid = item[5] if len(item) > 5 else True

        @pl.when(valid)
        def _():
            send(*item[:5])

    for item in plan:
        valid = item[5] if len(item) > 5 else True

        @pl.when(valid)
        def _():
            finish_send(*item[:5])

    for i in range(per):
        source = per * mine + i
        finish_recv(q_ref.at[0], q_out.at[i], q_send.at[0], q_recv.at[i], source)
    for slot in range(span):
        source = per * mine - back + slot

        @pl.when(source >= 0)
        def _():
            finish_recv(kv_ref.at[0], kv_out.at[slot], kv_send.at[0, 0], kv_recv.at[slot], source)


def spread(q, kv, blocks, per, back):
    heads = q.shape[0]
    span = back + per
    tries = back // per + 1
    return pl.pallas_call(
        functools.partial(spread_kernel, blocks, per, back),
        out_shape=(
            jax.ShapeDtypeStruct((per,) + q.shape[1:], q.dtype),
            jax.ShapeDtypeStruct((span,) + kv.shape[1:], kv.dtype),
        ),
        in_specs=[pl.BlockSpec(memory_space=pl.ANY)] * 2,
        out_specs=(pl.BlockSpec(memory_space=pl.ANY), pl.BlockSpec(memory_space=pl.ANY)),
        scratch_shapes=[
            pltpu.SemaphoreType.DMA((heads,)),
            pltpu.SemaphoreType.DMA((per,)),
            pltpu.SemaphoreType.DMA((heads, tries)),
            pltpu.SemaphoreType.DMA((span,)),
        ],
        compiler_params=pltpu.CompilerParams(has_side_effects=True),
    )(q, kv)


def gather_kernel(blocks, per, att_ref, out_ref, send_sem, recv_sem):
    me = lax.axis_index("seq")
    tp = lax.axis_index("tp")
    heads = out_ref.shape[0]
    head = me // blocks
    mine = me % blocks

    def copy(i, target):
        return pltpu.make_async_remote_copy(
            src_ref=att_ref.at[i],
            dst_ref=out_ref.at[head],
            send_sem=send_sem.at[i],
            recv_sem=recv_sem.at[head],
            device_id=(target, tp),
            device_id_type=pl.DeviceIdType.MESH,
        )

    for i in range(per):
        target = per * mine + i

        @pl.when(target == me)
        def _():
            pltpu.make_async_copy(att_ref.at[i], out_ref.at[head], send_sem.at[i]).start()

        @pl.when(target != me)
        def _():
            copy(i, target).start()

    for i in range(per):
        target = per * mine + i

        @pl.when(target == me)
        def _():
            pltpu.make_async_copy(att_ref.at[i], out_ref.at[head], send_sem.at[i]).wait()

        @pl.when(target != me)
        def _():
            copy(i, target).wait_send()

    for h in range(heads):
        source = h * blocks + me // per

        @pl.when(source != me)
        def _():
            pltpu.make_async_remote_copy(
                src_ref=att_ref.at[0],
                dst_ref=out_ref.at[h],
                send_sem=send_sem.at[0],
                recv_sem=recv_sem.at[h],
                device_id=(source, tp),
                device_id_type=pl.DeviceIdType.MESH,
            ).wait_recv()


def gather_back(att, heads, blocks):
    per = att.shape[0]
    return pl.pallas_call(
        functools.partial(gather_kernel, blocks, per),
        out_shape=jax.ShapeDtypeStruct((heads,) + att.shape[1:], att.dtype),
        in_specs=[pl.BlockSpec(memory_space=pl.ANY)],
        out_specs=pl.BlockSpec(memory_space=pl.ANY),
        scratch_shapes=[pltpu.SemaphoreType.DMA((per,)), pltpu.SemaphoreType.DMA((heads,))],
        compiler_params=pltpu.CompilerParams(has_side_effects=True),
    )(att)


def attend_kernel(
    blocks, per, back, scale, bounds_ref, q_ref, kv_ref, out_ref,
    q_in, kv_in, att, acc, top, total, kept,
    q_send, q_recv, kv_send, kv_recv, att_send, att_recv,
):
    me = lax.axis_index("seq")
    tp = lax.axis_index("tp")
    heads, rows, head_dim = q_ref.shape
    span = back + per
    tries = back // per + 1
    mine = me // heads
    head = me % heads

    def remote(src, dst, send, recv, device):
        return pltpu.make_async_remote_copy(
            src_ref=src, dst_ref=dst, send_sem=send, recv_sem=recv,
            device_id=(device, tp), device_id_type=pl.DeviceIdType.MESH,
        )

    plan = []
    for h in range(heads):
        target = (me // per) * heads + h
        plan.append(
            (q_ref.at[h], q_in.at[me % per], q_send.at[h], q_recv.at[me % per], target, True)
        )
        for r in range(tries):
            block = (me + back) // per - r
            slot = (me + back) % per + per * r
            valid = (block >= 0) & (block < blocks)
            plan.append(
                (kv_ref.at[h], kv_in.at[slot], kv_send.at[h, r], kv_recv.at[slot],
                 block * heads + h, valid)
            )
    for src, dst, send, recv, target, valid in plan:

        @pl.when(valid & (target == me))
        def _():
            pltpu.make_async_copy(src, dst, send).start()

        @pl.when(valid & (target != me))
        def _():
            remote(src, dst, send, recv, target).start()

    for src, dst, send, recv, target, valid in plan:

        @pl.when(valid & (target == me))
        def _():
            pltpu.make_async_copy(src, dst, send).wait()

    for i in range(per):
        source = per * mine + i

        @pl.when(source != me)
        def _():
            remote(q_ref.at[0], q_in.at[i], q_send.at[0], q_recv.at[i], source).wait_recv()

    query = q_in[...].reshape(per * rows, head_dim)
    query_pos = mine * per * rows + lax.broadcasted_iota(jnp.int32, (per * rows, 1), 0)
    first = jnp.zeros(query_pos.shape, jnp.int32)
    for k in range(bounds_ref.shape[0]):
        first = jnp.maximum(first, jnp.where(query_pos >= bounds_ref[k], bounds_ref[k], 0))

    top[...] = jnp.full(top.shape, -1e30, jnp.float32)
    total[...] = jnp.zeros(total.shape, jnp.float32)
    acc[...] = jnp.zeros(acc.shape, jnp.float32)

    def first_pass(slot, carry):
        source = per * mine - back + slot

        @pl.when(source >= 0)
        def _():
            @pl.when(source != me)
            def _():
                remote(
                    kv_ref.at[0], kv_in.at[slot], kv_send.at[0, 0], kv_recv.at[slot], source
                ).wait_recv()

            key_pos = source * rows + lax.broadcasted_iota(jnp.int32, (1, rows), 1)
            visible = (key_pos >= first) & (key_pos <= query_pos)
            scores = lax.dot_general(
                query, kv_in[slot, :, :head_dim], (((1,), (1,)), ((), ())),
                preferred_element_type=jnp.float32,
            ) * scale
            scores = jnp.where(visible, scores, -1e30)
            kept[slot] = scores
            top[...] = jnp.maximum(top[...], jnp.max(scores, axis=1, keepdims=True))

        return carry

    lax.fori_loop(0, span, first_pass, 0)

    def second_pass(slot, carry):
        source = per * mine - back + slot

        @pl.when(source >= 0)
        def _():
            weights = jnp.exp(kept[slot] - top[...])
            total[...] += jnp.sum(weights, axis=1, keepdims=True)
            acc[...] += jnp.dot(
                weights.astype(jnp.bfloat16), kv_in[slot, :, head_dim:],
                preferred_element_type=jnp.float32,
            )

        return carry

    lax.fori_loop(0, span, second_pass, 0)
    att[...] = (acc[...] / total[...]).astype(att.dtype).reshape(att.shape)

    for i in range(per):
        target = per * mine + i

        @pl.when(target == me)
        def _():
            pltpu.make_async_copy(att.at[i], out_ref.at[head], att_send.at[i]).start()

        @pl.when(target != me)
        def _():
            remote(att.at[i], out_ref.at[head], att_send.at[i], att_recv.at[head], target).start()

    for i in range(per):
        target = per * mine + i

        @pl.when(target == me)
        def _():
            pltpu.make_async_copy(att.at[i], out_ref.at[head], att_send.at[i]).wait()

        @pl.when(target != me)
        def _():
            remote(
                att.at[i], out_ref.at[head], att_send.at[i], att_recv.at[head], target
            ).wait_send()

    for h in range(heads):
        source = (me // per) * heads + h

        @pl.when(source != me)
        def _():
            remote(att.at[0], out_ref.at[h], att_send.at[0], att_recv.at[h], source).wait_recv()

    for src, dst, send, recv, target, valid in plan:

        @pl.when(valid & (target != me))
        def _():
            remote(src, dst, send, recv, target).wait_send()


def attend(bounds, q, kv, blocks, back, scale):
    heads, rows, head_dim = q.shape
    per = heads
    span = back + per
    tries = back // per + 1
    return pl.pallas_call(
        functools.partial(attend_kernel, blocks, per, back, scale),
        out_shape=jax.ShapeDtypeStruct(q.shape, q.dtype),
        in_specs=[
            pl.BlockSpec(memory_space=pltpu.SMEM),
            pl.BlockSpec(memory_space=pl.ANY),
            pl.BlockSpec(memory_space=pl.ANY),
        ],
        out_specs=pl.BlockSpec(memory_space=pl.ANY),
        scratch_shapes=[
            pltpu.VMEM((per, rows, head_dim), q.dtype),
            pltpu.VMEM((span,) + kv.shape[1:], kv.dtype),
            pltpu.VMEM((per, rows, head_dim), q.dtype),
            pltpu.VMEM((per * rows, head_dim), jnp.float32),
            pltpu.VMEM((per * rows, 1), jnp.float32),
            pltpu.VMEM((per * rows, 1), jnp.float32),
            pltpu.VMEM((span, per * rows, rows), jnp.float32),
            pltpu.SemaphoreType.DMA((heads,)),
            pltpu.SemaphoreType.DMA((per,)),
            pltpu.SemaphoreType.DMA((heads, tries)),
            pltpu.SemaphoreType.DMA((span,)),
            pltpu.SemaphoreType.DMA((per,)),
            pltpu.SemaphoreType.DMA((heads,)),
        ],
        compiler_params=pltpu.CompilerParams(has_side_effects=True),
    )(bounds, q, kv)


def shards(
    queries, keys, values, lengths, resid, w_out, moe_gain, routes, gates, w_gate_up, w_down
):
    seq_count = lax.axis_size("seq")
    me = lax.axis_index("seq")
    query_rows = queries.shape[0]
    local_heads = queries.shape[1] // HEAD_DIM
    cols = queries.shape[1]
    width = resid.shape[1]
    score_scale = 1.0 / math.sqrt(HEAD_DIM)
    longest = (seq_count * query_rows) // 2
    reach = min(seq_count - 1, -(-(longest - 1) // query_rows))
    blocks = seq_count // local_heads
    per = seq_count // blocks
    back = -(-reach // per) * per
    span = back + per
    head_q = queries.reshape(query_rows, local_heads, HEAD_DIM).transpose(1, 0, 2)
    head_kv = jnp.concatenate(
        [
            keys.reshape(query_rows, local_heads, HEAD_DIM),
            values.reshape(query_rows, local_heads, HEAD_DIM),
        ],
        axis=2,
    ).transpose(1, 0, 2)
    attention = (
        attend(
            jnp.cumsum(lengths).astype(jnp.int32), head_q, head_kv, blocks, back, score_scale
        )
        .transpose(1, 0, 2)
        .reshape(query_rows, local_heads * HEAD_DIM)
    )
    tp_index = lax.axis_index("tp")
    near_swap = [(t, t ^ 1) for t in range(lax.axis_size("tp"))]
    far_swap = [(t, t ^ 2) for t in range(lax.axis_size("tp"))]
    local_rows = resid.shape[0]
    partial_proj = jnp.dot(attention, w_out, preferred_element_type=jnp.float32).reshape(
        2, 2, local_rows, width
    )
    core = tp_index % 2
    keep = lax.dynamic_index_in_dim(partial_proj, core, axis=1, keepdims=False)
    give = lax.dynamic_index_in_dim(partial_proj, 1 - core, axis=1, keepdims=False)
    half = keep + lax.ppermute(give.astype(jnp.bfloat16), "tp", near_swap).astype(jnp.float32)
    far = tp_index // 2
    pair_resid = jnp.stack([resid, lax.ppermute(resid, "tp", far_swap)])
    pair_routes = jnp.stack([routes, lax.ppermute(routes, "tp", far_swap)])
    pair_gates = jnp.stack([gates, lax.ppermute(gates, "tp", far_swap)])
    half = half.astype(jnp.bfloat16)
    total = half.astype(jnp.float32) + lax.ppermute(half, "tp", far_swap).astype(jnp.float32)
    pair_proj = jnp.stack(
        [
            lax.dynamic_index_in_dim(total, far, axis=0, keepdims=False),
            lax.dynamic_index_in_dim(total, 1 - far, axis=0, keepdims=False),
        ]
    )
    pair_attended = (pair_resid.astype(jnp.float32) + pair_proj).astype(jnp.bfloat16)
    attended = pair_attended[0]
    widened = pair_attended.astype(jnp.float32)
    meansq = jnp.mean(widened * widened, axis=2, keepdims=True)
    pair_normed = (widened * lax.rsqrt(meansq + 1e-05) * moe_gain).astype(jnp.bfloat16)
    top_count = routes.shape[1]
    owned = w_gate_up.shape[0]
    experts_all = owned * seq_count
    capacity = 3 * local_rows * top_count // (2 * experts_all)
    matches = pair_routes[..., None] == jnp.arange(experts_all, dtype=jnp.int32)
    member = jnp.any(matches, axis=2)
    slot = jnp.cumsum(member.astype(jnp.int32), axis=1) - 1
    place = member[..., None] & (slot[..., None] == jnp.arange(capacity, dtype=jnp.int32))
    buffer = jnp.einsum(
        "xiec,xid->excd", place.astype(jnp.bfloat16), pair_normed,
        preferred_element_type=jnp.float32,
    ).astype(jnp.bfloat16)
    buffer = buffer.reshape(seq_count, owned, 2, capacity, width).transpose(1, 0, 2, 3, 4)
    arrived = lax.all_to_all(buffer, "seq", split_axis=1, concat_axis=1, tiled=True)
    near = lax.ppermute(arrived, "tp", near_swap)

    def expert_part(slots):
        projections = jnp.einsum(
            "xnd,xdgf->xngf", slots.reshape(owned, -1, width), w_gate_up,
            preferred_element_type=jnp.float32,
        )
        hidden = (jax.nn.silu(projections[..., 0, :]) * projections[..., 1, :]).astype(
            jnp.bfloat16
        )
        return jnp.einsum(
            "xnf,xfd->xnd", hidden, w_down, preferred_element_type=jnp.float32
        ).astype(jnp.bfloat16)

    from_near = lax.ppermute(expert_part(near), "tp", near_swap)
    reduced = (
        expert_part(arrived).astype(jnp.float32) + from_near.astype(jnp.float32)
    ).astype(jnp.bfloat16)
    returned = lax.all_to_all(
        reduced.reshape(arrived.shape), "seq", split_axis=1, concat_axis=1, tiled=True
    )
    weight_of = jnp.sum(jnp.where(matches, pair_gates[..., None], 0.0), axis=2)
    mix_weights = jnp.where(place, weight_of[..., None], 0.0)
    mixes = jnp.einsum(
        "xiec,xecd->xid",
        mix_weights.astype(jnp.bfloat16),
        returned.transpose(2, 1, 0, 3, 4).reshape(2, experts_all, capacity, width),
        preferred_element_type=jnp.float32,
    )
    from_far = lax.ppermute(mixes[1].astype(jnp.bfloat16), "tp", far_swap)
    expert_mix = (mixes[0] + from_far.astype(jnp.float32)).astype(jnp.bfloat16)
    return (attended, expert_mix)


def solution(mesh):
    return jax.shard_map(
        shards,
        mesh=mesh,
        in_specs=(
            P("seq", "tp"),
            P("seq", "tp"),
            P("seq", "tp"),
            P(),
            P(("seq", "tp"), None),
            P("tp", None),
            P(),
            P(("seq", "tp"), None),
            P(("seq", "tp"), None),
            P("seq", None, None, "tp"),
            P("seq", "tp", None),
        ),
        out_specs=(P(("seq", "tp"), None), P(("seq", "tp"), None)),
        check_vma=False,
    )
```

```python
import functools
import math

import jax
import jax.numpy as jnp
from jax import lax
from jax.experimental import pallas as pl
from jax.experimental.pallas import tpu as pltpu
from jax.sharding import PartitionSpec as P

HEAD_DIM = 128


def tenant_of(positions, lengths):
    bounds = jnp.cumsum(lengths)
    return jnp.sum((positions[:, None] >= bounds[None, :]).astype(jnp.int32), axis=1)


def spread_kernel(
    blocks, per, back, q_ref, kv_ref, q_out, kv_out, q_send, q_recv, kv_send, kv_recv
):
    me = lax.axis_index("seq")
    tp = lax.axis_index("tp")
    heads = q_ref.shape[0]
    span = back + per
    tries = back // per + 1
    mine = me % blocks

    def send(src, dst, sem, recv, target):
        @pl.when(target == me)
        def _():
            pltpu.make_async_copy(src, dst, sem).start()

        @pl.when(target != me)
        def _():
            pltpu.make_async_remote_copy(
                src_ref=src,
                dst_ref=dst,
                send_sem=sem,
                recv_sem=recv,
                device_id=(target, tp),
                device_id_type=pl.DeviceIdType.MESH,
            ).start()

    def finish_send(src, dst, sem, recv, target):
        @pl.when(target == me)
        def _():
            pltpu.make_async_copy(src, dst, sem).wait()

        @pl.when(target != me)
        def _():
            pltpu.make_async_remote_copy(
                src_ref=src,
                dst_ref=dst,
                send_sem=sem,
                recv_sem=recv,
                device_id=(target, tp),
                device_id_type=pl.DeviceIdType.MESH,
            ).wait_send()

    def finish_recv(src, dst, sem, recv, source):
        @pl.when(source != me)
        def _():
            pltpu.make_async_remote_copy(
                src_ref=src,
                dst_ref=dst,
                send_sem=sem,
                recv_sem=recv,
                device_id=(source, tp),
                device_id_type=pl.DeviceIdType.MESH,
            ).wait_recv()

    plan = []
    for h in range(heads):
        target = h * blocks + me // per
        plan.append((q_ref.at[h], q_out.at[me % per], q_send.at[h], q_recv.at[me % per], target))
        for r in range(tries):
            block = (me + back) // per - r
            slot = (me + back) % per + per * r
            plan.append(
                (
                    kv_ref.at[h],
                    kv_out.at[slot],
                    kv_send.at[h, r],
                    kv_recv.at[slot],
                    h * blocks + block,
                    (block >= 0) & (block < blocks),
                )
            )
    for item in plan:
        valid = item[5] if len(item) > 5 else True

        @pl.when(valid)
        def _():
            send(*item[:5])

    for item in plan:
        valid = item[5] if len(item) > 5 else True

        @pl.when(valid)
        def _():
            finish_send(*item[:5])

    for i in range(per):
        source = per * mine + i
        finish_recv(q_ref.at[0], q_out.at[i], q_send.at[0], q_recv.at[i], source)
    for slot in range(span):
        source = per * mine - back + slot

        @pl.when(source >= 0)
        def _():
            finish_recv(kv_ref.at[0], kv_out.at[slot], kv_send.at[0, 0], kv_recv.at[slot], source)


def spread(q, kv, blocks, per, back):
    heads = q.shape[0]
    span = back + per
    tries = back // per + 1
    return pl.pallas_call(
        functools.partial(spread_kernel, blocks, per, back),
        out_shape=(
            jax.ShapeDtypeStruct((per,) + q.shape[1:], q.dtype),
            jax.ShapeDtypeStruct((span,) + kv.shape[1:], kv.dtype),
        ),
        in_specs=[pl.BlockSpec(memory_space=pl.ANY)] * 2,
        out_specs=(pl.BlockSpec(memory_space=pl.ANY), pl.BlockSpec(memory_space=pl.ANY)),
        scratch_shapes=[
            pltpu.SemaphoreType.DMA((heads,)),
            pltpu.SemaphoreType.DMA((per,)),
            pltpu.SemaphoreType.DMA((heads, tries)),
            pltpu.SemaphoreType.DMA((span,)),
        ],
        compiler_params=pltpu.CompilerParams(has_side_effects=True),
    )(q, kv)


def gather_kernel(blocks, per, att_ref, out_ref, send_sem, recv_sem):
    me = lax.axis_index("seq")
    tp = lax.axis_index("tp")
    heads = out_ref.shape[0]
    head = me // blocks
    mine = me % blocks

    def copy(i, target):
        return pltpu.make_async_remote_copy(
            src_ref=att_ref.at[i],
            dst_ref=out_ref.at[head],
            send_sem=send_sem.at[i],
            recv_sem=recv_sem.at[head],
            device_id=(target, tp),
            device_id_type=pl.DeviceIdType.MESH,
        )

    for i in range(per):
        target = per * mine + i

        @pl.when(target == me)
        def _():
            pltpu.make_async_copy(att_ref.at[i], out_ref.at[head], send_sem.at[i]).start()

        @pl.when(target != me)
        def _():
            copy(i, target).start()

    for i in range(per):
        target = per * mine + i

        @pl.when(target == me)
        def _():
            pltpu.make_async_copy(att_ref.at[i], out_ref.at[head], send_sem.at[i]).wait()

        @pl.when(target != me)
        def _():
            copy(i, target).wait_send()

    for h in range(heads):
        source = h * blocks + me // per

        @pl.when(source != me)
        def _():
            pltpu.make_async_remote_copy(
                src_ref=att_ref.at[0],
                dst_ref=out_ref.at[h],
                send_sem=send_sem.at[0],
                recv_sem=recv_sem.at[h],
                device_id=(source, tp),
                device_id_type=pl.DeviceIdType.MESH,
            ).wait_recv()


def gather_back(att, heads, blocks):
    per = att.shape[0]
    return pl.pallas_call(
        functools.partial(gather_kernel, blocks, per),
        out_shape=jax.ShapeDtypeStruct((heads,) + att.shape[1:], att.dtype),
        in_specs=[pl.BlockSpec(memory_space=pl.ANY)],
        out_specs=pl.BlockSpec(memory_space=pl.ANY),
        scratch_shapes=[pltpu.SemaphoreType.DMA((per,)), pltpu.SemaphoreType.DMA((heads,))],
        compiler_params=pltpu.CompilerParams(has_side_effects=True),
    )(att)


def attend_kernel(
    blocks, per, back, scale, bounds_ref, q_ref, kv_ref, out_ref,
    q_in, kv_in, att, acc, top, total, kept,
    q_send, q_recv, kv_send, kv_recv, att_send, att_recv,
):
    me = lax.axis_index("seq")
    tp = lax.axis_index("tp")
    heads, rows, head_dim = q_ref.shape
    span = back + per
    tries = back // per + 1
    mine = me // heads
    head = me % heads

    def remote(src, dst, send, recv, device):
        return pltpu.make_async_remote_copy(
            src_ref=src, dst_ref=dst, send_sem=send, recv_sem=recv,
            device_id=(device, tp), device_id_type=pl.DeviceIdType.MESH,
        )

    plan = []
    for h in range(heads):
        target = (me // per) * heads + h
        plan.append(
            (q_ref.at[h], q_in.at[me % per], q_send.at[h], q_recv.at[me % per], target, True)
        )
        for r in range(tries):
            block = (me + back) // per - r
            slot = (me + back) % per + per * r
            valid = (block >= 0) & (block < blocks)
            plan.append(
                (kv_ref.at[h], kv_in.at[slot], kv_send.at[h, r], kv_recv.at[slot],
                 block * heads + h, valid)
            )
    for src, dst, send, recv, target, valid in plan:

        @pl.when(valid & (target == me))
        def _():
            pltpu.make_async_copy(src, dst, send).start()

        @pl.when(valid & (target != me))
        def _():
            remote(src, dst, send, recv, target).start()

    for src, dst, send, recv, target, valid in plan:

        @pl.when(valid & (target == me))
        def _():
            pltpu.make_async_copy(src, dst, send).wait()

    for i in range(per):
        source = per * mine + i

        @pl.when(source != me)
        def _():
            remote(q_ref.at[0], q_in.at[i], q_send.at[0], q_recv.at[i], source).wait_recv()

    query = q_in[...].reshape(per * rows, head_dim)
    query_pos = mine * per * rows + lax.broadcasted_iota(jnp.int32, (per * rows, 1), 0)
    first = jnp.zeros(query_pos.shape, jnp.int32)
    for k in range(bounds_ref.shape[0]):
        first = jnp.maximum(first, jnp.where(query_pos >= bounds_ref[k], bounds_ref[k], 0))

    top[...] = jnp.full(top.shape, -1e30, jnp.float32)
    total[...] = jnp.zeros(total.shape, jnp.float32)
    acc[...] = jnp.zeros(acc.shape, jnp.float32)

    def first_pass(step, carry):
        slot = span - 1 - step
        source = per * mine - back + slot

        @pl.when(source >= 0)
        def _():
            @pl.when(source != me)
            def _():
                remote(
                    kv_ref.at[0], kv_in.at[slot], kv_send.at[0, 0], kv_recv.at[slot], source
                ).wait_recv()

            key_pos = source * rows + lax.broadcasted_iota(jnp.int32, (1, rows), 1)
            visible = (key_pos >= first) & (key_pos <= query_pos)
            scores = lax.dot_general(
                query, kv_in[slot, :, :head_dim], (((1,), (1,)), ((), ())),
                preferred_element_type=jnp.float32,
            ) * scale
            scores = jnp.where(visible, scores, -1e30)
            kept[slot] = scores
            top[...] = jnp.maximum(top[...], jnp.max(scores, axis=1, keepdims=True))

        return carry

    lax.fori_loop(0, span, first_pass, 0)

    def second_pass(slot, carry):
        source = per * mine - back + slot

        @pl.when(source >= 0)
        def _():
            weights = jnp.exp(kept[slot] - top[...])
            total[...] += jnp.sum(weights, axis=1, keepdims=True)
            acc[...] += jnp.dot(
                weights.astype(jnp.bfloat16), kv_in[slot, :, head_dim:],
                preferred_element_type=jnp.float32,
            )

        return carry

    lax.fori_loop(0, span, second_pass, 0)
    att[...] = (acc[...] / total[...]).astype(att.dtype).reshape(att.shape)

    for i in range(per):
        target = per * mine + i

        @pl.when(target == me)
        def _():
            pltpu.make_async_copy(att.at[i], out_ref.at[head], att_send.at[i]).start()

        @pl.when(target != me)
        def _():
            remote(att.at[i], out_ref.at[head], att_send.at[i], att_recv.at[head], target).start()

    for i in range(per):
        target = per * mine + i

        @pl.when(target == me)
        def _():
            pltpu.make_async_copy(att.at[i], out_ref.at[head], att_send.at[i]).wait()

        @pl.when(target != me)
        def _():
            remote(
                att.at[i], out_ref.at[head], att_send.at[i], att_recv.at[head], target
            ).wait_send()

    for h in range(heads):
        source = (me // per) * heads + h

        @pl.when(source != me)
        def _():
            remote(att.at[0], out_ref.at[h], att_send.at[0], att_recv.at[h], source).wait_recv()

    for src, dst, send, recv, target, valid in plan:

        @pl.when(valid & (target != me))
        def _():
            remote(src, dst, send, recv, target).wait_send()


def attend(bounds, q, kv, blocks, back, scale):
    heads, rows, head_dim = q.shape
    per = heads
    span = back + per
    tries = back // per + 1
    return pl.pallas_call(
        functools.partial(attend_kernel, blocks, per, back, scale),
        out_shape=jax.ShapeDtypeStruct(q.shape, q.dtype),
        in_specs=[
            pl.BlockSpec(memory_space=pltpu.SMEM),
            pl.BlockSpec(memory_space=pl.ANY),
            pl.BlockSpec(memory_space=pl.ANY),
        ],
        out_specs=pl.BlockSpec(memory_space=pl.ANY),
        scratch_shapes=[
            pltpu.VMEM((per, rows, head_dim), q.dtype),
            pltpu.VMEM((span,) + kv.shape[1:], kv.dtype),
            pltpu.VMEM((per, rows, head_dim), q.dtype),
            pltpu.VMEM((per * rows, head_dim), jnp.float32),
            pltpu.VMEM((per * rows, 1), jnp.float32),
            pltpu.VMEM((per * rows, 1), jnp.float32),
            pltpu.VMEM((span, per * rows, rows), jnp.float32),
            pltpu.SemaphoreType.DMA((heads,)),
            pltpu.SemaphoreType.DMA((per,)),
            pltpu.SemaphoreType.DMA((heads, tries)),
            pltpu.SemaphoreType.DMA((span,)),
            pltpu.SemaphoreType.DMA((per,)),
            pltpu.SemaphoreType.DMA((heads,)),
        ],
        compiler_params=pltpu.CompilerParams(has_side_effects=True),
    )(bounds, q, kv)


def shards(
    queries, keys, values, lengths, resid, w_out, moe_gain, routes, gates, w_gate_up, w_down
):
    seq_count = lax.axis_size("seq")
    me = lax.axis_index("seq")
    query_rows = queries.shape[0]
    local_heads = queries.shape[1] // HEAD_DIM
    cols = queries.shape[1]
    width = resid.shape[1]
    score_scale = 1.0 / math.sqrt(HEAD_DIM)
    longest = (seq_count * query_rows) // 2
    reach = min(seq_count - 1, -(-(longest - 1) // query_rows))
    blocks = seq_count // local_heads
    per = seq_count // blocks
    back = -(-reach // per) * per
    span = back + per
    head_q = queries.reshape(query_rows, local_heads, HEAD_DIM).transpose(1, 0, 2)
    head_kv = jnp.concatenate(
        [
            keys.reshape(query_rows, local_heads, HEAD_DIM),
            values.reshape(query_rows, local_heads, HEAD_DIM),
        ],
        axis=2,
    ).transpose(1, 0, 2)
    attention = (
        attend(
            jnp.cumsum(lengths).astype(jnp.int32), head_q, head_kv, blocks, back, score_scale
        )
        .transpose(1, 0, 2)
        .reshape(query_rows, local_heads * HEAD_DIM)
    )
    tp_index = lax.axis_index("tp")
    near_swap = [(t, t ^ 1) for t in range(lax.axis_size("tp"))]
    far_swap = [(t, t ^ 2) for t in range(lax.axis_size("tp"))]
    local_rows = resid.shape[0]
    partial_proj = jnp.dot(attention, w_out, preferred_element_type=jnp.float32).reshape(
        2, 2, local_rows, width
    )
    core = tp_index % 2
    keep = lax.dynamic_index_in_dim(partial_proj, core, axis=1, keepdims=False)
    give = lax.dynamic_index_in_dim(partial_proj, 1 - core, axis=1, keepdims=False)
    half = keep + lax.ppermute(give.astype(jnp.bfloat16), "tp", near_swap).astype(jnp.float32)
    far = tp_index // 2
    pair_resid = jnp.stack([resid, lax.ppermute(resid, "tp", far_swap)])
    pair_routes = jnp.stack([routes, lax.ppermute(routes, "tp", far_swap)])
    pair_gates = jnp.stack([gates, lax.ppermute(gates, "tp", far_swap)])
    half = half.astype(jnp.bfloat16)
    total = half.astype(jnp.float32) + lax.ppermute(half, "tp", far_swap).astype(jnp.float32)
    pair_proj = jnp.stack(
        [
            lax.dynamic_index_in_dim(total, far, axis=0, keepdims=False),
            lax.dynamic_index_in_dim(total, 1 - far, axis=0, keepdims=False),
        ]
    )
    pair_attended = (pair_resid.astype(jnp.float32) + pair_proj).astype(jnp.bfloat16)
    attended = pair_attended[0]
    widened = pair_attended.astype(jnp.float32)
    meansq = jnp.mean(widened * widened, axis=2, keepdims=True)
    pair_normed = (widened * lax.rsqrt(meansq + 1e-05) * moe_gain).astype(jnp.bfloat16)
    top_count = routes.shape[1]
    owned = w_gate_up.shape[0]
    experts_all = owned * seq_count
    capacity = 3 * local_rows * top_count // (2 * experts_all)
    matches = pair_routes[..., None] == jnp.arange(experts_all, dtype=jnp.int32)
    member = jnp.any(matches, axis=2)
    slot = jnp.cumsum(member.astype(jnp.int32), axis=1) - 1
    place = member[..., None] & (slot[..., None] == jnp.arange(capacity, dtype=jnp.int32))
    buffer = jnp.einsum(
        "xiec,xid->excd", place.astype(jnp.bfloat16), pair_normed,
        preferred_element_type=jnp.float32,
    ).astype(jnp.bfloat16)
    buffer = buffer.reshape(seq_count, owned, 2, capacity, width).transpose(1, 0, 2, 3, 4)
    arrived = lax.all_to_all(buffer, "seq", split_axis=1, concat_axis=1, tiled=True)
    near = lax.ppermute(arrived, "tp", near_swap)

    def expert_part(slots):
        projections = jnp.einsum(
            "xnd,xdgf->xngf", slots.reshape(owned, -1, width), w_gate_up,
            preferred_element_type=jnp.float32,
        )
        hidden = (jax.nn.silu(projections[..., 0, :]) * projections[..., 1, :]).astype(
            jnp.bfloat16
        )
        return jnp.einsum(
            "xnf,xfd->xnd", hidden, w_down, preferred_element_type=jnp.float32
        ).astype(jnp.bfloat16)

    from_near = lax.ppermute(expert_part(near), "tp", near_swap)
    reduced = (
        expert_part(arrived).astype(jnp.float32) + from_near.astype(jnp.float32)
    ).astype(jnp.bfloat16)
    returned = lax.all_to_all(
        reduced.reshape(arrived.shape), "seq", split_axis=1, concat_axis=1, tiled=True
    )
    weight_of = jnp.sum(jnp.where(matches, pair_gates[..., None], 0.0), axis=2)
    mix_weights = jnp.where(place, weight_of[..., None], 0.0)
    mixes = jnp.einsum(
        "xiec,xecd->xid",
        mix_weights.astype(jnp.bfloat16),
        returned.transpose(2, 1, 0, 3, 4).reshape(2, experts_all, capacity, width),
        preferred_element_type=jnp.float32,
    )
    from_far = lax.ppermute(mixes[1].astype(jnp.bfloat16), "tp", far_swap)
    expert_mix = (mixes[0] + from_far.astype(jnp.float32)).astype(jnp.bfloat16)
    return (attended, expert_mix)


def solution(mesh):
    return jax.shard_map(
        shards,
        mesh=mesh,
        in_specs=(
            P("seq", "tp"),
            P("seq", "tp"),
            P("seq", "tp"),
            P(),
            P(("seq", "tp"), None),
            P("tp", None),
            P(),
            P(("seq", "tp"), None),
            P(("seq", "tp"), None),
            P("seq", None, None, "tp"),
            P("seq", "tp", None),
        ),
        out_specs=(P(("seq", "tp"), None), P(("seq", "tp"), None)),
        check_vma=False,
    )
```

```python
import functools
import math

import jax
import jax.numpy as jnp
from jax import lax
from jax.experimental import pallas as pl
from jax.experimental.pallas import tpu as pltpu
from jax.sharding import PartitionSpec as P

HEAD_DIM = 128


def tenant_of(positions, lengths):
    bounds = jnp.cumsum(lengths)
    return jnp.sum((positions[:, None] >= bounds[None, :]).astype(jnp.int32), axis=1)


def spread_kernel(
    blocks, per, back, q_ref, kv_ref, q_out, kv_out, q_send, q_recv, kv_send, kv_recv
):
    me = lax.axis_index("seq")
    tp = lax.axis_index("tp")
    heads = q_ref.shape[0]
    span = back + per
    tries = back // per + 1
    mine = me % blocks

    def send(src, dst, sem, recv, target):
        @pl.when(target == me)
        def _():
            pltpu.make_async_copy(src, dst, sem).start()

        @pl.when(target != me)
        def _():
            pltpu.make_async_remote_copy(
                src_ref=src,
                dst_ref=dst,
                send_sem=sem,
                recv_sem=recv,
                device_id=(target, tp),
                device_id_type=pl.DeviceIdType.MESH,
            ).start()

    def finish_send(src, dst, sem, recv, target):
        @pl.when(target == me)
        def _():
            pltpu.make_async_copy(src, dst, sem).wait()

        @pl.when(target != me)
        def _():
            pltpu.make_async_remote_copy(
                src_ref=src,
                dst_ref=dst,
                send_sem=sem,
                recv_sem=recv,
                device_id=(target, tp),
                device_id_type=pl.DeviceIdType.MESH,
            ).wait_send()

    def finish_recv(src, dst, sem, recv, source):
        @pl.when(source != me)
        def _():
            pltpu.make_async_remote_copy(
                src_ref=src,
                dst_ref=dst,
                send_sem=sem,
                recv_sem=recv,
                device_id=(source, tp),
                device_id_type=pl.DeviceIdType.MESH,
            ).wait_recv()

    plan = []
    for h in range(heads):
        target = h * blocks + me // per
        plan.append((q_ref.at[h], q_out.at[me % per], q_send.at[h], q_recv.at[me % per], target))
        for r in range(tries):
            block = (me + back) // per - r
            slot = (me + back) % per + per * r
            plan.append(
                (
                    kv_ref.at[h],
                    kv_out.at[slot],
                    kv_send.at[h, r],
                    kv_recv.at[slot],
                    h * blocks + block,
                    (block >= 0) & (block < blocks),
                )
            )
    for item in plan:
        valid = item[5] if len(item) > 5 else True

        @pl.when(valid)
        def _():
            send(*item[:5])

    for item in plan:
        valid = item[5] if len(item) > 5 else True

        @pl.when(valid)
        def _():
            finish_send(*item[:5])

    for i in range(per):
        source = per * mine + i
        finish_recv(q_ref.at[0], q_out.at[i], q_send.at[0], q_recv.at[i], source)
    for slot in range(span):
        source = per * mine - back + slot

        @pl.when(source >= 0)
        def _():
            finish_recv(kv_ref.at[0], kv_out.at[slot], kv_send.at[0, 0], kv_recv.at[slot], source)


def spread(q, kv, blocks, per, back):
    heads = q.shape[0]
    span = back + per
    tries = back // per + 1
    return pl.pallas_call(
        functools.partial(spread_kernel, blocks, per, back),
        out_shape=(
            jax.ShapeDtypeStruct((per,) + q.shape[1:], q.dtype),
            jax.ShapeDtypeStruct((span,) + kv.shape[1:], kv.dtype),
        ),
        in_specs=[pl.BlockSpec(memory_space=pl.ANY)] * 2,
        out_specs=(pl.BlockSpec(memory_space=pl.ANY), pl.BlockSpec(memory_space=pl.ANY)),
        scratch_shapes=[
            pltpu.SemaphoreType.DMA((heads,)),
            pltpu.SemaphoreType.DMA((per,)),
            pltpu.SemaphoreType.DMA((heads, tries)),
            pltpu.SemaphoreType.DMA((span,)),
        ],
        compiler_params=pltpu.CompilerParams(has_side_effects=True),
    )(q, kv)


def gather_kernel(blocks, per, att_ref, out_ref, send_sem, recv_sem):
    me = lax.axis_index("seq")
    tp = lax.axis_index("tp")
    heads = out_ref.shape[0]
    head = me // blocks
    mine = me % blocks

    def copy(i, target):
        return pltpu.make_async_remote_copy(
            src_ref=att_ref.at[i],
            dst_ref=out_ref.at[head],
            send_sem=send_sem.at[i],
            recv_sem=recv_sem.at[head],
            device_id=(target, tp),
            device_id_type=pl.DeviceIdType.MESH,
        )

    for i in range(per):
        target = per * mine + i

        @pl.when(target == me)
        def _():
            pltpu.make_async_copy(att_ref.at[i], out_ref.at[head], send_sem.at[i]).start()

        @pl.when(target != me)
        def _():
            copy(i, target).start()

    for i in range(per):
        target = per * mine + i

        @pl.when(target == me)
        def _():
            pltpu.make_async_copy(att_ref.at[i], out_ref.at[head], send_sem.at[i]).wait()

        @pl.when(target != me)
        def _():
            copy(i, target).wait_send()

    for h in range(heads):
        source = h * blocks + me // per

        @pl.when(source != me)
        def _():
            pltpu.make_async_remote_copy(
                src_ref=att_ref.at[0],
                dst_ref=out_ref.at[h],
                send_sem=send_sem.at[0],
                recv_sem=recv_sem.at[h],
                device_id=(source, tp),
                device_id_type=pl.DeviceIdType.MESH,
            ).wait_recv()


def gather_back(att, heads, blocks):
    per = att.shape[0]
    return pl.pallas_call(
        functools.partial(gather_kernel, blocks, per),
        out_shape=jax.ShapeDtypeStruct((heads,) + att.shape[1:], att.dtype),
        in_specs=[pl.BlockSpec(memory_space=pl.ANY)],
        out_specs=pl.BlockSpec(memory_space=pl.ANY),
        scratch_shapes=[pltpu.SemaphoreType.DMA((per,)), pltpu.SemaphoreType.DMA((heads,))],
        compiler_params=pltpu.CompilerParams(has_side_effects=True),
    )(att)


def attend_kernel(
    blocks, per, back, scale, bounds_ref, q_ref, kv_ref, out_ref,
    q_in, kv_in, att, acc, top, total, kept,
    q_send, q_recv, kv_send, kv_recv, att_send, att_recv,
):
    me = lax.axis_index("seq")
    tp = lax.axis_index("tp")
    heads, rows, head_dim = q_ref.shape
    span = back + per
    tries = back // per + 1
    mine = me // heads
    head = me % heads

    def remote(src, dst, send, recv, device):
        return pltpu.make_async_remote_copy(
            src_ref=src, dst_ref=dst, send_sem=send, recv_sem=recv,
            device_id=(device, tp), device_id_type=pl.DeviceIdType.MESH,
        )

    plan = []
    for h in range(heads):
        target = (me // per) * heads + h
        plan.append(
            (q_ref.at[h], q_in.at[me % per], q_send.at[h], q_recv.at[me % per], target, True)
        )
    for r in range(tries):
        for h in range(heads):
            block = (me + back) // per - r
            slot = (me + back) % per + per * r
            valid = (block >= 0) & (block < blocks)
            plan.append(
                (kv_ref.at[h], kv_in.at[slot], kv_send.at[h, r], kv_recv.at[slot],
                 block * heads + h, valid)
            )
    for src, dst, send, recv, target, valid in plan:

        @pl.when(valid & (target == me))
        def _():
            pltpu.make_async_copy(src, dst, send).start()

        @pl.when(valid & (target != me))
        def _():
            remote(src, dst, send, recv, target).start()

    for src, dst, send, recv, target, valid in plan:

        @pl.when(valid & (target == me))
        def _():
            pltpu.make_async_copy(src, dst, send).wait()

    for i in range(per):
        source = per * mine + i

        @pl.when(source != me)
        def _():
            remote(q_ref.at[0], q_in.at[i], q_send.at[0], q_recv.at[i], source).wait_recv()

    query = q_in[...].reshape(per * rows, head_dim)
    query_pos = mine * per * rows + lax.broadcasted_iota(jnp.int32, (per * rows, 1), 0)
    first = jnp.zeros(query_pos.shape, jnp.int32)
    for k in range(bounds_ref.shape[0]):
        first = jnp.maximum(first, jnp.where(query_pos >= bounds_ref[k], bounds_ref[k], 0))

    top[...] = jnp.full(top.shape, -1e30, jnp.float32)
    total[...] = jnp.zeros(total.shape, jnp.float32)
    acc[...] = jnp.zeros(acc.shape, jnp.float32)

    def first_pass(slot, carry):
        source = per * mine - back + slot

        @pl.when(source >= 0)
        def _():
            @pl.when(source != me)
            def _():
                remote(
                    kv_ref.at[0], kv_in.at[slot], kv_send.at[0, 0], kv_recv.at[slot], source
                ).wait_recv()

            key_pos = source * rows + lax.broadcasted_iota(jnp.int32, (1, rows), 1)
            visible = (key_pos >= first) & (key_pos <= query_pos)
            scores = lax.dot_general(
                query, kv_in[slot, :, :head_dim], (((1,), (1,)), ((), ())),
                preferred_element_type=jnp.float32,
            ) * scale
            scores = jnp.where(visible, scores, -1e30)
            kept[slot] = scores
            top[...] = jnp.maximum(top[...], jnp.max(scores, axis=1, keepdims=True))

        return carry

    lax.fori_loop(0, span, first_pass, 0)

    def second_pass(slot, carry):
        source = per * mine - back + slot

        @pl.when(source >= 0)
        def _():
            weights = jnp.exp(kept[slot] - top[...])
            total[...] += jnp.sum(weights, axis=1, keepdims=True)
            acc[...] += jnp.dot(
                weights.astype(jnp.bfloat16), kv_in[slot, :, head_dim:],
                preferred_element_type=jnp.float32,
            )

        return carry

    lax.fori_loop(0, span, second_pass, 0)
    att[...] = (acc[...] / total[...]).astype(att.dtype).reshape(att.shape)

    for i in range(per):
        target = per * mine + i

        @pl.when(target == me)
        def _():
            pltpu.make_async_copy(att.at[i], out_ref.at[head], att_send.at[i]).start()

        @pl.when(target != me)
        def _():
            remote(att.at[i], out_ref.at[head], att_send.at[i], att_recv.at[head], target).start()

    for i in range(per):
        target = per * mine + i

        @pl.when(target == me)
        def _():
            pltpu.make_async_copy(att.at[i], out_ref.at[head], att_send.at[i]).wait()

        @pl.when(target != me)
        def _():
            remote(
                att.at[i], out_ref.at[head], att_send.at[i], att_recv.at[head], target
            ).wait_send()

    for h in range(heads):
        source = (me // per) * heads + h

        @pl.when(source != me)
        def _():
            remote(att.at[0], out_ref.at[h], att_send.at[0], att_recv.at[h], source).wait_recv()

    for src, dst, send, recv, target, valid in plan:

        @pl.when(valid & (target != me))
        def _():
            remote(src, dst, send, recv, target).wait_send()


def attend(bounds, q, kv, blocks, back, scale):
    heads, rows, head_dim = q.shape
    per = heads
    span = back + per
    tries = back // per + 1
    return pl.pallas_call(
        functools.partial(attend_kernel, blocks, per, back, scale),
        out_shape=jax.ShapeDtypeStruct(q.shape, q.dtype),
        in_specs=[
            pl.BlockSpec(memory_space=pltpu.SMEM),
            pl.BlockSpec(memory_space=pl.ANY),
            pl.BlockSpec(memory_space=pl.ANY),
        ],
        out_specs=pl.BlockSpec(memory_space=pl.ANY),
        scratch_shapes=[
            pltpu.VMEM((per, rows, head_dim), q.dtype),
            pltpu.VMEM((span,) + kv.shape[1:], kv.dtype),
            pltpu.VMEM((per, rows, head_dim), q.dtype),
            pltpu.VMEM((per * rows, head_dim), jnp.float32),
            pltpu.VMEM((per * rows, 1), jnp.float32),
            pltpu.VMEM((per * rows, 1), jnp.float32),
            pltpu.VMEM((span, per * rows, rows), jnp.float32),
            pltpu.SemaphoreType.DMA((heads,)),
            pltpu.SemaphoreType.DMA((per,)),
            pltpu.SemaphoreType.DMA((heads, tries)),
            pltpu.SemaphoreType.DMA((span,)),
            pltpu.SemaphoreType.DMA((per,)),
            pltpu.SemaphoreType.DMA((heads,)),
        ],
        compiler_params=pltpu.CompilerParams(has_side_effects=True),
    )(bounds, q, kv)


def shards(
    queries, keys, values, lengths, resid, w_out, moe_gain, routes, gates, w_gate_up, w_down
):
    seq_count = lax.axis_size("seq")
    me = lax.axis_index("seq")
    query_rows = queries.shape[0]
    local_heads = queries.shape[1] // HEAD_DIM
    cols = queries.shape[1]
    width = resid.shape[1]
    score_scale = 1.0 / math.sqrt(HEAD_DIM)
    longest = (seq_count * query_rows) // 2
    reach = min(seq_count - 1, -(-(longest - 1) // query_rows))
    blocks = seq_count // local_heads
    per = seq_count // blocks
    back = -(-reach // per) * per
    span = back + per
    head_q = queries.reshape(query_rows, local_heads, HEAD_DIM).transpose(1, 0, 2)
    head_kv = jnp.concatenate(
        [
            keys.reshape(query_rows, local_heads, HEAD_DIM),
            values.reshape(query_rows, local_heads, HEAD_DIM),
        ],
        axis=2,
    ).transpose(1, 0, 2)
    attention = (
        attend(
            jnp.cumsum(lengths).astype(jnp.int32), head_q, head_kv, blocks, back, score_scale
        )
        .transpose(1, 0, 2)
        .reshape(query_rows, local_heads * HEAD_DIM)
    )
    tp_index = lax.axis_index("tp")
    near_swap = [(t, t ^ 1) for t in range(lax.axis_size("tp"))]
    far_swap = [(t, t ^ 2) for t in range(lax.axis_size("tp"))]
    local_rows = resid.shape[0]
    partial_proj = jnp.dot(attention, w_out, preferred_element_type=jnp.float32).reshape(
        2, 2, local_rows, width
    )
    core = tp_index % 2
    keep = lax.dynamic_index_in_dim(partial_proj, core, axis=1, keepdims=False)
    give = lax.dynamic_index_in_dim(partial_proj, 1 - core, axis=1, keepdims=False)
    half = keep + lax.ppermute(give.astype(jnp.bfloat16), "tp", near_swap).astype(jnp.float32)
    far = tp_index // 2
    pair_resid = jnp.stack([resid, lax.ppermute(resid, "tp", far_swap)])
    pair_routes = jnp.stack([routes, lax.ppermute(routes, "tp", far_swap)])
    pair_gates = jnp.stack([gates, lax.ppermute(gates, "tp", far_swap)])
    half = half.astype(jnp.bfloat16)
    total = half.astype(jnp.float32) + lax.ppermute(half, "tp", far_swap).astype(jnp.float32)
    pair_proj = jnp.stack(
        [
            lax.dynamic_index_in_dim(total, far, axis=0, keepdims=False),
            lax.dynamic_index_in_dim(total, 1 - far, axis=0, keepdims=False),
        ]
    )
    pair_attended = (pair_resid.astype(jnp.float32) + pair_proj).astype(jnp.bfloat16)
    attended = pair_attended[0]
    widened = pair_attended.astype(jnp.float32)
    meansq = jnp.mean(widened * widened, axis=2, keepdims=True)
    pair_normed = (widened * lax.rsqrt(meansq + 1e-05) * moe_gain).astype(jnp.bfloat16)
    top_count = routes.shape[1]
    owned = w_gate_up.shape[0]
    experts_all = owned * seq_count
    capacity = 3 * local_rows * top_count // (2 * experts_all)
    matches = pair_routes[..., None] == jnp.arange(experts_all, dtype=jnp.int32)
    member = jnp.any(matches, axis=2)
    slot = jnp.cumsum(member.astype(jnp.int32), axis=1) - 1
    place = member[..., None] & (slot[..., None] == jnp.arange(capacity, dtype=jnp.int32))
    buffer = jnp.einsum(
        "xiec,xid->excd", place.astype(jnp.bfloat16), pair_normed,
        preferred_element_type=jnp.float32,
    ).astype(jnp.bfloat16)
    buffer = buffer.reshape(seq_count, owned, 2, capacity, width).transpose(1, 0, 2, 3, 4)
    arrived = lax.all_to_all(buffer, "seq", split_axis=1, concat_axis=1, tiled=True)
    near = lax.ppermute(arrived, "tp", near_swap)

    def expert_part(slots):
        projections = jnp.einsum(
            "xnd,xdgf->xngf", slots.reshape(owned, -1, width), w_gate_up,
            preferred_element_type=jnp.float32,
        )
        hidden = (jax.nn.silu(projections[..., 0, :]) * projections[..., 1, :]).astype(
            jnp.bfloat16
        )
        return jnp.einsum(
            "xnf,xfd->xnd", hidden, w_down, preferred_element_type=jnp.float32
        ).astype(jnp.bfloat16)

    from_near = lax.ppermute(expert_part(near), "tp", near_swap)
    reduced = (
        expert_part(arrived).astype(jnp.float32) + from_near.astype(jnp.float32)
    ).astype(jnp.bfloat16)
    returned = lax.all_to_all(
        reduced.reshape(arrived.shape), "seq", split_axis=1, concat_axis=1, tiled=True
    )
    weight_of = jnp.sum(jnp.where(matches, pair_gates[..., None], 0.0), axis=2)
    mix_weights = jnp.where(place, weight_of[..., None], 0.0)
    mixes = jnp.einsum(
        "xiec,xecd->xid",
        mix_weights.astype(jnp.bfloat16),
        returned.transpose(2, 1, 0, 3, 4).reshape(2, experts_all, capacity, width),
        preferred_element_type=jnp.float32,
    )
    from_far = lax.ppermute(mixes[1].astype(jnp.bfloat16), "tp", far_swap)
    expert_mix = (mixes[0] + from_far.astype(jnp.float32)).astype(jnp.bfloat16)
    return (attended, expert_mix)


def solution(mesh):
    return jax.shard_map(
        shards,
        mesh=mesh,
        in_specs=(
            P("seq", "tp"),
            P("seq", "tp"),
            P("seq", "tp"),
            P(),
            P(("seq", "tp"), None),
            P("tp", None),
            P(),
            P(("seq", "tp"), None),
            P(("seq", "tp"), None),
            P("seq", None, None, "tp"),
            P("seq", "tp", None),
        ),
        out_specs=(P(("seq", "tp"), None), P(("seq", "tp"), None)),
        check_vma=False,
    )
```
